32 devices in a mesh: dp: 4 (over y, x), seq: 8 (over z, core).
Axes of the slice: x: 2, y: 2, z: 4, core: 2. Of those that a mesh axis runs over, the one named last changes fastest.
Arguments:
- tokens: bfloat16 [4, 1024, 2048], P('dp', 'seq'), may hold values from -6 to 6
- attn_gain: bfloat16 [2048], P(('dp', 'seq')), may hold values from 0.5 to 1.5
- w_query: bfloat16 [2048, 2048], P(('dp', 'seq')), may hold values from -0.125 to 0.125
- w_key: bfloat16 [2048, 2048], P(('dp', 'seq')), may hold values from -0.125 to 0.125
- w_value: bfloat16 [2048, 4096], P(('dp', 'seq')), may hold values from -0.125 to 0.125
- w_decay: bfloat16 [2048, 16], P(('dp', 'seq')), may hold values from -0.125 to 0.125
- w_beta: bfloat16 [2048, 16], P(('dp', 'seq')), may hold values from -0.125 to 0.125
- w_gate: bfloat16 [2048, 4096], P(('dp', 'seq')), may hold values from -0.125 to 0.125
- w_out: bfloat16 [2048, 4096], P(('dp', 'seq')), may hold values from -0.1875 to 0.1875
- conv_query: float32 [4, 2048], replicated, may hold values from -2.5 to 2.5
- conv_key: float32 [4, 2048], replicated, may hold values from -2.5 to 2.5
- conv_value: float32 [4, 4096], replicated, may hold values from -2.5 to 2.5
- decay_log: float32 [16], replicated, may hold values from -9 to -3
- decay_bias: float32 [16], replicated, may hold values from -1 to 1
- out_gain: float32 [256], replicated, may hold values from 0.5 to 1.5
- mlp_gain: bfloat16 [2048], P(('dp', 'seq')), may hold values from 0.5 to 1.5
- w_hidden: bfloat16 [2048, 5632], P(('dp', 'seq')), may hold values from -0.125 to 0.125
- w_up: bfloat16 [2048, 5632], P(('dp', 'seq')), may hold values from -0.125 to 0.125
- w_down: bfloat16 [2048, 5632], P(('dp', 'seq')), may hold values from -0.15625 to 0.15625
- offsets: int32 [4, 1024], P('dp', 'seq'), may hold values from 0 to 1023, as said below
- cotangent: bfloat16 [4, 1024, 2048], P('dp', 'seq'), may hold values from -6 to 6
Outputs:
- output: bfloat16 [4, 1024, 2048], P('dp', 'seq')
- grad_tokens: bfloat16 [4, 1024, 2048], P('dp', 'seq')
- grad_attn_gain: float32 [2048], P(('dp', 'seq'))
- grad_w_query: float32 [2048, 2048], P(('dp', 'seq'))
- grad_w_key: float32 [2048, 2048], P(('dp', 'seq'))
- grad_w_value: float32 [2048, 4096], P(('dp', 'seq'))
- grad_w_decay: float32 [2048, 16], P(('dp', 'seq'))
- grad_w_beta: float32 [2048, 16], P(('dp', 'seq'))
- grad_w_gate: float32 [2048, 4096], P(('dp', 'seq'))
- grad_w_out: float32 [2048, 4096], P(('dp', 'seq'))
- grad_conv_query: float32 [4, 2048], replicated
- grad_conv_key: float32 [4, 2048], replicated
- grad_conv_value: float32 [4, 4096], replicated
- grad_decay_log: float32 [16], replicated
- grad_decay_bias: float32 [16], replicated
- grad_out_gain: float32 [256], replicated
- grad_mlp_gain: float32 [2048], P(('dp', 'seq'))
- grad_w_hidden: float32 [2048, 5632], P(('dp', 'seq'))
- grad_w_up: float32 [2048, 5632], P(('dp', 'seq'))
- grad_w_down: float32 [2048, 5632], P(('dp', 'seq'))
The draws below stay inside these ranges and needn't reach their ends.
Inputs may be any that keep to these rules, and one draw needn't show every extreme that they name: `offsets`: every packed row begins a document: its first position has offset 0. Along a row, a position's offset is 0 where a new document starts and otherwise one more than the previous position's offset. The first packed row holds a single document.
All inputs are finite; a program needn't handle non-finite values.
Results may differ from the reference program's by a relative error of at most 0.017.
Values may be sent and summed in bfloat16 or wider, within the bound.
No kernel may reach another device: no remote copies, remote signals or barrier semaphores. Data moves between devices by JAX's collectives and lax.ppermute only.
A program may use at most 512 MiB of HBM per device.

```python
import math
import jax
import jax.numpy as jnp
from jax import lax

D = 2048
HEADS = 16
DK = 128
DV = 256
FF = 5632
KERNEL = 4
TOK_DEV = 128
ROWS = 4
SEQ_LEN = 1024


def draw_offsets(key, part):
    starts = jax.random.randint(key, (ROWS, SEQ_LEN), 0, 2 * TOK_DEV) == 0
    places = jnp.broadcast_to(jnp.arange(SEQ_LEN, dtype=jnp.int32), (ROWS, SEQ_LEN))
    row_index = jnp.broadcast_to(jnp.arange(ROWS, dtype=jnp.int32)[:, None], (ROWS, SEQ_LEN))
    starts = starts & (row_index > 0) | (places == 0)
    latest = lax.cummax(jnp.where(starts, places, 0), axis=1)
    return (places - latest).astype(jnp.int32)


def block_scale(key, shape, cuts, least, top_value):
    level = 1.0
    for position, shards_of in cuts:
        steps = jax.random.uniform(jax.random.fold_in(jax.random.fold_in(key, 6), position), (shards_of,), jnp.float32, least / len(cuts), top_value / len(cuts))
        level = level * jnp.repeat(jnp.exp(steps), shape[position] // shards_of).reshape((-1,) + (1,) * (len(shape) - 1 - position))
    return level


def bell_draw(rng, dims, deviation, limit, pieces=(), kind=jnp.bfloat16):
    result = jax.random.normal(rng, dims, jnp.float32) * deviation
    if len(pieces) > 0:
        result = block_scale(rng, dims, pieces, -0.22, 0.18) * result
    return jnp.clip(result, min=-limit, max=limit).astype(kind)


def setup_inputs(seed: int = 0) -> dict:
    arg_keys = jax.random.split(jax.random.key(seed), 22)
    return {
        "tokens": bell_draw(arg_keys[0], (ROWS, SEQ_LEN, D), 1.0, 6.0, ((0, 4), (1, 8))),
        "attn_gain": jnp.clip(1.0 + 0.1 * jax.random.normal(arg_keys[1], (D,), jnp.float32), 0.5, 1.5).astype(jnp.bfloat16),
        "w_query": bell_draw(arg_keys[2], (D, HEADS * DK), D ** -0.5, 0.125, ((0, 32),)),
        "w_key": bell_draw(arg_keys[3], (D, HEADS * DK), D ** -0.5, 0.125, ((0, 32),)),
        "w_value": bell_draw(arg_keys[4], (D, HEADS * DV), D ** -0.5, 0.125, ((0, 32),)),
        "w_decay": bell_draw(arg_keys[5], (D, HEADS), D ** -0.5, 0.125, ((0, 32),)),
        "w_beta": bell_draw(arg_keys[6], (D, HEADS), D ** -0.5, 0.125, ((0, 32),)),
        "w_gate": bell_draw(arg_keys[7], (D, HEADS * DV), D ** -0.5, 0.125, ((0, 32),)),
        "w_out": bell_draw(arg_keys[8], (D, HEADS * DV), (HEADS * DV // 4) ** -0.5, 0.1875, ((0, 32),)),
        "conv_query": bell_draw(arg_keys[9], (KERNEL, HEADS * DK), 0.5, 2.5, (), jnp.float32),
        "conv_key": bell_draw(arg_keys[10], (KERNEL, HEADS * DK), 0.5, 2.5, (), jnp.float32),
        "conv_value": bell_draw(arg_keys[11], (KERNEL, HEADS * DV), 0.5, 2.5, (), jnp.float32),
        "decay_log": jnp.clip(jax.random.uniform(arg_keys[12], (HEADS,), jnp.float32, -9.0, -3.0), -9.0, -3.0),
        "decay_bias": jnp.clip(jax.random.uniform(arg_keys[13], (HEADS,), jnp.float32, -1.0, 1.0), -1.0, 1.0),
        "out_gain": jnp.clip(1.0 + 0.1 * jax.random.normal(arg_keys[14], (DV,), jnp.float32), 0.5, 1.5),
        "mlp_gain": jnp.clip(1.0 + 0.1 * jax.random.normal(arg_keys[15], (D,), jnp.float32), 0.5, 1.5).astype(jnp.bfloat16),
        "w_hidden": bell_draw(arg_keys[16], (D, FF), D ** -0.5, 0.125, ((0, 32),)),
        "w_up": bell_draw(arg_keys[17], (D, FF), D ** -0.5, 0.125, ((0, 32),)),
        "w_down": bell_draw(arg_keys[18], (D, FF), (FF // 4) ** -0.5, 0.15625, ((0, 32),)),
        "offsets": draw_offsets(jax.random.fold_in(arg_keys[21], 71), 0),
        "cotangent": bell_draw(arg_keys[20], (ROWS, SEQ_LEN, D), 1.0, 6.0, ((0, 4), (1, 8))),
    }


HIGHEST = lax.Precision.HIGHEST

@jax.custom_vjp
def low(v):
    return lax.optimization_barrier(v.astype(jnp.bfloat16)).astype(jnp.float32)

@jax.custom_vjp
def low_back(v):
    return v

def low_keep(v):
    return (low(v), None)

def low_pass(kept, grad):
    return (grad,)

def back_keep(v):
    return (v, None)

def back_low(kept, grad):
    return (low(grad),)
low.defvjp(low_keep, low_pass)
low_back.defvjp(back_keep, back_low)

def rms_scale(value):
    return lax.rsqrt(lax.optimization_barrier(jnp.mean(value * value, axis=-1, keepdims=True)) + 1e-05)

def unit_rows(value):
    return value * lax.rsqrt(lax.optimization_barrier(jnp.sum(value * value, axis=-1, keepdims=True)) + 1e-06)

def project(left, weight):
    return jnp.einsum('rtd,de->rte', left, weight, precision=HIGHEST)

def project_back(left, weight):
    return jnp.einsum('rtc,dc->rtd', left, weight, precision=HIGHEST)

def causal_taps(pre_act, kernel_taps, offsets):
    summed = kernel_taps[0] * pre_act
    for shift_by in range(1, KERNEL):
        delayed = jnp.pad(pre_act, ((0, 0), (shift_by, 0), (0, 0)))[:, :-shift_by]
        summed = summed + kernel_taps[shift_by] * jnp.where((offsets >= shift_by)[..., None], delayed, 0.0)
    return summed

def delta_rule(queries, key_vecs, values, beta_rows, logdecay, offsets):
    row_count, seq_len = (queries.shape[0], queries.shape[1])
    keep_state = jnp.where(offsets == 0, 0.0, 1.0).astype(jnp.float32)
    factor = jnp.exp(logdecay) * keep_state[..., None]
    block_len = math.gcd(seq_len, 32)
    blocks = seq_len // block_len

    def time_major(array_in):
        turned = jnp.moveaxis(array_in, 1, 0)
        return turned.reshape((blocks, block_len) + turned.shape[1:])
    sequence_items = tuple((time_major(array_in) for array_in in (queries, key_vecs, values, beta_rows, factor)))

    def one_step(carried, step_items):
        query_now, key_now, value_now, beta_now, factor_now = step_items
        decayed = carried * factor_now[..., None, None]
        recalled = jnp.einsum('rhvk,rhk->rhv', decayed, key_now, precision=HIGHEST)
        update = beta_now[..., None] * (value_now - recalled)
        carried = decayed + update[..., :, None] * key_now[..., None, :]
        return (carried, jnp.einsum('rhvk,rhk->rhv', carried, query_now, precision=HIGHEST))

    @jax.checkpoint
    def one_block(carried, block_items):
        return lax.scan(one_step, carried, block_items)
    initial = jnp.zeros((row_count, queries.shape[2], values.shape[3], queries.shape[3]), jnp.float32)
    final_state, outputs = lax.scan(one_block, initial, sequence_items)
    outputs = outputs.reshape((seq_len,) + outputs.shape[2:])
    return jnp.moveaxis(outputs, 0, 1)

def layer(inputs, attn_gain, w_query, w_key, w_value, w_decay, w_beta, w_gate, w_out, conv_query, conv_key, conv_value, decay_log, decay_bias, out_gain, mlp_gain, w_hidden, w_up, w_down, offsets):
    row_count, seq_len = (inputs.shape[0], inputs.shape[1])
    head_count = decay_log.shape[0]
    attn_normed = low(inputs * rms_scale(inputs) * attn_gain)
    pre_query = low_back(low(project(attn_normed, w_query)))
    pre_key = low_back(low(project(attn_normed, w_key)))
    pre_value = low_back(low(project(attn_normed, w_value)))
    pre_gate = low_back(project(attn_normed, w_gate))
    pre_decay = project(attn_normed, w_decay)
    pre_beta = project(attn_normed, w_beta)
    shape_rows = (row_count, seq_len, head_count, -1)
    queries = unit_rows(jax.nn.silu(causal_taps(pre_query, conv_query, offsets)).reshape(shape_rows))
    queries = queries * queries.shape[-1] ** (-0.5)
    key_vecs = unit_rows(jax.nn.silu(causal_taps(pre_key, conv_key, offsets)).reshape(shape_rows))
    values = jax.nn.silu(causal_taps(pre_value, conv_value, offsets)).reshape(shape_rows)
    beta_rows = jax.nn.sigmoid(pre_beta)
    logdecay = -jnp.exp(decay_log) * jax.nn.softplus(pre_decay + decay_bias)
    mixed = delta_rule(queries, key_vecs, values, beta_rows, logdecay, offsets)
    gate_rows = jax.nn.silu(pre_gate).reshape(mixed.shape)
    gated = low((mixed * rms_scale(mixed) * out_gain * gate_rows).reshape(row_count, seq_len, -1))
    middle = inputs + low_back(project_back(gated, w_out))
    mlp_normed = low(middle * rms_scale(middle) * mlp_gain)
    hidden_pre = low_back(project(mlp_normed, w_hidden))
    up_pre = low_back(project(mlp_normed, w_up))
    product = low(jax.nn.silu(hidden_pre) * up_pre)
    return middle + low_back(project_back(product, w_down))

def reference(tokens, attn_gain, w_query, w_key, w_value, w_decay, w_beta, w_gate, w_out, conv_query, conv_key, conv_value, decay_log, decay_bias, out_gain, mlp_gain, w_hidden, w_up, w_down, offsets, cotangent):
    given_arrays = (tokens, attn_gain, w_query, w_key, w_value, w_decay, w_beta, w_gate, w_out, conv_query, conv_key, conv_value, decay_log, decay_bias, out_gain, mlp_gain, w_hidden, w_up, w_down)
    floats = tuple((array_in.astype(jnp.float32) for array_in in given_arrays))

    def forward(*float_args):
        return layer(*float_args, offsets)
    output, pullback = jax.vjp(forward, *floats)
    gradients = pullback(cotangent.astype(jnp.float32))
    return (output.astype(jnp.bfloat16), gradients[0].astype(jnp.bfloat16), gradients[1], gradients[2], gradients[3], gradients[4], gradients[5], gradients[6], gradients[7], gradients[8], gradients[9], gradients[10], gradients[11], gradients[12], gradients[13], gradients[14], gradients[15], gradients[16], gradients[17], gradients[18])
```

```python
import jax
import jax.numpy as jnp
from jax import lax
from jax.sharding import PartitionSpec as P

KERNEL = 4
LANES = 128
HIGHEST = lax.Precision.HIGHEST
BF = jnp.bfloat16
F32 = jnp.float32
CHUNK = 128


def rms_scale(value):
    return lax.rsqrt(jnp.mean(value * value, axis=-1, keepdims=True) + 1e-05)


def dot_f32(left, right, dims):
    return lax.dot_general(left, right, (dims, ((), ())), preferred_element_type=F32)


def nn(left, right):
    return dot_f32(left, right, ((1,), (0,)))


def nt(left, right):
    return dot_f32(left, right, ((1,), (1,)))


def tn(left, right):
    return dot_f32(left, right, ((0,), (0,)))


def exact(spec, left, right):
    return jnp.einsum(spec, left, right, precision=HIGHEST)


def silu(value):
    return value * jax.nn.sigmoid(value)


def silu_slope(value):
    s = jax.nn.sigmoid(value)
    return s * (1.0 + value * (1.0 - s))


class Plan:
    def __init__(self, ranks, heads, key_dim, value_dim, hidden):
        self.ranks = ranks
        self.heads = heads
        self.key_dim = key_dim
        self.hp = max(1, heads // ranks)
        self.vs = max(1, ranks // heads)
        self.dv = value_dim // self.vs
        self.value_dim = value_dim
        self.ff = hidden // ranks

    def split_keys(self, array):
        rows = array.shape[0]
        grouped = array.reshape(rows, self.heads // self.hp, -1)
        return jnp.repeat(grouped, self.vs, axis=1) if self.vs > 1 else grouped

    def split_even(self, array):
        return array.reshape(array.shape[0], self.ranks, -1)

    def join_keys(self, array):
        ranks, rows, width = array.shape
        array = array.astype(F32)
        if self.vs > 1:
            array = array.reshape(ranks // self.vs, self.vs, rows, width).sum(axis=1)
        return jnp.transpose(array, (1, 0, 2)).reshape(rows, -1)

    def join_even(self, array):
        return jnp.transpose(array, (1, 0, 2)).reshape(array.shape[1], -1).astype(F32)

    def value_sum(self, array):
        step = 1
        while step < self.vs:
            pairs = [(i, i ^ step) for i in range(self.ranks)]
            array = array + lax.ppermute(array, "seq", pairs)
            step *= 2
        return array


def to_columns(packed):
    ranks = packed.shape[1]
    turned = jnp.transpose(packed, (1, 0, 2)).reshape(-1, packed.shape[2])
    own = lax.all_to_all(turned, "seq", 0, 0, tiled=True)
    return lax.all_gather(own, "dp", axis=0, tiled=True)


def to_rows(grads, ranks):
    mine = lax.psum_scatter(grads.astype(BF), "dp", scatter_dimension=0, tiled=True)
    turned = lax.all_to_all(mine, "seq", 0, 0, tiled=True)
    return turned.reshape(ranks, -1, grads.shape[1])


def causal_taps(pre, taps, offsets):
    summed = taps[0] * pre
    for by in range(1, KERNEL):
        delayed = jnp.pad(pre, ((by, 0), (0, 0)))[:-by]
        summed = summed + taps[by] * jnp.where((offsets >= by)[:, None], delayed, 0.0)
    return summed


def unit_lower_inverse(strict):
    n = strict.shape[-1]
    where = jnp.arange(n, dtype=jnp.int32)
    base = 8
    same = (where[:, None] // base) == (where[None, :] // base)
    eye = jnp.eye(n, dtype=F32)
    small = jnp.where(same, strict, 0.0)
    square = exact("...ij,...jk->...ik", small, small)
    fourth = exact("...ij,...jk->...ik", square, square)
    inverse = exact("...ij,...jk->...ik", eye - small, eye + square)
    inverse = exact("...ij,...jk->...ik", inverse, eye + fourth)
    size = base
    while size < n:
        pair = (where[:, None] // (2 * size)) == (where[None, :] // (2 * size))
        other = (where[:, None] // size) != (where[None, :] // size)
        part = jnp.where(pair & other, strict, 0.0)
        merged = exact("...ij,...jk->...ik", inverse, part)
        inverse = inverse - exact("...ij,...jk->...ik", merged, inverse)
        size *= 2
    return inverse


def delta_rule(queries, key_vecs, values, beta_rows, logdecay, offsets):
    h, t, k = queries.shape
    n = CHUNK
    b = t // n
    q = queries.reshape(h, b, n, k)
    ks = key_vecs.reshape(h, b, n, k)
    v = values.reshape(h, b, n, -1)
    beta = beta_rows.reshape(h, b, n)
    logs = logdecay.reshape(h, b, n)
    offs = offsets.reshape(b, n)
    where = jnp.arange(n, dtype=jnp.int32)
    distance = where[:, None] - where[None, :]
    same_doc = (distance >= 0) & (offs[:, :, None] >= distance)
    total = exact("hbs,ts->hbt", logs, (distance >= 0).astype(F32))
    exponent = total[..., :, None] - total[..., None, :]
    decay = jnp.where(same_doc, jnp.exp(jnp.where(same_doc, exponent, 0.0)), 0.0)
    start = jnp.where(offs > where, jnp.exp(total), 0.0)
    key_key = exact("hbtk,hbsk->hbts", ks, ks)
    strict = jnp.where(distance > 0, decay * key_key, 0.0) * beta[..., None]
    inverse = unit_lower_inverse(strict)
    fresh = exact("hbts,hbsv->hbtv", inverse, beta[..., None] * v)
    seen = exact("hbts,hbsk->hbtk", inverse, (beta * start)[..., None] * ks)
    query_key = decay * exact("hbtk,hbsk->hbts", q, ks)
    q_start = q * start[..., None]
    k_end = ks * decay[..., n - 1, :][..., None]
    last = start[..., n - 1]
    state = jnp.zeros((h, k, v.shape[-1]), F32)
    outs = []
    for c in range(b):
        update = fresh[:, c] - exact("htk,hkv->htv", seen[:, c], state)
        outs.append(
            exact("htk,hkv->htv", q_start[:, c], state)
            + exact("hts,hsv->htv", query_key[:, c], update)
        )
        state = last[:, c][:, None, None] * state + exact("htk,htv->hkv", k_end[:, c], update)
    return jnp.concatenate(outs, axis=1)


def local(
    tokens,
    attn_gain,
    w_query,
    w_key,
    w_value,
    w_decay,
    w_beta,
    w_gate,
    w_out,
    conv_query,
    conv_key,
    conv_value,
    decay_log,
    decay_bias,
    out_gain,
    mlp_gain,
    w_hidden,
    w_up,
    w_down,
    offsets,
    cotangent,
):
    ranks = lax.axis_size("seq")
    rank = lax.axis_index("seq")
    heads = decay_log.shape[0]
    width = tokens.shape[-1]
    tok = tokens.shape[1]
    length = tok * ranks
    plan = Plan(ranks, heads, w_query.shape[1] // heads, out_gain.shape[0], w_hidden.shape[1])
    hp, vs, dk, dv, ff = plan.hp, plan.vs, plan.key_dim, plan.dv, plan.ff
    rows = w_query.shape[0]

    own_tokens = tokens[0]
    own_cot = cotangent[0]
    rider = jnp.concatenate(
        [
            (offsets[0] // 64).astype(BF)[:, None],
            (offsets[0] % 64).astype(BF)[:, None],
            jnp.zeros((tok, LANES - 2), BF),
        ],
        axis=1,
    )
    gathered = lax.all_gather(
        jnp.concatenate([own_tokens, rider], axis=1), "seq", axis=0, tiled=True
    )
    small = jnp.concatenate(
        [
            plan.split_keys(w_decay),
            plan.split_keys(w_beta),
            jnp.broadcast_to(attn_gain[:, None, None], (rows, ranks, 1)),
            jnp.broadcast_to(mlp_gain[:, None, None], (rows, ranks, 1)),
            jnp.zeros((rows, ranks, LANES - 2 - 2 * hp), BF),
        ],
        axis=2,
    )
    w_in = to_columns(
        jnp.concatenate(
            [
                plan.split_keys(w_query),
                plan.split_keys(w_key),
                plan.split_even(w_value),
                plan.split_even(w_gate),
                small,
            ],
            axis=2,
        )
    )
    out_cols = to_columns(plan.split_even(w_out))
    mlp_cols = to_columns(
        jnp.concatenate(
            [plan.split_even(w_hidden), plan.split_even(w_up), plan.split_even(w_down)], axis=2
        )
    )
    cot_all = lax.all_gather(own_cot, "seq", axis=0, tiled=True)

    at_k = hp * dk
    at_v = 2 * hp * dk
    at_g = at_v + hp * dv
    at_s = at_g + hp * dv
    attn_gain_full = w_in[:, at_s + 2 * hp].astype(F32)
    mlp_gain_full = w_in[:, at_s + 2 * hp + 1].astype(F32)

    tokens_all = gathered[:, :width].astype(F32)
    offs = (
        gathered[:, width].astype(F32) * 64.0 + gathered[:, width + 1].astype(F32)
    ).astype(jnp.int32)
    normed_all = tokens_all * rms_scale(tokens_all)
    attn = (normed_all * attn_gain_full).astype(BF)
    pre = nn(attn, w_in)
    pre_query = pre[:, :at_k].astype(BF).astype(F32)
    pre_key = pre[:, at_k:at_v].astype(BF).astype(F32)
    pre_value = pre[:, at_v:at_g].astype(BF).astype(F32)
    pre_gate = pre[:, at_g:at_s]
    pre_decay = pre[:, at_s : at_s + hp]
    pre_beta = pre[:, at_s + hp : at_s + 2 * hp]

    group = rank // vs
    taps_query = lax.dynamic_slice_in_dim(conv_query, group * hp * dk, hp * dk, 1)
    taps_key = lax.dynamic_slice_in_dim(conv_key, group * hp * dk, hp * dk, 1)
    taps_value = lax.dynamic_slice_in_dim(conv_value, rank * hp * dv, hp * dv, 1)
    own_log = lax.dynamic_slice_in_dim(decay_log, group * hp, hp, 0)
    own_bias = lax.dynamic_slice_in_dim(decay_bias, group * hp, hp, 0)
    own_gain = lax.dynamic_slice_in_dim(out_gain, (rank % vs) * dv, dv, 0)

    def head_major(array):
        return jnp.transpose(array.reshape(length, hp, -1), (1, 0, 2))

    def front(query_in, key_in, value_in, tq, tk, tv, decay_in, beta_in, log_rates, rate_bias):
        q = head_major(silu(causal_taps(query_in, tq, offs)))
        q = q * lax.rsqrt(jnp.sum(q * q, axis=-1, keepdims=True) + 1e-06) * dk ** (-0.5)
        k = head_major(silu(causal_taps(key_in, tk, offs)))
        k = k * lax.rsqrt(jnp.sum(k * k, axis=-1, keepdims=True) + 1e-06)
        v = head_major(silu(causal_taps(value_in, tv, offs)))
        beta = jax.nn.sigmoid(beta_in).T
        logs = (-jnp.exp(log_rates) * jax.nn.softplus(decay_in + rate_bias)).T
        return q, k, v, beta, logs

    fronted, front_back = jax.vjp(
        front,
        pre_query,
        pre_key,
        pre_value,
        taps_query,
        taps_key,
        taps_value,
        pre_decay,
        pre_beta,
        own_log,
        own_bias,
    )
    mixed, rule_back = jax.vjp(lambda *a: delta_rule(*a, offs), *fronted)
    gate = head_major(pre_gate)
    mix_scale = lax.rsqrt(
        plan.value_sum(jnp.sum(mixed * mixed, axis=-1, keepdims=True)) / plan.value_dim + 1e-05
    )
    m = mixed * mix_scale
    sg = silu(gate)

    def token_major(array):
        return jnp.transpose(array, (1, 0, 2)).reshape(length, -1)

    gated = token_major(m * own_gain * sg).astype(BF)
    branch = lax.psum_scatter(
        nt(gated, out_cols).astype(BF), "seq", scatter_dimension=0, tiled=True
    )
    inputs = own_tokens.astype(F32)
    middle = inputs + branch.astype(F32)
    r2 = rms_scale(middle)
    n2 = middle * r2
    mlp_own = (n2 * mlp_gain_full).astype(BF)
    mlp_all = lax.all_gather(mlp_own, "seq", axis=0, tiled=True)
    hidden_w = mlp_cols[:, :ff]
    up_w = mlp_cols[:, ff : 2 * ff]
    down_w = mlp_cols[:, 2 * ff :]
    hidden_pre = nn(mlp_all, hidden_w)
    up_pre = nn(mlp_all, up_w)
    sh = silu(hidden_pre)
    product = (sh * up_pre).astype(BF)
    d_product = nn(cot_all, down_w)
    d_hidden = (d_product * up_pre * silu_slope(hidden_pre)).astype(BF)
    d_up = (d_product * sh).astype(BF)
    d_mlp = lax.psum_scatter(
        (nt(d_hidden, hidden_w) + nt(d_up, up_w)).astype(BF), "seq", scatter_dimension=0, tiled=True
    ).astype(F32)
    d_output = own_cot.astype(F32)
    grad_mlp_gain = jnp.sum(d_mlp * n2, axis=0)
    e2 = d_mlp * mlp_gain_full
    d_middle = d_output + r2 * (e2 - n2 * jnp.mean(e2 * n2, axis=-1, keepdims=True))
    d_branch_all = lax.all_gather(d_middle.astype(BF), "seq", axis=0, tiled=True)
    mlp_out = lax.psum_scatter(
        nt(product, down_w).astype(BF), "seq", scatter_dimension=0, tiled=True
    )
    output = (middle + mlp_out.astype(F32)).astype(BF)
    grad_mlp = jnp.concatenate(
        [tn(mlp_all, d_hidden), tn(mlp_all, d_up), tn(cot_all, product)], axis=1
    )
    mlp_rows = to_rows(grad_mlp, ranks)

    d_gated = head_major(nn(d_branch_all, out_cols))
    out_rows = to_rows(tn(d_branch_all, gated), ranks)
    grad_out_gain = jnp.sum(d_gated * m * sg, axis=(0, 1))
    em = d_gated * own_gain * sg
    em_mean = plan.value_sum(jnp.sum(em * m, axis=-1, keepdims=True)) / plan.value_dim
    d_mixed = mix_scale * (em - m * em_mean)
    d_gate = token_major(d_gated * m * own_gain * silu_slope(gate)).astype(BF)
    back = front_back(rule_back(d_mixed))
    d_pre = jnp.concatenate(
        [
            back[0].astype(BF),
            back[1].astype(BF),
            back[2].astype(BF),
            d_gate,
            back[6].astype(BF),
            back[7].astype(BF),
            jnp.zeros((length, LANES - 2 * hp), BF),
        ],
        axis=1,
    )
    d_attn_part = nt(d_pre, w_in)
    grad_attn_gain = jnp.sum(d_attn_part * normed_all, axis=0)
    d_attn = lax.psum_scatter(
        d_attn_part.astype(BF), "seq", scatter_dimension=0, tiled=True
    ).astype(F32)
    grad_in = tn(attn, d_pre)
    grad_in = jnp.concatenate(
        [
            grad_in[:, : at_s + 2 * hp],
            grad_attn_gain[:, None],
            grad_mlp_gain[:, None],
            grad_in[:, at_s + 2 * hp + 2 :],
        ],
        axis=1,
    )
    in_rows = to_rows(grad_in, ranks)

    n = inputs * rms_scale(inputs)
    e = d_attn * attn_gain_full
    grad_tokens = (
        d_middle + rms_scale(inputs) * (e - n * jnp.mean(e * n, axis=-1, keepdims=True))
    ).astype(BF)

    sums = jnp.concatenate(
        [
            back[3].reshape(-1),
            back[4].reshape(-1),
            back[5].reshape(-1),
            back[8],
            back[9],
            grad_out_gain,
        ]
    )
    every = lax.all_gather(sums, ("dp", "seq"), axis=0, tiled=False)
    every = every.reshape(-1, ranks, sums.shape[0]).sum(axis=0)

    def per_head(part, lead):
        part = part.reshape(ranks // vs, vs, lead, -1).sum(axis=1)
        return jnp.transpose(part, (1, 0, 2)).reshape(lead, -1)

    a0 = KERNEL * hp * dk
    a1 = 2 * a0
    a2 = a1 + KERNEL * hp * dv
    grad_conv_value = jnp.transpose(
        every[:, a1:a2].reshape(ranks, KERNEL, -1), (1, 0, 2)
    ).reshape(KERNEL, -1)
    gain_sum = every[:, a2 + 2 * hp :].reshape(ranks // vs, vs, dv).sum(axis=0).reshape(-1)
    grad_small = in_rows[:, :, at_s : at_s + LANES].astype(F32)
    gain_rows = jnp.sum(grad_small[:, :, 2 * hp : 2 * hp + 2], axis=0)
    return (
        output[None],
        grad_tokens[None],
        gain_rows[:, 0],
        plan.join_keys(in_rows[:, :, :at_k]),
        plan.join_keys(in_rows[:, :, at_k:at_v]),
        plan.join_even(in_rows[:, :, at_v:at_g]),
        plan.join_keys(grad_small[:, :, :hp]),
        plan.join_keys(grad_small[:, :, hp : 2 * hp]),
        plan.join_even(in_rows[:, :, at_g:at_s]),
        plan.join_even(out_rows),
        per_head(every[:, :a0], KERNEL),
        per_head(every[:, a0:a1], KERNEL),
        grad_conv_value,
        per_head(every[:, a2 : a2 + hp], 1)[0],
        per_head(every[:, a2 + hp : a2 + 2 * hp], 1)[0],
        gain_sum,
        gain_rows[:, 1],
        plan.join_even(mlp_rows[:, :, :ff]),
        plan.join_even(mlp_rows[:, :, ff : 2 * ff]),
        plan.join_even(mlp_rows[:, :, 2 * ff :]),
    )


def solution(mesh):
    flat = ("dp", "seq")
    tok_spec = P("dp", "seq", None)
    row_spec = P(flat, None)
    gain_spec = P(flat)
    in_specs = (
        (tok_spec, gain_spec)
        + (row_spec,) * 7
        + (P(),) * 6
        + (gain_spec,)
        + (row_spec,) * 3
        + (P("dp", "seq"), tok_spec)
    )
    out_specs = (
        (tok_spec, tok_spec, gain_spec)
        + (row_spec,) * 7
        + (P(),) * 6
        + (gain_spec,)
        + (row_spec,) * 3
    )
    return jax.shard_map(local, mesh=mesh, in_specs=in_specs, out_specs=out_specs, check_vma=False)
```

```python
import jax
import jax.numpy as jnp
from jax import lax
from jax.sharding import PartitionSpec as P

KERNEL = 4
LANES = 128
HIGHEST = lax.Precision.HIGHEST
BF = jnp.bfloat16
F32 = jnp.float32
CHUNK = 128


def rms_scale(value):
    return lax.rsqrt(jnp.mean(value * value, axis=-1, keepdims=True) + 1e-05)


def dot_f32(left, right, dims):
    return lax.dot_general(left, right, (dims, ((), ())), preferred_element_type=F32)


def nn(left, right):
    return dot_f32(left, right, ((1,), (0,)))


def nt(left, right):
    return dot_f32(left, right, ((1,), (1,)))


def tn(left, right):
    return dot_f32(left, right, ((0,), (0,)))


def exact(spec, left, right):
    return jnp.einsum(spec, left, right, precision=HIGHEST)


def silu(value):
    return value * jax.nn.sigmoid(value)


def silu_slope(value):
    s = jax.nn.sigmoid(value)
    return s * (1.0 + value * (1.0 - s))


class Plan:
    def __init__(self, ranks, heads, key_dim, value_dim, hidden):
        self.ranks = ranks
        self.heads = heads
        self.key_dim = key_dim
        self.hp = max(1, heads // ranks)
        self.vs = max(1, ranks // heads)
        self.dv = value_dim // self.vs
        self.value_dim = value_dim
        self.ff = hidden // ranks

    def split_keys(self, array):
        rows = array.shape[0]
        grouped = array.reshape(rows, self.heads // self.hp, -1)
        return jnp.repeat(grouped, self.vs, axis=1) if self.vs > 1 else grouped

    def split_even(self, array):
        return array.reshape(array.shape[0], self.ranks, -1)

    def join_keys(self, array):
        ranks, rows, width = array.shape
        array = array.astype(F32)
        if self.vs > 1:
            array = array.reshape(ranks // self.vs, self.vs, rows, width).sum(axis=1)
        return jnp.transpose(array, (1, 0, 2)).reshape(rows, -1)

    def join_even(self, array):
        return jnp.transpose(array, (1, 0, 2)).reshape(array.shape[1], -1).astype(F32)

    def value_sum(self, array):
        step = 1
        while step < self.vs:
            pairs = [(i, i ^ step) for i in range(self.ranks)]
            array = array + lax.ppermute(array, "seq", pairs)
            step *= 2
        return array


def after(value, *earlier):
    return lax.optimization_barrier((value,) + earlier)[0]


def ring_order(count):
    return [0, 1, 3, 2] if count == 4 else list(range(count))


def ring_pairs(count):
    order = ring_order(count)
    right = [(order[i], order[(i + 1) % count]) for i in range(count)]
    return right, [(there, here) for here, there in right]


def ring_places():
    me = lax.axis_index("dp")
    order = ring_order(4)
    place = jnp.array([order.index(i) for i in range(4)], jnp.int32)[me]
    ring = jnp.array(order, jnp.int32)
    return me, ring[(place + 3) % 4], ring[(place + 1) % 4], ring[(place + 2) % 4]


def gather_dp(own):
    if lax.axis_size("dp") != 4:
        return lax.all_gather(own, "dp", axis=0, tiled=True)
    right, left = ring_pairs(4)
    rows = own.shape[0]
    half = rows // 2
    from_left = lax.ppermute(own, "dp", right)
    from_right = lax.ppermute(own, "dp", left)
    far_a = lax.ppermute(from_left[:half], "dp", right)
    far_b = lax.ppermute(from_right[half:], "dp", left)
    me, at_left, at_right, at_far = ring_places()
    full = jnp.zeros((4 * rows, own.shape[1]), own.dtype)
    full = lax.dynamic_update_slice(full, own, (me * rows, 0))
    full = lax.dynamic_update_slice(full, from_left, (at_left * rows, 0))
    full = lax.dynamic_update_slice(full, from_right, (at_right * rows, 0))
    full = lax.dynamic_update_slice(full, far_a, (at_far * rows, 0))
    return lax.dynamic_update_slice(full, far_b, (at_far * rows + half, 0))


def scatter_dp(partial):
    if lax.axis_size("dp") != 4:
        return lax.psum_scatter(partial, "dp", scatter_dimension=0, tiled=True)
    right, left = ring_pairs(4)
    rows = partial.shape[0] // 4
    half = rows // 2
    me, at_left, at_right, at_far = ring_places()

    def part(block, offset, size):
        return lax.dynamic_slice_in_dim(partial, block * rows + offset, size, 0)

    def plus(own, received):
        return (own.astype(F32) + received.astype(F32)).astype(BF)

    far_a = lax.ppermute(part(at_far, 0, half), "dp", right)
    far_b = lax.ppermute(part(at_far, half, half), "dp", left)
    right_b = lax.ppermute(part(at_right, half, half), "dp", right)
    left_a = lax.ppermute(part(at_left, 0, half), "dp", left)
    right_a = lax.ppermute(plus(part(at_right, 0, half), far_a), "dp", right)
    left_b = lax.ppermute(plus(part(at_left, half, half), far_b), "dp", left)
    own = part(me, 0, rows).astype(F32)
    from_left = jnp.concatenate([right_a, right_b]).astype(F32)
    from_right = jnp.concatenate([left_a, left_b]).astype(F32)
    return (own + from_left + from_right).astype(BF)


def exchange(packed):
    turned = jnp.transpose(packed, (1, 0, 2)).reshape(-1, packed.shape[2])
    return lax.all_to_all(turned, "seq", 0, 0, tiled=True)


def to_rows(grads, ranks):
    mine = scatter_dp(grads.astype(BF))
    turned = lax.all_to_all(mine, "seq", 0, 0, tiled=True)
    return turned.reshape(ranks, -1, grads.shape[1])


def sum_everywhere(values):
    count = lax.axis_size("dp")
    ranks = lax.axis_size("seq")
    if count & (count - 1) or ranks & (ranks - 1):
        return lax.all_gather(lax.psum(values, "dp"), "seq", axis=0, tiled=False)
    step = 1
    while step < count:
        values = values + lax.ppermute(values, "dp", [(i, i ^ step) for i in range(count)])
        step *= 2
    rank = lax.axis_index("seq")
    held = values.reshape(1, -1)
    step = 1
    while step < ranks:
        other = lax.ppermute(held, "seq", [(i, i ^ step) for i in range(ranks)])
        upper = (rank & step) != 0
        held = jnp.concatenate([jnp.where(upper, other, held), jnp.where(upper, held, other)])
        step *= 2
    return held


def causal_taps(pre, taps, offsets):
    summed = taps[0] * pre
    for by in range(1, KERNEL):
        delayed = jnp.pad(pre, ((by, 0), (0, 0)))[:-by]
        summed = summed + taps[by] * jnp.where((offsets >= by)[:, None], delayed, 0.0)
    return summed


def unit_lower_inverse(strict):
    n = strict.shape[-1]
    where = jnp.arange(n, dtype=jnp.int32)
    base = 8
    same = (where[:, None] // base) == (where[None, :] // base)
    eye = jnp.eye(n, dtype=F32)
    small = jnp.where(same, strict, 0.0)
    square = exact("...ij,...jk->...ik", small, small)
    fourth = exact("...ij,...jk->...ik", square, square)
    inverse = exact("...ij,...jk->...ik", eye - small, eye + square)
    inverse = exact("...ij,...jk->...ik", inverse, eye + fourth)
    size = base
    while size < n:
        pair = (where[:, None] // (2 * size)) == (where[None, :] // (2 * size))
        other = (where[:, None] // size) != (where[None, :] // size)
        part = jnp.where(pair & other, strict, 0.0)
        merged = exact("...ij,...jk->...ik", inverse, part)
        inverse = inverse - exact("...ij,...jk->...ik", merged, inverse)
        size *= 2
    return inverse


def delta_rule(queries, key_vecs, values, beta_rows, logdecay, offsets):
    h, t, k = queries.shape
    n = CHUNK
    b = t // n
    q = queries.reshape(h, b, n, k)
    ks = key_vecs.reshape(h, b, n, k)
    v = values.reshape(h, b, n, -1)
    beta = beta_rows.reshape(h, b, n)
    logs = logdecay.reshape(h, b, n)
    offs = offsets.reshape(b, n)
    where = jnp.arange(n, dtype=jnp.int32)
    distance = where[:, None] - where[None, :]
    same_doc = (distance >= 0) & (offs[:, :, None] >= distance)
    total = exact("hbs,ts->hbt", logs, (distance >= 0).astype(F32))
    exponent = total[..., :, None] - total[..., None, :]
    decay = jnp.where(same_doc, jnp.exp(jnp.where(same_doc, exponent, 0.0)), 0.0)
    start = jnp.where(offs > where, jnp.exp(total), 0.0)
    key_key = exact("hbtk,hbsk->hbts", ks, ks)
    strict = jnp.where(distance > 0, decay * key_key, 0.0) * beta[..., None]
    inverse = unit_lower_inverse(strict)
    fresh = exact("hbts,hbsv->hbtv", inverse, beta[..., None] * v)
    seen = exact("hbts,hbsk->hbtk", inverse, (beta * start)[..., None] * ks)
    query_key = decay * exact("hbtk,hbsk->hbts", q, ks)
    q_start = q * start[..., None]
    k_end = ks * decay[..., n - 1, :][..., None]
    last = start[..., n - 1]
    state = jnp.zeros((h, k, v.shape[-1]), F32)
    outs = []
    for c in range(b):
        update = fresh[:, c] - exact("htk,hkv->htv", seen[:, c], state)
        outs.append(
            exact("htk,hkv->htv", q_start[:, c], state)
            + exact("hts,hsv->htv", query_key[:, c], update)
        )
        state = last[:, c][:, None, None] * state + exact("htk,htv->hkv", k_end[:, c], update)
    return jnp.concatenate(outs, axis=1)


def local(
    tokens,
    attn_gain,
    w_query,
    w_key,
    w_value,
    w_decay,
    w_beta,
    w_gate,
    w_out,
    conv_query,
    conv_key,
    conv_value,
    decay_log,
    decay_bias,
    out_gain,
    mlp_gain,
    w_hidden,
    w_up,
    w_down,
    offsets,
    cotangent,
):
    ranks = lax.axis_size("seq")
    rank = lax.axis_index("seq")
    heads = decay_log.shape[0]
    width = tokens.shape[-1]
    tok = tokens.shape[1]
    length = tok * ranks
    plan = Plan(ranks, heads, w_query.shape[1] // heads, out_gain.shape[0], w_hidden.shape[1])
    hp, vs, dk, dv, ff = plan.hp, plan.vs, plan.key_dim, plan.dv, plan.ff
    rows = w_query.shape[0]

    own_tokens = tokens[0]
    own_cot = cotangent[0]
    rider = jnp.concatenate(
        [
            (offsets[0] // 64).astype(BF)[:, None],
            (offsets[0] % 64).astype(BF)[:, None],
            jnp.zeros((tok, LANES - 2), BF),
        ],
        axis=1,
    )
    small = jnp.concatenate(
        [
            plan.split_keys(w_decay),
            plan.split_keys(w_beta),
            jnp.broadcast_to(attn_gain[:, None, None], (rows, ranks, 1)),
            jnp.broadcast_to(mlp_gain[:, None, None], (rows, ranks, 1)),
            jnp.zeros((rows, ranks, LANES - 2 - 2 * hp), BF),
        ],
        axis=2,
    )
    mix_own = exchange(
        jnp.concatenate(
            [
                plan.split_keys(w_query),
                plan.split_keys(w_key),
                plan.split_even(w_value),
                small,
            ],
            axis=2,
        )
    )
    gathered = lax.all_gather(
        after(jnp.concatenate([own_tokens, rider], axis=1), mix_own), "seq", axis=0, tiled=True
    )
    w_mix = gather_dp(mix_own)
    side_own = exchange(
        after(
            jnp.concatenate([plan.split_even(w_gate), plan.split_even(w_out)], axis=2), gathered
        )
    )
    w_side = gather_dp(after(side_own, w_mix))
    mlp_own_cols = exchange(
        after(
            jnp.concatenate(
                [plan.split_even(w_hidden), plan.split_even(w_up), plan.split_even(w_down)],
                axis=2,
            ),
            side_own,
        )
    )
    mlp_cols = gather_dp(after(mlp_own_cols, w_side))
    cot_all = lax.all_gather(after(own_cot, gathered), "seq", axis=0, tiled=True)

    at_k = hp * dk
    at_v = 2 * hp * dk
    at_s = at_v + hp * dv
    attn_gain_full = w_mix[:, at_s + 2 * hp].astype(F32)
    mlp_gain_full = w_mix[:, at_s + 2 * hp + 1].astype(F32)
    gate_cols = w_side[:, : hp * dv]
    out_cols = w_side[:, hp * dv :]

    tokens_all = gathered[:, :width].astype(F32)
    offs = (
        gathered[:, width].astype(F32) * 64.0 + gathered[:, width + 1].astype(F32)
    ).astype(jnp.int32)
    normed_all = tokens_all * rms_scale(tokens_all)
    attn = (normed_all * attn_gain_full).astype(BF)
    pre = nn(attn, w_mix)
    pre_query = pre[:, :at_k].astype(BF).astype(F32)
    pre_key = pre[:, at_k:at_v].astype(BF).astype(F32)
    pre_value = pre[:, at_v:at_s].astype(BF).astype(F32)
    pre_gate = nn(attn, gate_cols)
    pre_decay = pre[:, at_s : at_s + hp]
    pre_beta = pre[:, at_s + hp : at_s + 2 * hp]

    group = rank // vs
    taps_query = lax.dynamic_slice_in_dim(conv_query, group * hp * dk, hp * dk, 1)
    taps_key = lax.dynamic_slice_in_dim(conv_key, group * hp * dk, hp * dk, 1)
    taps_value = lax.dynamic_slice_in_dim(conv_value, rank * hp * dv, hp * dv, 1)
    own_log = lax.dynamic_slice_in_dim(decay_log, group * hp, hp, 0)
    own_bias = lax.dynamic_slice_in_dim(decay_bias, group * hp, hp, 0)
    own_gain = lax.dynamic_slice_in_dim(out_gain, (rank % vs) * dv, dv, 0)

    def head_major(array):
        return jnp.transpose(array.reshape(length, hp, -1), (1, 0, 2))

    def front(query_in, key_in, value_in, tq, tk, tv, decay_in, beta_in, log_rates, rate_bias):
        q = head_major(silu(causal_taps(query_in, tq, offs)))
        q = q * lax.rsqrt(jnp.sum(q * q, axis=-1, keepdims=True) + 1e-06) * dk ** (-0.5)
        k = head_major(silu(causal_taps(key_in, tk, offs)))
        k = k * lax.rsqrt(jnp.sum(k * k, axis=-1, keepdims=True) + 1e-06)
        v = head_major(silu(causal_taps(value_in, tv, offs)))
        beta = jax.nn.sigmoid(beta_in).T
        logs = (-jnp.exp(log_rates) * jax.nn.softplus(decay_in + rate_bias)).T
        return q, k, v, beta, logs

    fronted_free, front_back = jax.vjp(
        front,
        pre_query,
        pre_key,
        pre_value,
        taps_query,
        taps_key,
        taps_value,
        pre_decay,
        pre_beta,
        own_log,
        own_bias,
    )
    fronted = lax.optimization_barrier(tuple(fronted_free) + (side_own,))[:5]
    mixed, rule_back = jax.vjp(lambda *a: delta_rule(*a, offs), *fronted)
    gate = head_major(pre_gate)
    mix_scale = lax.rsqrt(
        plan.value_sum(jnp.sum(mixed * mixed, axis=-1, keepdims=True)) / plan.value_dim + 1e-05
    )
    m = mixed * mix_scale
    sg = silu(gate)

    def token_major(array):
        return jnp.transpose(array, (1, 0, 2)).reshape(length, -1)

    gated = after(token_major(m * own_gain * sg).astype(BF), mlp_own_cols, cot_all)
    branch = lax.psum_scatter(
        nt(gated, out_cols).astype(BF), "seq", scatter_dimension=0, tiled=True
    )
    inputs = own_tokens.astype(F32)
    middle = inputs + branch.astype(F32)
    r2 = rms_scale(middle)
    n2 = middle * r2
    mlp_own = (n2 * mlp_gain_full).astype(BF)
    mlp_all = lax.all_gather(mlp_own, "seq", axis=0, tiled=True)
    both_w = mlp_cols[:, : 2 * ff]
    down_w = mlp_cols[:, 2 * ff :]
    d_product = nn(cot_all, down_w)
    both_pre = nn(mlp_all, both_w)
    hidden_pre = both_pre[:, :ff]
    up_pre = both_pre[:, ff:]
    sh = silu(hidden_pre)
    product = (sh * up_pre).astype(BF)
    d_both = jnp.concatenate(
        [
            (d_product * up_pre * silu_slope(hidden_pre)).astype(BF),
            (d_product * sh).astype(BF),
        ],
        axis=1,
    )
    d_mlp = lax.psum_scatter(
        nt(d_both, both_w).astype(BF), "seq", scatter_dimension=0, tiled=True
    ).astype(F32)
    d_output = own_cot.astype(F32)
    e2 = d_mlp * mlp_gain_full
    d_middle = d_output + r2 * (e2 - n2 * jnp.mean(e2 * n2, axis=-1, keepdims=True))
    d_branch_all = lax.all_gather(d_middle.astype(BF), "seq", axis=0, tiled=True)
    mlp_out = lax.psum_scatter(
        after(nt(product, down_w).astype(BF), d_branch_all), "seq", scatter_dimension=0, tiled=True
    )
    output = (middle + mlp_out.astype(F32)).astype(BF)
    both_rows = to_rows(tn(mlp_all, d_both), ranks)
    down_rows = to_rows(tn(cot_all, product), ranks)

    d_gated = head_major(nn(d_branch_all, out_cols))
    out_rows = to_rows(tn(d_branch_all, gated), ranks)
    grad_out_gain = jnp.sum(d_gated * m * sg, axis=(0, 1))
    em = d_gated * own_gain * sg
    em_mean = plan.value_sum(jnp.sum(em * m, axis=-1, keepdims=True)) / plan.value_dim
    d_mixed = mix_scale * (em - m * em_mean)
    d_gate = token_major(d_gated * m * own_gain * silu_slope(gate)).astype(BF)
    gate_rows = to_rows(tn(attn, d_gate), ranks)
    d_attn_gate = nt(d_gate, gate_cols)
    ruled = lax.optimization_barrier(
        tuple(rule_back(d_mixed)) + (mlp_out, both_rows, down_rows, out_rows, gate_rows)
    )[:5]
    back = front_back(ruled)
    d_pre = jnp.concatenate(
        [
            back[0],
            back[1],
            back[2],
            back[6],
            back[7],
            jnp.zeros((length, LANES - 2 * hp), F32),
        ],
        axis=1,
    ).astype(BF)
    mix_rows = to_rows(tn(attn, d_pre), ranks)
    d_attn = lax.psum_scatter(
        (d_attn_gate + nt(d_pre, w_mix)).astype(BF), "seq", scatter_dimension=0, tiled=True
    ).astype(F32)

    n = inputs * rms_scale(inputs)
    e = d_attn * attn_gain_full
    grad_tokens = (
        d_middle + rms_scale(inputs) * (e - n * jnp.mean(e * n, axis=-1, keepdims=True))
    ).astype(BF)

    sums = jnp.concatenate(
        [
            back[3].reshape(-1),
            back[4].reshape(-1),
            back[5].reshape(-1),
            back[8],
            back[9],
            grad_out_gain,
        ]
    )
    every = sum_everywhere(jnp.pad(sums, (0, -sums.shape[0] % 1024)))

    def per_head(part, lead):
        part = part.reshape(ranks // vs, vs, lead, -1).sum(axis=1)
        return jnp.transpose(part, (1, 0, 2)).reshape(lead, -1)

    a0 = KERNEL * hp * dk
    a1 = 2 * a0
    a2 = a1 + KERNEL * hp * dv
    grad_conv_value = jnp.transpose(
        every[:, a1:a2].reshape(ranks, KERNEL, -1), (1, 0, 2)
    ).reshape(KERNEL, -1)
    gain_sum = every[:, a2 + 2 * hp : a2 + 2 * hp + dv].reshape(ranks // vs, vs, dv).sum(axis=0).reshape(-1)
    grad_query = plan.join_keys(mix_rows[:, :, :at_k])
    grad_key = plan.join_keys(mix_rows[:, :, at_k:at_v])
    grad_value = plan.join_even(mix_rows[:, :, at_v:at_s])
    grad_decay = plan.join_keys(mix_rows[:, :, at_s : at_s + hp])
    grad_beta = plan.join_keys(mix_rows[:, :, at_s + hp : at_s + 2 * hp])
    grad_gate = plan.join_even(gate_rows)
    grad_hidden = plan.join_even(both_rows[:, :, :ff])
    grad_up = plan.join_even(both_rows[:, :, ff:])

    def gain_grad(gain, pairs):
        total = sum(jnp.sum(w.astype(F32) * g, axis=1) for w, g in pairs)
        return total / gain.astype(F32)

    return (
        output[None],
        grad_tokens[None],
        gain_grad(
            attn_gain,
            (
                (w_query, grad_query),
                (w_key, grad_key),
                (w_value, grad_value),
                (w_decay, grad_decay),
                (w_beta, grad_beta),
                (w_gate, grad_gate),
            ),
        ),
        grad_query,
        grad_key,
        grad_value,
        grad_decay,
        grad_beta,
        grad_gate,
        plan.join_even(out_rows),
        per_head(every[:, :a0], KERNEL),
        per_head(every[:, a0:a1], KERNEL),
        grad_conv_value,
        per_head(every[:, a2 : a2 + hp], 1)[0],
        per_head(every[:, a2 + hp : a2 + 2 * hp], 1)[0],
        gain_sum,
        gain_grad(mlp_gain, ((w_hidden, grad_hidden), (w_up, grad_up))),
        grad_hidden,
        grad_up,
        plan.join_even(down_rows),
    )


def solution(mesh):
    flat = ("dp", "seq")
    tok_spec = P("dp", "seq", None)
    row_spec = P(flat, None)
    gain_spec = P(flat)
    in_specs = (
        (tok_spec, gain_spec)
        + (row_spec,) * 7
        + (P(),) * 6
        + (gain_spec,)
        + (row_spec,) * 3
        + (P("dp", "seq"), tok_spec)
    )
    out_specs = (
        (tok_spec, tok_spec, gain_spec)
        + (row_spec,) * 7
        + (P(),) * 6
        + (gain_spec,)
        + (row_spec,) * 3
    )
    return jax.shard_map(local, mesh=mesh, in_specs=in_specs, out_specs=out_specs, check_vma=False)
```

```python
import functools

import jax
import jax.numpy as jnp
from jax import lax
from jax.experimental import pallas as pl
from jax.experimental.pallas import tpu as pltpu
from jax.sharding import PartitionSpec as P

KERNEL = 4
LANES = 128
HIGHEST = lax.Precision.HIGHEST
BF = jnp.bfloat16
F32 = jnp.float32
CHUNK = 128


def rms_scale(value):
    return lax.rsqrt(jnp.mean(value * value, axis=-1, keepdims=True) + 1e-05)


def dot_f32(left, right, dims):
    return lax.dot_general(left, right, (dims, ((), ())), preferred_element_type=F32)


def nn(left, right):
    return dot_f32(left, right, ((1,), (0,)))


def nt(left, right):
    return dot_f32(left, right, ((1,), (1,)))


def tn(left, right):
    return dot_f32(left, right, ((0,), (0,)))


def exact(spec, left, right):
    return jnp.einsum(spec, left, right, precision=HIGHEST)


def silu(value):
    return value * jax.nn.sigmoid(value)


def silu_slope(value):
    s = jax.nn.sigmoid(value)
    return s * (1.0 + value * (1.0 - s))


class Plan:
    def __init__(self, ranks, heads, key_dim, value_dim, hidden):
        self.ranks = ranks
        self.heads = heads
        self.key_dim = key_dim
        self.hp = max(1, heads // ranks)
        self.vs = max(1, ranks // heads)
        self.dv = value_dim // self.vs
        self.value_dim = value_dim
        self.ff = hidden // ranks

    def split_keys(self, array):
        rows = array.shape[0]
        grouped = array.reshape(rows, self.heads // self.hp, -1)
        return jnp.repeat(grouped, self.vs, axis=1) if self.vs > 1 else grouped

    def split_even(self, array):
        return array.reshape(array.shape[0], self.ranks, -1)

    def join_keys(self, array):
        ranks, rows, width = array.shape
        array = array.astype(F32)
        if self.vs > 1:
            array = array.reshape(ranks // self.vs, self.vs, rows, width).sum(axis=1)
        return jnp.transpose(array, (1, 0, 2)).reshape(rows, -1)

    def join_even(self, array):
        return jnp.transpose(array, (1, 0, 2)).reshape(array.shape[1], -1).astype(F32)

    def value_sum(self, array):
        step = 1
        while step < self.vs:
            pairs = [(i, i ^ step) for i in range(self.ranks)]
            array = array + lax.ppermute(array, "seq", pairs)
            step *= 2
        return array


def after(value, *earlier):
    return lax.optimization_barrier((value,) + earlier)[0]


def ring_order(count):
    return [0, 1, 3, 2] if count == 4 else list(range(count))


def ring_pairs(count):
    order = ring_order(count)
    right = [(order[i], order[(i + 1) % count]) for i in range(count)]
    return right, [(there, here) for here, there in right]


def ring_places():
    me = lax.axis_index("dp")
    order = ring_order(4)
    place = jnp.array([order.index(i) for i in range(4)], jnp.int32)[me]
    ring = jnp.array(order, jnp.int32)
    return me, ring[(place + 3) % 4], ring[(place + 1) % 4], ring[(place + 2) % 4]


def to_ring(array):
    if lax.axis_size("dp") != 4:
        return array
    size = array.shape[1] // 4
    return jnp.concatenate(
        [lax.dynamic_slice_in_dim(array, at * size, size, 1) for at in ring_places()], axis=1
    )


def from_ring(array):
    if lax.axis_size("dp") != 4:
        return array
    size = array.shape[1] // 4
    me, left, right, _ = ring_places()
    parts = []
    for block in range(4):
        at = jnp.where(block == me, 0, jnp.where(block == left, 1, jnp.where(block == right, 2, 3)))
        parts.append(lax.dynamic_slice_in_dim(array, at * size, size, 1))
    return jnp.concatenate(parts, axis=1)


def gather_start(own):
    if lax.axis_size("dp") != 4:
        return ()
    right, left = ring_pairs(4)
    return lax.ppermute(own, "dp", right), lax.ppermute(own, "dp", left)


def gather_end(own, near):
    if lax.axis_size("dp") != 4:
        return lax.all_gather(own, "dp", axis=0, tiled=True)
    right, left = ring_pairs(4)
    half = own.shape[0] // 2
    from_left, from_right = near
    far_a = lax.ppermute(from_left[:half], "dp", right)
    far_b = lax.ppermute(from_right[half:], "dp", left)
    return jnp.concatenate([own, from_left, from_right, far_a, far_b])


def add_low(own, received):
    return (own.astype(F32) + received.astype(F32)).astype(BF)


class RingSum:
    def __init__(self, partial):
        self.ring = lax.axis_size("dp") == 4
        self.partial = partial
        rows = self.rows = partial.shape[0] // lax.axis_size("dp")
        half = self.half = rows // 2
        if self.ring:
            right, left = ring_pairs(4)
            far = 3 * rows
            self.far_a = lax.ppermute(partial[far : far + half], "dp", right)
            self.far_b = lax.ppermute(partial[far + half :], "dp", left)
            self.right_b = lax.ppermute(partial[2 * rows + half : far], "dp", right)
            self.left_a = lax.ppermute(partial[rows : rows + half], "dp", left)

    def second(self, *earlier):
        if self.ring:
            right, left = ring_pairs(4)
            rows, half = self.rows, self.half
            held = lax.optimization_barrier((self.partial, self.far_a, self.far_b) + earlier)
            part, far_a, far_b = held[:3]
            self.right_a = lax.ppermute(
                add_low(part[2 * rows : 2 * rows + half], far_a), "dp", right
            )
            self.left_b = lax.ppermute(add_low(part[rows + half : 2 * rows], far_b), "dp", left)

    def total(self, *earlier):
        if not self.ring:
            return lax.psum_scatter(self.partial, "dp", scatter_dimension=0, tiled=True)
        held = lax.optimization_barrier(
            (self.partial, self.right_a, self.right_b, self.left_a, self.left_b) + earlier
        )
        part, right_a, right_b, left_a, left_b = held[:5]
        from_left = jnp.concatenate([right_a, right_b]).astype(F32)
        from_right = jnp.concatenate([left_a, left_b]).astype(F32)
        return (part[: self.rows].astype(F32) + from_left + from_right).astype(BF)


def exchange(packed):
    turned = jnp.transpose(packed, (1, 0, 2)).reshape(-1, packed.shape[2])
    return lax.all_to_all(turned, "seq", 0, 0, tiled=True)


def to_rows(mine, ranks):
    turned = lax.all_to_all(mine, "seq", 0, 0, tiled=True)
    return turned.reshape(ranks, -1, mine.shape[1])


def sum_everywhere(values):
    count = lax.axis_size("dp")
    ranks = lax.axis_size("seq")
    if count & (count - 1) or ranks & (ranks - 1):
        return lax.all_gather(lax.psum(values, "dp"), "seq", axis=0, tiled=False)
    step = 1
    while step < count:
        values = values + lax.ppermute(values, "dp", [(i, i ^ step) for i in range(count)])
        step *= 2
    rank = lax.axis_index("seq")
    held = values.reshape(1, -1)
    step = 1
    while step < ranks:
        other = lax.ppermute(held, "seq", [(i, i ^ step) for i in range(ranks)])
        upper = (rank & step) != 0
        held = jnp.concatenate([jnp.where(upper, other, held), jnp.where(upper, held, other)])
        step *= 2
    return held


def causal_taps(pre, taps, offsets):
    summed = taps[0] * pre
    for by in range(1, KERNEL):
        delayed = jnp.pad(pre, ((by, 0), (0, 0)))[:-by]
        summed = summed + taps[by] * jnp.where((offsets >= by)[:, None], delayed, 0.0)
    return summed


class Pair:
    def __init__(self, value):
        self.value = value
        self.high = value.astype(BF)
        self.low = (value - self.high.astype(F32)).astype(BF)

def pair(x):
    return x if isinstance(x, Pair) else Pair(x)

def dot3(a, b, dims):
    a, b = pair(a), pair(b)
    d = lambda x, y: lax.dot_general(x, y, (dims, ((), ())), preferred_element_type=F32)
    return d(a.high, b.high) + (d(a.high, b.low) + d(a.low, b.high))

NN=((1,),(0,)); NT=((1,),(1,)); TN=((0,),(0,))

def stack(a, b):
    return jnp.concatenate([a, b], axis=0)

def masks(n):
    t = lax.broadcasted_iota(jnp.int32, (n, n), 0)
    s = lax.broadcasted_iota(jnp.int32, (n, n), 1)
    return t, s

def inverses(stricts, t, s, dot):
    n = t.shape[0]
    eye = jnp.where(t == s, 1.0, 0.0).astype(F32)
    same = (t // 8) == (s // 8)
    small = [Pair(jnp.where(same, a, 0.0)) for a in stricts]
    square = [Pair(dot(a, a, NN)) for a in small]
    fourth = [dot(a, a, NN) for a in square]
    first = [eye - a.value for a in small]
    inv = [f + dot(f, a, NN) for f, a in zip(first, square)]
    inv = [f + dot(f, a, NN) for f, a in zip(inv, fourth)]
    size = 8
    while size < n:
        take = ((t // (2 * size)) == (s // (2 * size))) & ((t // size) != (s // size))
        held = [Pair(f) for f in inv]
        part = [dot(f, jnp.where(take, a, 0.0), NN) for f, a in zip(held, stricts)]
        inv = [f.value - dot(p, f, NN) for f, p in zip(held, part)]
        size *= 2
    return inv

def decays(cols_block, hp, t, s, dot):
    n = t.shape[0]
    tri = jnp.where(t >= s, 1.0, 0.0).astype(F32)
    run = dot(tri, cols_block, NN)
    turned = jnp.transpose(run)
    offs = cols_block[:, 2 * hp : 2 * hp + 1]
    row = t[:, :1].astype(F32)
    gap = (t - s).astype(F32)
    same = (gap >= 0.0) & (offs >= gap)
    out = []
    for h in range(hp):
        g = run[:, hp + h : hp + h + 1]
        g_row = turned[hp + h : hp + h + 1, :]
        pairwise = jnp.where(same, jnp.exp(jnp.where(same, g - g_row, 0.0)), 0.0)
        start = jnp.where(offs > row, jnp.exp(g), 0.0)
        keep = offs[n - 1 : n, :] >= (n - 1.0) - row
        end = jnp.where(keep, jnp.exp(jnp.where(keep, g[n - 1 : n, :] - g, 0.0)), 0.0)
        out.append((pairwise, start, end, start[n - 1 : n, :], cols_block[:, h : h + 1]))
    return out

def fwd_kernel(hp, dk, dv, group, q_ref, k_ref, v_ref, cols_ref, mixed_ref, state_ref, upd_ref, inv_ref, seen_ref, p_ref, cur_ref):
    n = CHUNK
    total = q_ref.shape[0]
    chunks = total // n
    t, s = masks(n)
    dot = dot3

    def prepare(step, carry):
        jobs = []
        for j in range(group):
            rows = pl.ds(pl.multiple_of((step * group + j) * n, n), n)
            for h, d in enumerate(decays(cols_ref[rows, :], hp, t, s, dot)):
                jobs.append((step * group + j, rows, h) + d)
        ks = [k_ref[r, h * dk : (h + 1) * dk] for _, r, h, *_ in jobs]
        qs = [q_ref[r, h * dk : (h + 1) * dk] for _, r, h, *_ in jobs]
        both = [dot(stack(k, q), k, NT) for k, q in zip(ks, qs)]
        strict = [jnp.where(t > s, job[3] * b[:n], 0.0) * job[7] for job, b in zip(jobs, both)]
        inv = [Pair(i) for i in inverses(strict, t, s, dot)]
        for job, b, i, k in zip(jobs, both, inv, ks):
            c, r, h, pairwise, start, end, last, beta = job
            p_ref[c * hp + h] = pairwise * b[n:]
            inv_ref[c * hp + h] = i.value
            upd_ref[r, h * dv : (h + 1) * dv] = dot(i, beta * v_ref[r, h * dv : (h + 1) * dv], NN)
            seen_ref[r, h * dk : (h + 1) * dk] = dot(i, (beta * start) * k, NN)
        return carry

    lax.fori_loop(0, chunks // group, prepare, 0)
    cur_ref[...] = jnp.zeros_like(cur_ref)

    def advance(c, carry):
        rows = pl.ds(pl.multiple_of(c * n, n), n)
        for h, (pairwise, start, end, last, beta) in enumerate(decays(cols_ref[rows, :], hp, t, s, dot)):
            kk = slice(h * dk, (h + 1) * dk)
            vv = slice(h * dv, (h + 1) * dv)
            state = cur_ref[h]
            state_ref[c * hp + h] = state
            both = dot(stack(seen_ref[rows, kk], q_ref[rows, kk] * start), state, NN)
            update = Pair(upd_ref[rows, vv] - both[:n])
            upd_ref[rows, vv] = update.value
            mixed_ref[rows, vv] = both[n:] + dot(p_ref[c * hp + h], update, NN)
            cur_ref[h] = last * state + dot(k_ref[rows, kk] * end, update, TN)
        return carry

    lax.fori_loop(0, chunks, advance, 0)

def bwd_kernel(hp, dk, dv, group, q_ref, k_ref, v_ref, cols_ref, state_ref, upd_ref, inv_ref, seen_ref, dm_ref,
               dq_ref, dk_ref, dv_ref, dcols_ref, du_ref, ds_ref, cur_ref):
    n = CHUNK
    total = q_ref.shape[0]
    chunks = total // n
    t, s = masks(n)
    dot = dot3
    cur_ref[...] = jnp.zeros_like(cur_ref)

    def retreat(step, carry):
        c = chunks - 1 - step
        rows = pl.ds(pl.multiple_of(c * n, n), n)
        for h, (pairwise, start, end, last, beta) in enumerate(decays(cols_ref[rows, :], hp, t, s, dot)):
            kk = slice(h * dk, (h + 1) * dk)
            vv = slice(h * dv, (h + 1) * dv)
            d_state = cur_ref[h]
            ds_ref[c * hp + h] = d_state
            dm = Pair(dm_ref[rows, vv])
            k = k_ref[rows, kk]
            p = pairwise * dot(q_ref[rows, kk], k, NT)
            du = dot(p, dm, TN) + dot(k * end, d_state, NN)
            du_ref[rows, vv] = du
            cur_ref[h] = last * d_state + dot(q_ref[rows, kk] * start, dm, TN) - dot(seen_ref[rows, kk], du, TN)
        return carry

    lax.fori_loop(0, chunks, retreat, 0)
    lane = lax.broadcasted_iota(jnp.int32, (n, LANES), 1)

    def finish(step, carry):
        for j in range(group):
            c = step * group + j
            rows = pl.ds(pl.multiple_of(c * n, n), n)
            d_cols = jnp.zeros((n, LANES), F32)
            for h, (pairwise, start, end, last, beta) in enumerate(decays(cols_ref[rows, :], hp, t, s, dot)):
                kk = slice(h * dk, (h + 1) * dk)
                vv = slice(h * dv, (h + 1) * dv)
                q, k, v, dm = q_ref[rows, kk], k_ref[rows, kk], v_ref[rows, vv], dm_ref[rows, vv]
                q_p, k_p, u_p = Pair(q), Pair(k), Pair(upd_ref[rows, vv])
                state = Pair(state_ref[c * hp + h])
                d_state = Pair(ds_ref[c * hp + h])
                w = dot(inv_ref[c * hp + h], du_ref[rows, vv], TN)
                scores = dot(stack(w, dm), u_p, NT)
                d_a = jnp.where(t > s, -scores[:n], 0.0)
                d_p = scores[n:]
                keys = dot(stack(k, q), k_p, NT)
                seen = dot(stack(k, q), state, NN)
                r, qs = seen[:n], seen[n:]
                d_r = -(beta * start) * w
                back = dot(stack(start * dm, d_r), state, NT)
                x = dot(u_p, d_state, NT)
                d_qk = pairwise * d_p
                d_kk = beta * (pairwise * d_a)
                dq_ref[rows, kk] = back[:n] + dot(d_qk, k_p, NN)
                dk_ref[rows, kk] = back[n:] + dot(d_qk, q_p, TN) + dot(d_kk + jnp.transpose(d_kk), k_p, NN) + end * x
                dv_ref[rows, vv] = beta * w
                inner = pairwise * d_a * keys[:n]
                d_beta = jnp.sum(w * (v - start * r), axis=1, keepdims=True) + jnp.sum(inner, axis=1, keepdims=True)
                d_start = jnp.sum(dm * qs, axis=1, keepdims=True) - beta * jnp.sum(w * r, axis=1, keepdims=True)
                e = pairwise * d_p * keys[n:] + beta * inner
                d_end = end * jnp.sum(k * x, axis=1, keepdims=True)
                d_g = (jnp.sum(e, axis=1, keepdims=True) - jnp.sum(jnp.transpose(e), axis=1, keepdims=True)
                       + d_start * start - d_end)
                tail = jnp.sum(d_end, axis=0, keepdims=True) + last * jnp.sum(
                    jnp.sum(state.value * d_state.value, axis=1, keepdims=True), axis=0, keepdims=True)
                d_g = d_g + jnp.where(t[:, :1] == n - 1, tail, 0.0)
                d_cols = jnp.where(lane == h, d_beta, d_cols)
                d_cols = jnp.where(lane == hp + h, d_g, d_cols)
            tri = jnp.where(t >= s, 1.0, 0.0).astype(F32)
            dcols_ref[rows, :] = jnp.where(lane < hp, d_cols, dot(tri, d_cols, TN))
        return carry

    lax.fori_loop(0, chunks // group, finish, 0)

LIMIT = 60 * 2**20

def delta_forward(q, k, v, cols, hp):
    total = q.shape[0]
    dk, dv = q.shape[1] // hp, v.shape[1] // hp
    jobs = total // CHUNK * hp
    sd = jax.ShapeDtypeStruct
    return pl.pallas_call(
        functools.partial(fwd_kernel, hp, dk, dv, 2),
        out_shape=(sd((total, hp * dv), F32), sd((jobs, dk, dv), F32), sd((total, hp * dv), F32),
                   sd((jobs, CHUNK, CHUNK), F32), sd((total, hp * dk), F32)),
        scratch_shapes=[pltpu.VMEM((jobs, CHUNK, CHUNK), F32), pltpu.VMEM((hp, dk, dv), F32)],
        compiler_params=pltpu.CompilerParams(vmem_limit_bytes=LIMIT),
        cost_estimate=pl.CostEstimate(
            flops=total * hp * 9_000_000, transcendentals=total * hp * CHUNK, bytes_accessed=total * hp * 10_000
        ),
        name="delta_forward",
    )(q, k, v, cols)

def delta_backward(q, k, v, cols, saved, dm, hp):
    total = q.shape[0]
    dk, dv = q.shape[1] // hp, v.shape[1] // hp
    jobs = total // CHUNK * hp
    sd = jax.ShapeDtypeStruct
    return pl.pallas_call(
        functools.partial(bwd_kernel, hp, dk, dv, 1),
        out_shape=(sd((total, hp * dk), F32), sd((total, hp * dk), F32), sd((total, hp * dv), F32), sd((total, LANES), F32)),
        scratch_shapes=[pltpu.VMEM((total, hp * dv), F32), pltpu.VMEM((jobs, dk, dv), F32), pltpu.VMEM((hp, dk, dv), F32)],
        compiler_params=pltpu.CompilerParams(vmem_limit_bytes=LIMIT),
        cost_estimate=pl.CostEstimate(
            flops=total * hp * 14_000_000, transcendentals=total * hp * CHUNK, bytes_accessed=total * hp * 15_000
        ),
        name="delta_backward",
    )(q, k, v, cols, *saved, dm)


def local(
    tokens,
    attn_gain,
    w_query,
    w_key,
    w_value,
    w_decay,
    w_beta,
    w_gate,
    w_out,
    conv_query,
    conv_key,
    conv_value,
    decay_log,
    decay_bias,
    out_gain,
    mlp_gain,
    w_hidden,
    w_up,
    w_down,
    offsets,
    cotangent,
):
    ranks = lax.axis_size("seq")
    rank = lax.axis_index("seq")
    heads = decay_log.shape[0]
    width = tokens.shape[-1]
    tok = tokens.shape[1]
    length = tok * ranks
    plan = Plan(ranks, heads, w_query.shape[1] // heads, out_gain.shape[0], w_hidden.shape[1])
    hp, vs, dk, dv, ff = plan.hp, plan.vs, plan.key_dim, plan.dv, plan.ff
    rows = w_query.shape[0]

    own_tokens = to_ring(tokens[0])
    own_cot = to_ring(cotangent[0])
    rider = jnp.concatenate(
        [
            (offsets[0] // 64).astype(BF)[:, None],
            (offsets[0] % 64).astype(BF)[:, None],
            jnp.zeros((tok, LANES - 2), BF),
        ],
        axis=1,
    )
    small = jnp.concatenate(
        [
            plan.split_keys(w_decay),
            plan.split_keys(w_beta),
            jnp.broadcast_to(attn_gain[:, None, None], (rows, ranks, 1)),
            jnp.broadcast_to(mlp_gain[:, None, None], (rows, ranks, 1)),
            jnp.zeros((rows, ranks, LANES - 2 - 2 * hp), BF),
        ],
        axis=2,
    )
    mix_own = exchange(
        jnp.concatenate(
            [
                plan.split_keys(w_query),
                plan.split_keys(w_key),
                plan.split_even(w_value),
                small,
            ],
            axis=2,
        )
    )
    gathered = lax.all_gather(
        after(jnp.concatenate([own_tokens, rider], axis=1), mix_own), "seq", axis=0, tiled=True
    )
    w_mix = gather_end(mix_own, gather_start(mix_own))
    side_own = exchange(
        after(
            jnp.concatenate([plan.split_even(w_gate), plan.split_even(w_out)], axis=2), gathered
        )
    )
    side_own = after(side_own, w_mix)
    w_side = gather_end(side_own, gather_start(side_own))
    mlp_own_cols = exchange(
        after(
            jnp.concatenate(
                [plan.split_even(w_hidden), plan.split_even(w_up), plan.split_even(w_down)],
                axis=2,
            ),
            side_own,
        )
    )
    mlp_near = gather_start(after(mlp_own_cols, w_side))
    cot_all = lax.all_gather(after(own_cot, side_own), "seq", axis=0, tiled=True)

    at_k = hp * dk
    at_v = 2 * hp * dk
    at_s = at_v + hp * dv
    attn_gain_full = w_mix[:, at_s + 2 * hp].astype(F32)
    mlp_gain_full = w_mix[:, at_s + 2 * hp + 1].astype(F32)
    gate_cols = w_side[:, : hp * dv]
    out_cols = w_side[:, hp * dv :]

    tokens_all = gathered[:, :width].astype(F32)
    offs = (
        gathered[:, width].astype(F32) * 64.0 + gathered[:, width + 1].astype(F32)
    ).astype(jnp.int32)
    normed_all = tokens_all * rms_scale(tokens_all)
    attn = (normed_all * attn_gain_full).astype(BF)
    pre = nn(attn, w_mix)
    pre_query = pre[:, :at_k].astype(BF).astype(F32)
    pre_key = pre[:, at_k:at_v].astype(BF).astype(F32)
    pre_value = pre[:, at_v:at_s].astype(BF).astype(F32)
    pre_gate = nn(attn, gate_cols)
    pre_decay = pre[:, at_s : at_s + hp]
    pre_beta = pre[:, at_s + hp : at_s + 2 * hp]

    group = rank // vs
    taps_query = lax.dynamic_slice_in_dim(conv_query, group * hp * dk, hp * dk, 1)
    taps_key = lax.dynamic_slice_in_dim(conv_key, group * hp * dk, hp * dk, 1)
    taps_value = lax.dynamic_slice_in_dim(conv_value, rank * hp * dv, hp * dv, 1)
    own_log = lax.dynamic_slice_in_dim(decay_log, group * hp, hp, 0)
    own_bias = lax.dynamic_slice_in_dim(decay_bias, group * hp, hp, 0)
    own_gain = lax.dynamic_slice_in_dim(out_gain, (rank % vs) * dv, dv, 0)

    def by_head(array):
        return array.reshape(length, hp, -1)

    def flat(array):
        return array.reshape(length, -1)

    def unit(array):
        array = by_head(array)
        return flat(array * lax.rsqrt(jnp.sum(array * array, axis=-1, keepdims=True) + 1e-06))

    def front(query_in, key_in, value_in, tq, tk, tv, decay_in, beta_in, log_rates, rate_bias):
        q = unit(silu(causal_taps(query_in, tq, offs))) * dk ** (-0.5)
        k = unit(silu(causal_taps(key_in, tk, offs)))
        v = silu(causal_taps(value_in, tv, offs))
        beta = jax.nn.sigmoid(beta_in)
        logs = -jnp.exp(log_rates) * jax.nn.softplus(decay_in + rate_bias)
        return q, k, v, beta, logs

    fronted_free, front_back = jax.vjp(
        front,
        pre_query,
        pre_key,
        pre_value,
        taps_query,
        taps_key,
        taps_value,
        pre_decay,
        pre_beta,
        own_log,
        own_bias,
    )
    query_rows, key_rows, value_rows, beta_rows, logdecay = lax.optimization_barrier(
        tuple(fronted_free) + (side_own,)
    )[:5]
    cols = jnp.concatenate(
        [
            beta_rows,
            logdecay,
            offs.astype(F32)[:, None],
            jnp.zeros((length, LANES - 2 * hp - 1), F32),
        ],
        axis=1,
    )
    mixed_flat, *saved = delta_forward(query_rows, key_rows, value_rows, cols, hp)
    mixed_flat = after(mixed_flat, mlp_own_cols, cot_all)
    mixed = by_head(mixed_flat)
    gate = by_head(pre_gate)
    mix_scale = lax.rsqrt(
        plan.value_sum(jnp.sum(mixed * mixed, axis=-1, keepdims=True)) / plan.value_dim + 1e-05
    )
    m = mixed * mix_scale
    sg = silu(gate)
    gated = flat(m * own_gain * sg).astype(BF)
    branch = lax.psum_scatter(
        nt(gated, out_cols).astype(BF), "seq", scatter_dimension=0, tiled=True
    )
    inputs = own_tokens.astype(F32)
    middle = inputs + branch.astype(F32)
    r2 = rms_scale(middle)
    n2 = middle * r2
    near_and_cot = lax.optimization_barrier(
        ((n2 * mlp_gain_full).astype(BF), cot_all) + tuple(mlp_near)
    )
    mlp_own, cot_all, mlp_near = near_and_cot[0], near_and_cot[1], near_and_cot[2:]
    mlp_cols = gather_end(mlp_own_cols, mlp_near)
    mlp_all = lax.all_gather(mlp_own, "seq", axis=0, tiled=True)
    both_w = mlp_cols[:, : 2 * ff]
    down_w = mlp_cols[:, 2 * ff :]
    d_product = nn(cot_all, down_w)
    both_pre = nn(mlp_all, both_w)
    hidden_pre = both_pre[:, :ff]
    up_pre = both_pre[:, ff:]
    sh = silu(hidden_pre)
    product = (sh * up_pre).astype(BF)
    d_both = jnp.concatenate(
        [
            (d_product * up_pre * silu_slope(hidden_pre)).astype(BF),
            (d_product * sh).astype(BF),
        ],
        axis=1,
    )
    d_mlp = lax.psum_scatter(
        nt(d_both, both_w).astype(BF), "seq", scatter_dimension=0, tiled=True
    ).astype(F32)
    d_output = own_cot.astype(F32)
    e2 = d_mlp * mlp_gain_full
    d_middle = d_output + r2 * (e2 - n2 * jnp.mean(e2 * n2, axis=-1, keepdims=True))
    d_branch_all = lax.all_gather(d_middle.astype(BF), "seq", axis=0, tiled=True)
    both_sum = RingSum(tn(mlp_all, d_both).astype(BF))
    down_sum = RingSum(tn(cot_all, product).astype(BF))
    mlp_out = lax.psum_scatter(
        after(nt(product, down_w).astype(BF), d_branch_all), "seq", scatter_dimension=0, tiled=True
    )
    output = from_ring((middle + mlp_out.astype(F32)).astype(BF))

    d_gated = by_head(nn(d_branch_all, out_cols))
    grad_out_gain = jnp.sum(d_gated * m * sg, axis=(0, 1))
    em = d_gated * own_gain * sg
    em_mean = plan.value_sum(jnp.sum(em * m, axis=-1, keepdims=True)) / plan.value_dim
    d_mixed = flat(mix_scale * (em - m * em_mean))
    d_gate = flat(d_gated * m * own_gain * silu_slope(gate)).astype(BF)
    side_sum = RingSum(
        jnp.concatenate([tn(attn, d_gate).astype(BF), tn(d_branch_all, gated).astype(BF)], axis=1)
    )
    d_attn_gate = nt(d_gate, gate_cols)
    both_sum.second(d_mixed)
    down_sum.second(d_mixed)
    d_query, d_key, d_value, d_cols = delta_backward(
        query_rows, key_rows, value_rows, cols, saved, d_mixed, hp
    )
    side_sum.second(d_cols)
    both_rows = to_rows(both_sum.total(d_cols), ranks)
    down_rows = to_rows(down_sum.total(d_cols), ranks)
    ruled = lax.optimization_barrier((d_query, d_key, d_value, d_cols, mlp_out))
    back = front_back(
        (ruled[0], ruled[1], ruled[2], ruled[3][:, :hp], ruled[3][:, hp : 2 * hp])
    )
    d_pre = jnp.concatenate(
        [
            back[0],
            back[1],
            back[2],
            back[6],
            back[7],
            jnp.zeros((length, LANES - 2 * hp), F32),
        ],
        axis=1,
    ).astype(BF)
    side_rows = to_rows(side_sum.total(d_pre), ranks)
    mix_sum = RingSum(tn(attn, d_pre).astype(BF))
    mix_sum.second()
    mix_rows = to_rows(mix_sum.total(), ranks)
    d_attn = lax.psum_scatter(
        (d_attn_gate + nt(d_pre, w_mix)).astype(BF), "seq", scatter_dimension=0, tiled=True
    ).astype(F32)

    n = inputs * rms_scale(inputs)
    e = d_attn * attn_gain_full
    grad_tokens = from_ring(
        (d_middle + rms_scale(inputs) * (e - n * jnp.mean(e * n, axis=-1, keepdims=True))).astype(BF)
    )

    sums = jnp.concatenate(
        [
            back[3].reshape(-1),
            back[4].reshape(-1),
            back[5].reshape(-1),
            back[8],
            back[9],
            grad_out_gain,
        ]
    )
    every = sum_everywhere(jnp.pad(sums, (0, -sums.shape[0] % 1024)))

    def per_head(part, lead):
        part = part.reshape(ranks // vs, vs, lead, -1).sum(axis=1)
        return jnp.transpose(part, (1, 0, 2)).reshape(lead, -1)

    a0 = KERNEL * hp * dk
    a1 = 2 * a0
    a2 = a1 + KERNEL * hp * dv
    grad_conv_value = jnp.transpose(
        every[:, a1:a2].reshape(ranks, KERNEL, -1), (1, 0, 2)
    ).reshape(KERNEL, -1)
    gain_sum = every[:, a2 + 2 * hp : a2 + 2 * hp + dv].reshape(ranks // vs, vs, dv).sum(axis=0).reshape(-1)
    grad_query = plan.join_keys(mix_rows[:, :, :at_k])
    grad_key = plan.join_keys(mix_rows[:, :, at_k:at_v])
    grad_value = plan.join_even(mix_rows[:, :, at_v:at_s])
    grad_decay = plan.join_keys(mix_rows[:, :, at_s : at_s + hp])
    grad_beta = plan.join_keys(mix_rows[:, :, at_s + hp : at_s + 2 * hp])
    grad_gate = plan.join_even(side_rows[:, :, : hp * dv])
    grad_hidden = plan.join_even(both_rows[:, :, :ff])
    grad_up = plan.join_even(both_rows[:, :, ff:])

    def gain_grad(gain, pairs):
        total = sum(jnp.sum(w.astype(F32) * g, axis=1) for w, g in pairs)
        return total / gain.astype(F32)

    return (
        output[None],
        grad_tokens[None],
        gain_grad(
            attn_gain,
            (
                (w_query, grad_query),
                (w_key, grad_key),
                (w_value, grad_value),
                (w_decay, grad_decay),
                (w_beta, grad_beta),
                (w_gate, grad_gate),
            ),
        ),
        grad_query,
        grad_key,
        grad_value,
        grad_decay,
        grad_beta,
        grad_gate,
        plan.join_even(side_rows[:, :, hp * dv :]),
        per_head(every[:, :a0], KERNEL),
        per_head(every[:, a0:a1], KERNEL),
        grad_conv_value,
        per_head(every[:, a2 : a2 + hp], 1)[0],
        per_head(every[:, a2 + hp : a2 + 2 * hp], 1)[0],
        gain_sum,
        gain_grad(mlp_gain, ((w_hidden, grad_hidden), (w_up, grad_up))),
        grad_hidden,
        grad_up,
        plan.join_even(down_rows),
    )


def solution(mesh):
    flat = ("dp", "seq")
    tok_spec = P("dp", "seq", None)
    row_spec = P(flat, None)
    gain_spec = P(flat)
    in_specs = (
        (tok_spec, gain_spec)
        + (row_spec,) * 7
        + (P(),) * 6
        + (gain_spec,)
        + (row_spec,) * 3
        + (P("dp", "seq"), tok_spec)
    )
    out_specs = (
        (tok_spec, tok_spec, gain_spec)
        + (row_spec,) * 7
        + (P(),) * 6
        + (gain_spec,)
        + (row_spec,) * 3
    )
    return jax.shard_map(local, mesh=mesh, in_specs=in_specs, out_specs=out_specs, check_vma=False)
```

```python
import functools

import jax
import jax.numpy as jnp
from jax import lax
from jax.experimental import pallas as pl
from jax.experimental.pallas import tpu as pltpu
from jax.sharding import PartitionSpec as P

KERNEL = 4
LANES = 128
BF = jnp.bfloat16
F32 = jnp.float32
CHUNK = 128


def rms_scale(value):
    return lax.rsqrt(jnp.mean(value * value, axis=-1, keepdims=True) + 1e-05)


def dot_f32(left, right, dims):
    return lax.dot_general(left, right, (dims, ((), ())), preferred_element_type=F32)


def nn(left, right):
    return dot_f32(left, right, ((1,), (0,)))


def nt(left, right):
    return dot_f32(left, right, ((1,), (1,)))


def tn(left, right):
    return dot_f32(left, right, ((0,), (0,)))


def silu(value):
    return value * jax.nn.sigmoid(value)


def silu_slope(value):
    s = jax.nn.sigmoid(value)
    return s * (1.0 + value * (1.0 - s))


class Plan:
    def __init__(self, ranks, heads, key_dim, value_dim, hidden):
        self.ranks = ranks
        self.heads = heads
        self.key_dim = key_dim
        self.hp = max(1, heads // ranks)
        self.vs = max(1, ranks // heads)
        self.dv = value_dim // self.vs
        self.value_dim = value_dim
        self.ff = hidden // ranks

    def split_keys(self, array):
        rows = array.shape[0]
        grouped = array.reshape(rows, self.heads // self.hp, -1)
        return jnp.repeat(grouped, self.vs, axis=1) if self.vs > 1 else grouped

    def split_even(self, array):
        return array.reshape(array.shape[0], self.ranks, -1)

    def join_keys(self, array):
        ranks, rows, width = array.shape
        array = array.astype(F32)
        if self.vs > 1:
            array = array.reshape(ranks // self.vs, self.vs, rows, width).sum(axis=1)
        return jnp.transpose(array, (1, 0, 2)).reshape(rows, -1)

    def join_even(self, array):
        return jnp.transpose(array, (1, 0, 2)).reshape(array.shape[1], -1).astype(F32)

    def value_sum(self, array):
        step = 1
        while step < self.vs:
            pairs = [(i, i ^ step) for i in range(self.ranks)]
            array = array + lax.ppermute(array, "seq", pairs)
            step *= 2
        return array


def after(value, *earlier):
    return lax.optimization_barrier((value,) + earlier)[0]


def ring_order(count):
    return [0, 1, 3, 2] if count == 4 else list(range(count))


def ring_pairs(count):
    order = ring_order(count)
    right = [(order[i], order[(i + 1) % count]) for i in range(count)]
    return right, [(there, here) for here, there in right]


def ring_place():
    me = lax.axis_index("dp")
    return me ^ (me >> 1)


def swap_blocks(array):
    size = array.shape[1] // 4
    return jnp.concatenate(
        [array[:, : 2 * size], array[:, 3 * size :], array[:, 2 * size : 3 * size]], axis=1
    )


def to_ring(array):
    if lax.axis_size("dp") != 4:
        return array
    width = array.shape[1]
    turned = swap_blocks(array)
    twice = jnp.concatenate([turned, turned], axis=1)
    return lax.dynamic_slice_in_dim(twice, ring_place() * (width // 4), width, 1)


def from_ring(array):
    if lax.axis_size("dp") != 4:
        return array
    width = array.shape[1]
    twice = jnp.concatenate([array, array], axis=1)
    at = (4 - ring_place()) * (width // 4)
    return swap_blocks(lax.dynamic_slice_in_dim(twice, at, width, 1))


def gather_start(own):
    if lax.axis_size("dp") != 4:
        return ()
    right, left = ring_pairs(4)
    return lax.ppermute(own, "dp", right), lax.ppermute(own, "dp", left)


def gather_end(own, near):
    if lax.axis_size("dp") != 4:
        return lax.all_gather(own, "dp", axis=0, tiled=True)
    right, left = ring_pairs(4)
    half = own.shape[0] // 2
    from_left, from_right = near
    far_a = lax.ppermute(from_left[:half], "dp", right)
    far_b = lax.ppermute(from_right[half:], "dp", left)
    return jnp.concatenate([own, from_right, far_a, far_b, from_left])


class RingGrad:
    def __init__(self, left, right):
        self.ring = lax.axis_size("dp") == 4
        self.left, self.right = left, right
        rows = self.rows = left.shape[1] // lax.axis_size("dp")
        self.half = rows // 2
        self.sent, self.near, self.late = (), (), ()
        if self.ring:
            to_right, to_left = ring_pairs(4)
            self.sent = tuple(self.part(i).astype(BF) for i in (4, 5, 3, 6))
            self.near = (
                lax.ppermute(self.sent[0], "dp", to_right),
                lax.ppermute(self.sent[1], "dp", to_left),
                lax.ppermute(self.sent[2], "dp", to_right),
                lax.ppermute(self.sent[3], "dp", to_left),
            )

    def part(self, index):
        at = index * self.half
        return tn(self.left[:, at : at + self.half], self.right)

    def second(self, *earlier):
        if self.ring:
            to_right, to_left = ring_pairs(4)
            far_a, far_b = lax.optimization_barrier(self.near[:2] + earlier)[:2]
            self.late = (
                lax.ppermute((self.part(2) + far_a.astype(F32)).astype(BF), "dp", to_right),
                lax.ppermute((self.part(7) + far_b.astype(F32)).astype(BF), "dp", to_left),
            )

    def total(self, *earlier):
        if not self.ring:
            whole = tn(self.left, self.right).astype(BF)
            return lax.psum_scatter(whole, "dp", scatter_dimension=0, tiled=True)
        held = lax.optimization_barrier(self.near[2:] + self.late + earlier)
        right_b, left_a, right_a, left_b = held[:4]
        own = tn(self.left[:, : self.rows], self.right)
        from_left = jnp.concatenate([right_a, right_b]).astype(F32)
        from_right = jnp.concatenate([left_a, left_b]).astype(F32)
        return (own + from_left + from_right).astype(BF)


def exchange(packed):
    turned = jnp.transpose(packed, (1, 0, 2)).reshape(-1, packed.shape[2])
    return lax.all_to_all(turned, "seq", 0, 0, tiled=True)


def to_rows(mine, ranks):
    turned = lax.all_to_all(mine, "seq", 0, 0, tiled=True)
    return turned.reshape(ranks, -1, mine.shape[1])


def sum_everywhere(values):
    count = lax.axis_size("dp")
    ranks = lax.axis_size("seq")
    if count & (count - 1) or ranks & (ranks - 1):
        return lax.all_gather(lax.psum(values, "dp"), "seq", axis=0, tiled=False)
    step = 1
    while step < count:
        values = values + lax.ppermute(values, "dp", [(i, i ^ step) for i in range(count)])
        step *= 2
    rank = lax.axis_index("seq")
    held = values.reshape(1, -1)
    step = 1
    while step < ranks:
        other = lax.ppermute(held, "seq", [(i, i ^ step) for i in range(ranks)])
        upper = (rank & step) != 0
        held = jnp.concatenate([jnp.where(upper, other, held), jnp.where(upper, held, other)])
        step *= 2
    return held


class Pair:
    def __init__(self, value):
        self.value = value
        self.high = value.astype(BF)
        self.low = (value - self.high.astype(F32)).astype(BF)


def pair(value):
    return value if isinstance(value, Pair) else Pair(value)


NN = ((1,), (0,))
NT = ((1,), (1,))
TN = ((0,), (0,))


def dot(left, right, dims):
    a, b = pair(left), pair(right)
    return dot_f32(a.high, b.high, dims) + (
        dot_f32(a.high, b.low, dims) + dot_f32(a.low, b.high, dims)
    )


def stack(top, bottom):
    return jnp.concatenate([top, bottom], axis=0)


def grids(n):
    t = lax.broadcasted_iota(jnp.int32, (n, n), 0)
    s = lax.broadcasted_iota(jnp.int32, (n, n), 1)
    return t, s


def inverses(stricts, t, s):
    n = t.shape[0]
    eye = jnp.where(t == s, 1.0, 0.0).astype(F32)
    same = (t // 8) == (s // 8)
    small = [Pair(jnp.where(same, a, 0.0)) for a in stricts]
    square = [Pair(dot(a, a, NN)) for a in small]
    fourth = [dot(a, a, NN) for a in square]
    first = [eye - a.value for a in small]
    inv = [f + dot(f, a, NN) for f, a in zip(first, square)]
    inv = [f + dot(f, a, NN) for f, a in zip(inv, fourth)]
    size = 8
    while size < n:
        take = ((t // (2 * size)) == (s // (2 * size))) & ((t // size) != (s // size))
        held = [Pair(f) for f in inv]
        part = [dot(f, jnp.where(take, a, 0.0), NN) for f, a in zip(held, stricts)]
        inv = [f.value - dot(p, f, NN) for f, p in zip(held, part)]
        size *= 2
    return inv


def decays(cols, hp, t, s):
    n = t.shape[0]
    tri = jnp.where(t >= s, 1.0, 0.0).astype(F32)
    run = dot(tri, cols, NN)
    turned = jnp.transpose(run)
    offs = cols[:, 2 * hp : 2 * hp + 1]
    row = t[:, :1].astype(F32)
    gap = (t - s).astype(F32)
    same = (gap >= 0.0) & (offs >= gap)
    keep = offs[n - 1 : n, :] >= (n - 1.0) - row
    out = []
    for h in range(hp):
        g = run[:, h : h + 1]
        g_row = turned[h : h + 1, :]
        pairwise = jnp.where(same, jnp.exp(jnp.where(same, g - g_row, 0.0)), 0.0)
        start = jnp.where(offs > row, jnp.exp(g), 0.0)
        end = jnp.where(keep, jnp.exp(jnp.where(keep, g[n - 1 : n, :] - g, 0.0)), 0.0)
        out.append((pairwise, start, end, start[n - 1 : n, :], cols[:, hp + h : hp + h + 1]))
    return out


def lanes_of(hp, dk, dv):
    q = [slice(h * dk, (h + 1) * dk) for h in range(hp)]
    k = [slice((hp + h) * dk, (hp + h + 1) * dk) for h in range(hp)]
    v = [slice(2 * hp * dk + h * dv, 2 * hp * dk + (h + 1) * dv) for h in range(hp)]
    return q, k, v


def chunk_rows(c):
    return pl.ds(pl.multiple_of(c * CHUNK, CHUNK), CHUNK)


def chunk_cols(hp, rows, small_ref, rider_ref, const_ref):
    lane = lax.broadcasted_iota(jnp.int32, (CHUNK, LANES), 1)
    x = small_ref[rows, :]
    y = x + const_ref[1:2, :]
    logs = const_ref[0:1, :] * (jnp.maximum(y, 0.0) + jnp.log1p(jnp.exp(-jnp.abs(y))))
    beta = jax.nn.sigmoid(x)
    rider = rider_ref[rows, :].astype(F32)
    offs = rider[:, 0:1] * 64.0 + rider[:, 1:2]
    cols = jnp.where(lane < hp, logs, jnp.where(lane < 2 * hp, beta, 0.0))
    return jnp.where(lane == 2 * hp, offs, cols), offs


def conved_lanes(c, lanes, offs, pre_ref, taps_ref):
    rows = chunk_rows(c)
    above = pl.ds(pl.multiple_of(jnp.maximum(c * CHUNK - 16, 0), 16), 16)
    block = pre_ref[rows, lanes].astype(F32)
    ext = stack(pre_ref[above, lanes].astype(F32), block)
    total = taps_ref[0:1, lanes] * block
    for by in range(1, KERNEL):
        moved = pltpu.roll(ext, by, 0)[16:]
        total = total + taps_ref[by : by + 1, lanes] * jnp.where(offs >= by, moved, 0.0)
    return total


def unit_scale(u):
    return lax.rsqrt(jnp.sum(u * u, axis=1, keepdims=True) + 1e-06)


def fill_front(hp, dk, dv, c, pre_ref, small_ref, rider_ref, taps_ref, const_ref, qkv_ref, cols_ref, conv_ref):
    rows = chunk_rows(c)
    cols, offs = chunk_cols(hp, rows, small_ref, rider_ref, const_ref)
    cols_ref[rows, :] = cols
    for kind, slices in enumerate(lanes_of(hp, dk, dv)):
        for lanes in slices:
            conved = conved_lanes(c, lanes, offs, pre_ref, taps_ref)
            if conv_ref is not None:
                conv_ref[rows, lanes] = conved
            u = conved * jax.nn.sigmoid(conved)
            if kind == 0:
                u = u * (unit_scale(u) * dk ** (-0.5))
            elif kind == 1:
                u = u * unit_scale(u)
            qkv_ref[rows, lanes] = u


def fwd_kernel(
    hp, dk, dv, pre_ref, small_ref, rider_ref, taps_ref, const_ref,
    mixed_ref, state_ref, upd_ref, inv_ref, seen_ref,
    qkv_ref, cols_ref, p_ref, cur_ref,
):
    n = CHUNK
    chunks = pre_ref.shape[0] // n
    group = 2 if chunks % 2 == 0 else 1
    t, s = grids(n)
    q_at, k_at, v_at = lanes_of(hp, dk, dv)

    def prepare(step, carry):
        jobs = []
        for j in range(group):
            c = step * group + j
            fill_front(
                hp, dk, dv, c, pre_ref, small_ref, rider_ref, taps_ref, const_ref, qkv_ref, cols_ref, None
            )
            rows = chunk_rows(c)
            for h, d in enumerate(decays(cols_ref[rows, :], hp, t, s)):
                jobs.append((c, rows, h) + d)
        keys = [qkv_ref[r, k_at[h]] for _, r, h, *_ in jobs]
        both = [dot(stack(k, qkv_ref[job[1], q_at[job[2]]]), k, NT) for k, job in zip(keys, jobs)]
        strict = [jnp.where(t > s, job[3] * b[:n], 0.0) * job[7] for job, b in zip(jobs, both)]
        inv = [Pair(i) for i in inverses(strict, t, s)]
        for job, b, i, k in zip(jobs, both, inv, keys):
            c, r, h, pairwise, start, end, last, beta = job
            p_ref[c * hp + h] = pairwise * b[n:]
            inv_ref[c * hp + h] = i.value
            upd_ref[r, h * dv : (h + 1) * dv] = dot(i, beta * qkv_ref[r, v_at[h]], NN)
            seen_ref[r, h * dk : (h + 1) * dk] = dot(i, (beta * start) * k, NN)
        return carry

    lax.fori_loop(0, chunks // group, prepare, 0)
    cur_ref[...] = jnp.zeros_like(cur_ref)

    def advance(c, carry):
        rows = chunk_rows(c)
        for h, (pairwise, start, end, last, beta) in enumerate(decays(cols_ref[rows, :], hp, t, s)):
            vv = slice(h * dv, (h + 1) * dv)
            state = cur_ref[h]
            state_ref[c * hp + h] = state
            seen = seen_ref[rows, h * dk : (h + 1) * dk]
            both = dot(stack(seen, qkv_ref[rows, q_at[h]] * start), state, NN)
            update = Pair(upd_ref[rows, vv] - both[:n])
            upd_ref[rows, vv] = update.value
            mixed_ref[rows, vv] = both[n:] + dot(p_ref[c * hp + h], update, NN)
            cur_ref[h] = last * state + dot(qkv_ref[rows, k_at[h]] * end, update, TN)
        return carry

    lax.fori_loop(0, chunks, advance, 0)


def bwd_kernel(
    hp, dk, dv, pre_ref, small_ref, rider_ref, taps_ref, const_ref,
    state_ref, upd_ref, inv_ref, seen_ref, dm_ref,
    dpre_ref, dtaps_ref, sums_ref,
    qkv_ref, cols_ref, conv_ref, dcon_ref, dcols_ref, du_ref, ds_ref, cur_ref,
):
    n = CHUNK
    total = pre_ref.shape[0]
    chunks = total // n
    t, s = grids(n)
    q_at, k_at, v_at = lanes_of(hp, dk, dv)
    wide = 2 * hp * dk + hp * dv
    cur_ref[...] = jnp.zeros_like(cur_ref)
    dtaps_ref[...] = jnp.zeros_like(dtaps_ref)
    sums_ref[...] = jnp.zeros_like(sums_ref)
    dcon_ref[total:, :] = jnp.zeros((dcon_ref.shape[0] - total, wide), F32)
    cols_ref[total:, :] = jnp.zeros((cols_ref.shape[0] - total, LANES), F32)

    def retreat(step, carry):
        c = chunks - 1 - step
        rows = chunk_rows(c)
        fill_front(
            hp, dk, dv, c, pre_ref, small_ref, rider_ref, taps_ref, const_ref, qkv_ref, cols_ref, conv_ref
        )
        for h, (pairwise, start, end, last, beta) in enumerate(decays(cols_ref[rows, :], hp, t, s)):
            vv = slice(h * dv, (h + 1) * dv)
            d_state = cur_ref[h]
            ds_ref[c * hp + h] = d_state
            dm = Pair(dm_ref[rows, vv])
            q, k = qkv_ref[rows, q_at[h]], qkv_ref[rows, k_at[h]]
            p = pairwise * dot(q, k, NT)
            du = dot(p, dm, TN) + dot(k * end, d_state, NN)
            du_ref[rows, vv] = du
            seen = seen_ref[rows, h * dk : (h + 1) * dk]
            cur_ref[h] = last * d_state + dot(q * start, dm, TN) - dot(seen, du, TN)
        return carry

    lax.fori_loop(0, chunks, retreat, 0)
    lane = lax.broadcasted_iota(jnp.int32, (n, LANES), 1)

    def through_silu(rows, lanes, dy, unit):
        conved = conv_ref[rows, lanes]
        sig = jax.nn.sigmoid(conved)
        if unit:
            u = conved * sig
            scale = unit_scale(u)
            dy = scale * dy - (scale * scale * scale) * u * jnp.sum(u * dy, axis=1, keepdims=True)
        dcon_ref[rows, lanes] = dy * (sig * (1.0 + conved * (1.0 - sig)))

    def finish(c, carry):
        rows = chunk_rows(c)
        d_cols = jnp.zeros((n, LANES), F32)
        for h, (pairwise, start, end, last, beta) in enumerate(decays(cols_ref[rows, :], hp, t, s)):
            vv = slice(h * dv, (h + 1) * dv)
            q, k, v = qkv_ref[rows, q_at[h]], qkv_ref[rows, k_at[h]], qkv_ref[rows, v_at[h]]
            dm = dm_ref[rows, vv]
            q_p, k_p, u_p = Pair(q), Pair(k), Pair(upd_ref[rows, vv])
            state = Pair(state_ref[c * hp + h])
            d_state = Pair(ds_ref[c * hp + h])
            w = dot(inv_ref[c * hp + h], du_ref[rows, vv], TN)
            scores = dot(stack(w, dm), u_p, NT)
            d_a = jnp.where(t > s, -scores[:n], 0.0)
            d_p = scores[n:]
            keys = dot(stack(k, q), k_p, NT)
            met = dot(stack(k, q), state, NN)
            r, qs = met[:n], met[n:]
            back = dot(stack(start * dm, -(beta * start) * w), state, NT)
            x = dot(u_p, d_state, NT)
            d_qk = pairwise * d_p
            d_kk = beta * (pairwise * d_a)
            d_query = back[:n] + dot(d_qk, k_p, NN)
            d_key = (
                back[n:]
                + dot(d_qk, q_p, TN)
                + dot(d_kk + jnp.transpose(d_kk), k_p, NN)
                + end * x
            )
            through_silu(rows, q_at[h], d_query * dk ** (-0.5), True)
            through_silu(rows, k_at[h], d_key, True)
            through_silu(rows, v_at[h], beta * w, False)
            inner = pairwise * d_a * keys[:n]
            d_beta = jnp.sum(w * (v - start * r), axis=1, keepdims=True) + jnp.sum(
                inner, axis=1, keepdims=True
            )
            d_start = jnp.sum(dm * qs, axis=1, keepdims=True) - beta * jnp.sum(
                w * r, axis=1, keepdims=True
            )
            e = pairwise * d_p * keys[n:] + beta * inner
            d_end = end * jnp.sum(k * x, axis=1, keepdims=True)
            d_g = (
                jnp.sum(e, axis=1, keepdims=True)
                - jnp.sum(jnp.transpose(e), axis=1, keepdims=True)
                + d_start * start
                - d_end
            )
            held = jnp.sum(
                jnp.sum(state.value * d_state.value, axis=1, keepdims=True), axis=0, keepdims=True
            )
            tail = jnp.sum(d_end, axis=0, keepdims=True) + last * held
            d_g = d_g + jnp.where(t[:, :1] == n - 1, tail, 0.0)
            d_cols = jnp.where(lane == h, d_g, d_cols)
            d_cols = jnp.where(lane == hp + h, d_beta, d_cols)
        tri = jnp.where(t >= s, 1.0, 0.0).astype(F32)
        dcols_ref[rows, :] = jnp.where(lane < hp, dot(tri, d_cols, TN), d_cols)
        return carry

    lax.fori_loop(0, chunks, finish, 0)

    def spread(c, carry):
        rows = chunk_rows(c)
        below = pl.ds(pl.multiple_of((c + 1) * n, n), 8)
        cols = cols_ref[rows, :]
        offs = cols[:, 2 * hp : 2 * hp + 1]
        offs_below = cols_ref[below, 2 * hp : 2 * hp + 1]
        for slices in (q_at, k_at, v_at):
            for lanes in slices:
                pre = pre_ref[rows, lanes].astype(F32)
                d_con = dcon_ref[rows, lanes]
                d_below = dcon_ref[below, lanes]
                out = taps_ref[0:1, lanes] * d_con
                dtaps_ref[0:1, lanes] += jnp.sum(pre * d_con, axis=0, keepdims=True)
                for by in range(1, KERNEL):
                    ext = stack(
                        jnp.where(offs >= by, d_con, 0.0), jnp.where(offs_below >= by, d_below, 0.0)
                    )
                    moved = pltpu.roll(ext, n + 8 - by, 0)[:n]
                    out = out + taps_ref[by : by + 1, lanes] * moved
                    dtaps_ref[by : by + 1, lanes] += jnp.sum(pre * moved, axis=0, keepdims=True)
                dpre_ref[rows, lanes] = out.astype(BF)
        d_cols = dcols_ref[rows, :]
        slope = const_ref[0:1, :] * jax.nn.sigmoid(small_ref[rows, :] + const_ref[1:2, :])
        d_small = jnp.where(lane < hp, d_cols * slope, d_cols * cols * (1.0 - cols))
        d_small = jnp.where(lane < 2 * hp, d_small, 0.0)
        dpre_ref[rows, wide:] = d_small.astype(BF)
        sums_ref[0:1, :] += jnp.sum(d_small, axis=0, keepdims=True)
        sums_ref[1:2, :] += jnp.sum(d_cols * cols, axis=0, keepdims=True)
        return carry

    lax.fori_loop(0, chunks, spread, 0)


def gate_kernel(hp, dv, mixed_ref, gate_ref, gain_ref, out_ref):
    for h in range(hp):
        at = slice(h * dv, (h + 1) * dv)
        mixed = mixed_ref[:, at]
        scale = lax.rsqrt(jnp.mean(mixed * mixed, axis=1, keepdims=True) + 1e-05)
        gate = gate_ref[:, at]
        out_ref[:, at] = (mixed * scale * gain_ref[0:1, :] * (gate * jax.nn.sigmoid(gate))).astype(BF)


def gate_back_kernel(hp, dv, d_ref, mixed_ref, gate_ref, gain_ref, dm_ref, dgate_ref, dgain_ref):
    @pl.when(pl.program_id(0) == 0)
    def _():
        dgain_ref[...] = jnp.zeros_like(dgain_ref)

    gain = gain_ref[0:1, :]
    for h in range(hp):
        at = slice(h * dv, (h + 1) * dv)
        mixed = mixed_ref[:, at]
        scale = lax.rsqrt(jnp.mean(mixed * mixed, axis=1, keepdims=True) + 1e-05)
        m = mixed * scale
        gate = gate_ref[:, at]
        sig = jax.nn.sigmoid(gate)
        through = d_ref[:, at] * (gate * sig)
        dgain_ref[0:1, :] += jnp.sum(through * m, axis=0, keepdims=True)
        em = through * gain
        dm_ref[:, at] = scale * (em - m * jnp.mean(em * m, axis=1, keepdims=True))
        slope = sig * (1.0 + gate * (1.0 - sig))
        dgate_ref[:, at] = (d_ref[:, at] * m * gain * slope).astype(BF)


VMEM_LIMIT = 60 * 2**20


def shape_of(*dims, dtype=F32):
    return jax.ShapeDtypeStruct(dims, dtype)


def delta_forward(pre, small, rider, taps, const, hp, dk, dv):
    total, wide = pre.shape
    jobs = total // CHUNK * hp
    return pl.pallas_call(
        functools.partial(fwd_kernel, hp, dk, dv),
        out_shape=(
            shape_of(total, hp * dv),
            shape_of(jobs, dk, dv),
            shape_of(total, hp * dv),
            shape_of(jobs, CHUNK, CHUNK),
            shape_of(total, hp * dk),
        ),
        scratch_shapes=[
            pltpu.VMEM((total, wide), F32),
            pltpu.VMEM((total, LANES), F32),
            pltpu.VMEM((jobs, CHUNK, CHUNK), F32),
            pltpu.VMEM((hp, dk, dv), F32),
        ],
        compiler_params=pltpu.CompilerParams(vmem_limit_bytes=VMEM_LIMIT),
        cost_estimate=pl.CostEstimate(
            flops=total * hp * 21_000_000,
            transcendentals=total * hp * CHUNK,
            bytes_accessed=total * wide * 16,
        ),
        name="delta_forward",
    )(pre, small, rider, taps, const)


def delta_backward(pre, small, rider, taps, const, saved, d_mixed, hp, dk, dv):
    total, wide = pre.shape
    jobs = total // CHUNK * hp
    return pl.pallas_call(
        functools.partial(bwd_kernel, hp, dk, dv),
        out_shape=(
            shape_of(total, wide + LANES, dtype=BF),
            shape_of(8, wide),
            shape_of(8, LANES),
        ),
        scratch_shapes=[
            pltpu.VMEM((total, wide), F32),
            pltpu.VMEM((total + 8, LANES), F32),
            pltpu.VMEM((total, wide), F32),
            pltpu.VMEM((total + 8, wide), F32),
            pltpu.VMEM((total, LANES), F32),
            pltpu.VMEM((total, hp * dv), F32),
            pltpu.VMEM((jobs, dk, dv), F32),
            pltpu.VMEM((hp, dk, dv), F32),
        ],
        compiler_params=pltpu.CompilerParams(vmem_limit_bytes=VMEM_LIMIT),
        cost_estimate=pl.CostEstimate(
            flops=total * hp * 34_000_000,
            transcendentals=total * hp * CHUNK,
            bytes_accessed=total * wide * 20,
        ),
        name="delta_backward",
    )(pre, small, rider, taps, const, *saved, d_mixed)


GATE_ROWS = 256


def gate_forward(mixed, gate, gain, hp, dv):
    total, wide = mixed.shape
    rows = min(GATE_ROWS, total)
    block = pl.BlockSpec((rows, wide), lambda i: (i, 0))
    return pl.pallas_call(
        functools.partial(gate_kernel, hp, dv),
        grid=(total // rows,),
        in_specs=[block, block, pl.BlockSpec((1, dv), lambda i: (0, 0))],
        out_specs=block,
        out_shape=shape_of(total, wide, dtype=BF),
        name="gate_forward",
    )(mixed, gate, gain)


def gate_backward(d_gated, mixed, gate, gain, hp, dv):
    total, wide = mixed.shape
    rows = min(GATE_ROWS, total)
    block = pl.BlockSpec((rows, wide), lambda i: (i, 0))
    return pl.pallas_call(
        functools.partial(gate_back_kernel, hp, dv),
        grid=(total // rows,),
        in_specs=[block, block, block, pl.BlockSpec((1, dv), lambda i: (0, 0))],
        out_specs=(block, block, pl.BlockSpec((8, dv), lambda i: (0, 0))),
        out_shape=(
            shape_of(total, wide),
            shape_of(total, wide, dtype=BF),
            shape_of(8, dv),
        ),
        name="gate_backward",
    )(d_gated, mixed, gate, gain)


def local(
    tokens,
    attn_gain,
    w_query,
    w_key,
    w_value,
    w_decay,
    w_beta,
    w_gate,
    w_out,
    conv_query,
    conv_key,
    conv_value,
    decay_log,
    decay_bias,
    out_gain,
    mlp_gain,
    w_hidden,
    w_up,
    w_down,
    offsets,
    cotangent,
):
    ranks = lax.axis_size("seq")
    rank = lax.axis_index("seq")
    heads = decay_log.shape[0]
    width = tokens.shape[-1]
    tok = tokens.shape[1]
    length = tok * ranks
    plan = Plan(ranks, heads, w_query.shape[1] // heads, out_gain.shape[0], w_hidden.shape[1])
    hp, vs, dk, dv, ff = plan.hp, plan.vs, plan.key_dim, plan.dv, plan.ff
    rows = w_query.shape[0]

    own_tokens = to_ring(tokens[0])
    own_cot = to_ring(cotangent[0])
    rider = jnp.concatenate(
        [
            (offsets[0] // 64).astype(BF)[:, None],
            (offsets[0] % 64).astype(BF)[:, None],
            jnp.zeros((tok, LANES - 2), BF),
        ],
        axis=1,
    )
    small = jnp.concatenate(
        [
            plan.split_keys(w_decay),
            plan.split_keys(w_beta),
            jnp.broadcast_to(attn_gain[:, None, None], (rows, ranks, 1)),
            jnp.broadcast_to(mlp_gain[:, None, None], (rows, ranks, 1)),
            jnp.zeros((rows, ranks, LANES - 2 - 2 * hp), BF),
        ],
        axis=2,
    )
    mix_own = exchange(
        jnp.concatenate(
            [
                plan.split_keys(w_query),
                plan.split_keys(w_key),
                plan.split_even(w_value),
                small,
            ],
            axis=2,
        )
    )
    gathered = lax.all_gather(
        after(jnp.concatenate([own_tokens, rider], axis=1), mix_own), "seq", axis=0, tiled=True
    )
    w_mix = gather_end(mix_own, gather_start(mix_own))
    side_own = exchange(
        after(
            jnp.concatenate([plan.split_even(w_gate), plan.split_even(w_out)], axis=2), mix_own
        )
    )
    side_own = after(side_own, w_mix)
    w_side = gather_end(side_own, gather_start(side_own))
    mlp_own_cols = exchange(
        after(
            jnp.concatenate(
                [plan.split_even(w_hidden), plan.split_even(w_up), plan.split_even(w_down)],
                axis=2,
            ),
            side_own,
            gathered,
        )
    )
    mlp_near = gather_start(after(mlp_own_cols, w_side))

    at_k = hp * dk
    at_v = 2 * hp * dk
    at_s = at_v + hp * dv
    attn_gain_full = w_mix[:, at_s + 2 * hp].astype(F32)
    mlp_gain_full = w_mix[:, at_s + 2 * hp + 1].astype(F32)
    gate_cols = w_side[:, : hp * dv]
    out_cols = w_side[:, hp * dv :]

    tokens_all = gathered[:, :width].astype(F32)
    normed_all = tokens_all * rms_scale(tokens_all)
    attn = (normed_all * attn_gain_full).astype(BF)
    pre = nn(attn, w_mix[:, :at_s]).astype(BF)
    pre_small = nn(attn, w_mix[:, at_s:])
    cot_all = lax.all_gather(after(own_cot, pre), "seq", axis=0, tiled=True)
    pre_gate = nn(attn, gate_cols)

    group = rank // vs
    taps_query = lax.dynamic_slice_in_dim(conv_query, group * hp * dk, hp * dk, 1)
    taps_key = lax.dynamic_slice_in_dim(conv_key, group * hp * dk, hp * dk, 1)
    taps_value = lax.dynamic_slice_in_dim(conv_value, rank * hp * dv, hp * dv, 1)
    own_log = lax.dynamic_slice_in_dim(decay_log, group * hp, hp, 0)
    own_bias = lax.dynamic_slice_in_dim(decay_bias, group * hp, hp, 0)
    own_gain = lax.dynamic_slice_in_dim(out_gain, (rank % vs) * dv, dv, 0)

    taps = jnp.concatenate([taps_query, taps_key, taps_value], axis=1)
    const = jnp.pad(jnp.stack([-jnp.exp(own_log), own_bias]), ((0, 0), (0, LANES - hp)))
    pre, pre_small = lax.optimization_barrier((pre, pre_small, side_own))[:2]
    rider_all = gathered[:, width:]
    mixed, *saved = delta_forward(pre, pre_small, rider_all, taps, const, hp, dk, dv)

    def by_head(array):
        return array.reshape(length, hp, -1)

    def gate_apply(mixed_in, gate_in, gain_in):
        m = by_head(mixed_in)
        square = plan.value_sum(jnp.sum(m * m, axis=-1, keepdims=True))
        scale = lax.rsqrt(square / plan.value_dim + 1e-05)
        return (m * scale * gain_in * silu(by_head(gate_in))).reshape(length, -1)

    def gate_apply_back(d_out, mixed_in, gate_in, gain_in):
        d, mixed_in, gate_in = by_head(d_out), by_head(mixed_in), by_head(gate_in)
        square = plan.value_sum(jnp.sum(mixed_in * mixed_in, axis=-1, keepdims=True))
        scale = lax.rsqrt(square / plan.value_dim + 1e-05)
        m = mixed_in * scale
        through = d * silu(gate_in)
        em = through * gain_in
        mean = plan.value_sum(jnp.sum(em * m, axis=-1, keepdims=True)) / plan.value_dim
        d_mix = scale * (em - m * mean)
        d_gt = d * m * gain_in * silu_slope(gate_in)
        return (
            d_mix.reshape(length, -1),
            d_gt.reshape(length, -1).astype(BF),
            jnp.sum(through * m, axis=(0, 1)),
        )

    if vs == 1:
        gated = gate_forward(mixed, pre_gate, own_gain[None], hp, dv)
    else:
        gated = gate_apply(mixed, pre_gate, own_gain).astype(BF)
    gated = after(gated, mlp_own_cols, cot_all)
    branch = lax.psum_scatter(
        nt(gated, out_cols).astype(BF), "seq", scatter_dimension=0, tiled=True
    )
    inputs = own_tokens.astype(F32)
    middle = inputs + branch.astype(F32)
    r2 = rms_scale(middle)
    n2 = middle * r2
    near_and_cot = lax.optimization_barrier(
        ((n2 * mlp_gain_full).astype(BF), cot_all) + tuple(mlp_near)
    )
    mlp_own, cot_all, mlp_near = near_and_cot[0], near_and_cot[1], near_and_cot[2:]
    mlp_cols = gather_end(mlp_own_cols, mlp_near)
    mlp_all = lax.all_gather(mlp_own, "seq", axis=0, tiled=True)
    both_w = mlp_cols[:, : 2 * ff]
    down_w = mlp_cols[:, 2 * ff :]
    d_product = nn(cot_all, down_w)
    both_pre = nn(mlp_all, both_w)
    hidden_pre = both_pre[:, :ff]
    up_pre = both_pre[:, ff:]
    sh = silu(hidden_pre)
    product = (sh * up_pre).astype(BF)
    d_both = jnp.concatenate(
        [
            (d_product * up_pre * silu_slope(hidden_pre)).astype(BF),
            (d_product * sh).astype(BF),
        ],
        axis=1,
    )
    d_mlp = lax.psum_scatter(
        nt(d_both, both_w).astype(BF), "seq", scatter_dimension=0, tiled=True
    ).astype(F32)
    d_output = own_cot.astype(F32)
    e2 = d_mlp * mlp_gain_full
    d_middle = d_output + r2 * (e2 - n2 * jnp.mean(e2 * n2, axis=-1, keepdims=True))
    both_sum = RingGrad(mlp_all, d_both)
    down_sum = RingGrad(cot_all, product)
    d_branch_own = after(d_middle.astype(BF), *both_sum.near, *down_sum.sent)
    both_sum.second(d_branch_own)
    d_branch_all = lax.all_gather(d_branch_own, "seq", axis=0, tiled=True)
    mlp_part = after(nt(product, down_w).astype(BF), d_branch_all)
    mlp_out = lax.psum_scatter(mlp_part, "seq", scatter_dimension=0, tiled=True)

    d_gated = nn(d_branch_all, out_cols)
    if vs == 1:
        d_mixed, d_gate, gain_part = gate_backward(
            d_gated, mixed, pre_gate, own_gain[None], hp, dv
        )
        grad_out_gain = gain_part[0]
    else:
        d_mixed, d_gate, grad_out_gain = gate_apply_back(d_gated, mixed, pre_gate, own_gain)
    gate_sum = RingGrad(attn, d_gate)
    out_sum = RingGrad(d_branch_all, gated)
    d_attn_gate = nt(d_gate, gate_cols)
    down_sum.second(d_branch_all)
    d_mixed = after(
        d_mixed,
        *both_sum.late,
        *down_sum.late,
        *gate_sum.sent,
        *out_sum.sent,
        mlp_part,
        d_attn_gate,
    )
    both_rows = to_rows(both_sum.total(d_mixed), ranks)
    down_rows = to_rows(down_sum.total(d_mixed), ranks)
    d_pre, d_taps, d_sums = delta_backward(
        pre, pre_small, rider_all, taps, const, saved, d_mixed, hp, dk, dv
    )
    d_pre, d_taps, d_sums, mlp_out, both_rows, down_rows = lax.optimization_barrier(
        (d_pre, d_taps, d_sums, mlp_out, both_rows, down_rows) + gate_sum.near + out_sum.near
    )[:6]
    mix_sum = RingGrad(attn, d_pre)
    gate_sum.second(d_pre)
    out_sum.second(d_pre)
    gate_rows = to_rows(gate_sum.total(), ranks)
    out_rows = to_rows(out_sum.total(), ranks)
    mix_sum.second()
    mix_rows = to_rows(mix_sum.total(), ranks)
    d_attn = lax.psum_scatter(
        (d_attn_gate + nt(d_pre, w_mix)).astype(BF), "seq", scatter_dimension=0, tiled=True
    ).astype(F32)

    output = from_ring((middle + mlp_out.astype(F32)).astype(BF))
    n = inputs * rms_scale(inputs)
    e = d_attn * attn_gain_full
    grad_tokens = from_ring(
        (d_middle + rms_scale(inputs) * (e - n * jnp.mean(e * n, axis=-1, keepdims=True))).astype(BF)
    )

    sums = jnp.concatenate(
        [
            d_taps[:KERNEL, :at_k].reshape(-1),
            d_taps[:KERNEL, at_k:at_v].reshape(-1),
            d_taps[:KERNEL, at_v:].reshape(-1),
            d_sums[1, :hp],
            d_sums[0, :hp],
            grad_out_gain,
        ]
    )
    every = sum_everywhere(jnp.pad(sums, (0, -sums.shape[0] % 1024)))

    def per_head(part, lead):
        part = part.reshape(ranks // vs, vs, lead, -1).sum(axis=1)
        return jnp.transpose(part, (1, 0, 2)).reshape(lead, -1)

    a0 = KERNEL * hp * dk
    a1 = 2 * a0
    a2 = a1 + KERNEL * hp * dv
    grad_conv_value = jnp.transpose(
        every[:, a1:a2].reshape(ranks, KERNEL, -1), (1, 0, 2)
    ).reshape(KERNEL, -1)
    gain_sum = every[:, a2 + 2 * hp : a2 + 2 * hp + dv].reshape(ranks // vs, vs, dv).sum(axis=0).reshape(-1)
    grad_query = plan.join_keys(mix_rows[:, :, :at_k])
    grad_key = plan.join_keys(mix_rows[:, :, at_k:at_v])
    grad_value = plan.join_even(mix_rows[:, :, at_v:at_s])
    grad_decay = plan.join_keys(mix_rows[:, :, at_s : at_s + hp])
    grad_beta = plan.join_keys(mix_rows[:, :, at_s + hp : at_s + 2 * hp])
    grad_gate = plan.join_even(gate_rows)
    grad_hidden = plan.join_even(both_rows[:, :, :ff])
    grad_up = plan.join_even(both_rows[:, :, ff:])

    def gain_grad(gain, pairs):
        total = sum(jnp.sum(w.astype(F32) * g, axis=1) for w, g in pairs)
        return total / gain.astype(F32)

    return (
        output[None],
        grad_tokens[None],
        gain_grad(
            attn_gain,
            (
                (w_query, grad_query),
                (w_key, grad_key),
                (w_value, grad_value),
                (w_decay, grad_decay),
                (w_beta, grad_beta),
                (w_gate, grad_gate),
            ),
        ),
        grad_query,
        grad_key,
        grad_value,
        grad_decay,
        grad_beta,
        grad_gate,
        plan.join_even(out_rows),
        per_head(every[:, :a0], KERNEL),
        per_head(every[:, a0:a1], KERNEL),
        grad_conv_value,
        per_head(every[:, a2 : a2 + hp], 1)[0],
        per_head(every[:, a2 + hp : a2 + 2 * hp], 1)[0],
        gain_sum,
        gain_grad(mlp_gain, ((w_hidden, grad_hidden), (w_up, grad_up))),
        grad_hidden,
        grad_up,
        plan.join_even(down_rows),
    )


def solution(mesh):
    flat = ("dp", "seq")
    tok_spec = P("dp", "seq", None)
    row_spec = P(flat, None)
    gain_spec = P(flat)
    in_specs = (
        (tok_spec, gain_spec)
        + (row_spec,) * 7
        + (P(),) * 6
        + (gain_spec,)
        + (row_spec,) * 3
        + (P("dp", "seq"), tok_spec)
    )
    out_specs = (
        (tok_spec, tok_spec, gain_spec)
        + (row_spec,) * 7
        + (P(),) * 6
        + (gain_spec,)
        + (row_spec,) * 3
    )
    return jax.shard_map(local, mesh=mesh, in_specs=in_specs, out_specs=out_specs, check_vma=False)
```

```python
import functools

import jax
import jax.numpy as jnp
from jax import lax
from jax.experimental import pallas as pl
from jax.experimental.pallas import tpu as pltpu
from jax.sharding import PartitionSpec as P

KERNEL = 4
LANES = 128
BF = jnp.bfloat16
F32 = jnp.float32
CHUNK = 128


def rms_scale(value):
    return lax.rsqrt(jnp.mean(value * value, axis=-1, keepdims=True) + 1e-05)


def dot_f32(left, right, dims):
    return lax.dot_general(left, right, (dims, ((), ())), preferred_element_type=F32)


def nn(left, right):
    return dot_f32(left, right, ((1,), (0,)))


def nt(left, right):
    return dot_f32(left, right, ((1,), (1,)))


def tn(left, right):
    return dot_f32(left, right, ((0,), (0,)))


def silu(value):
    return value * jax.nn.sigmoid(value)


def silu_slope(value):
    s = jax.nn.sigmoid(value)
    return s * (1.0 + value * (1.0 - s))


class Plan:
    def __init__(self, ranks, heads, key_dim, value_dim, hidden):
        self.ranks = ranks
        self.heads = heads
        self.key_dim = key_dim
        self.hp = max(1, heads // ranks)
        self.vs = max(1, ranks // heads)
        self.dv = value_dim // self.vs
        self.value_dim = value_dim
        self.ff = hidden // ranks

    def split_keys(self, array):
        rows = array.shape[0]
        grouped = array.reshape(rows, self.heads // self.hp, -1)
        return jnp.repeat(grouped, self.vs, axis=1) if self.vs > 1 else grouped

    def split_even(self, array):
        return array.reshape(array.shape[0], self.ranks, -1)

    def join_keys(self, array):
        ranks, rows, width = array.shape
        array = array.astype(F32)
        if self.vs > 1:
            array = array.reshape(ranks // self.vs, self.vs, rows, width).sum(axis=1)
        return jnp.transpose(array, (1, 0, 2)).reshape(rows, -1)

    def join_even(self, array):
        return jnp.transpose(array, (1, 0, 2)).reshape(array.shape[1], -1).astype(F32)

    def value_sum(self, array):
        step = 1
        while step < self.vs:
            pairs = [(i, i ^ step) for i in range(self.ranks)]
            array = array + lax.ppermute(array, "seq", pairs)
            step *= 2
        return array


def after(value, *earlier):
    return lax.optimization_barrier((value,) + earlier)[0]


def ring_order(count):
    return [0, 1, 3, 2] if count == 4 else list(range(count))


def ring_pairs(count):
    order = ring_order(count)
    right = [(order[i], order[(i + 1) % count]) for i in range(count)]
    return right, [(there, here) for here, there in right]


def ring_place():
    me = lax.axis_index("dp")
    return me ^ (me >> 1)


def swap_blocks(array):
    size = array.shape[1] // 4
    return jnp.concatenate(
        [array[:, : 2 * size], array[:, 3 * size :], array[:, 2 * size : 3 * size]], axis=1
    )


def to_ring(array):
    if lax.axis_size("dp") != 4:
        return array
    width = array.shape[1]
    turned = swap_blocks(array)
    twice = jnp.concatenate([turned, turned], axis=1)
    return lax.dynamic_slice_in_dim(twice, ring_place() * (width // 4), width, 1)


def from_ring(array):
    if lax.axis_size("dp") != 4:
        return array
    width = array.shape[1]
    twice = jnp.concatenate([array, array], axis=1)
    at = (4 - ring_place()) * (width // 4)
    return swap_blocks(lax.dynamic_slice_in_dim(twice, at, width, 1))


def gather_start(own):
    if lax.axis_size("dp") != 4:
        return ()
    right, left = ring_pairs(4)
    return lax.ppermute(own, "dp", right), lax.ppermute(own, "dp", left)


def gather_end(own, near):
    if lax.axis_size("dp") != 4:
        return lax.all_gather(own, "dp", axis=0, tiled=True)
    right, left = ring_pairs(4)
    half = own.shape[0] // 2
    from_left, from_right = near
    far_a = lax.ppermute(from_left[:half], "dp", right)
    far_b = lax.ppermute(from_right[half:], "dp", left)
    return jnp.concatenate([own, from_right, far_a, far_b, from_left])


class RingGrad:
    def __init__(self, left, right):
        self.ring = lax.axis_size("dp") == 4
        self.left, self.right = left, right
        rows = self.rows = left.shape[1] // lax.axis_size("dp")
        self.half = rows // 2
        self.sent, self.near, self.late = (), (), ()
        if self.ring:
            to_right, to_left = ring_pairs(4)
            self.sent = tuple(self.part(i).astype(BF) for i in (4, 5, 3, 6))
            self.near = (
                lax.ppermute(self.sent[0], "dp", to_right),
                lax.ppermute(self.sent[1], "dp", to_left),
                lax.ppermute(self.sent[2], "dp", to_right),
                lax.ppermute(self.sent[3], "dp", to_left),
            )

    def part(self, index):
        at = index * self.half
        return tn(self.left[:, at : at + self.half], self.right)

    def second(self, *earlier):
        if self.ring:
            to_right, to_left = ring_pairs(4)
            far_a, far_b = lax.optimization_barrier(self.near[:2] + earlier)[:2]
            self.late = (
                lax.ppermute((self.part(2) + far_a.astype(F32)).astype(BF), "dp", to_right),
                lax.ppermute((self.part(7) + far_b.astype(F32)).astype(BF), "dp", to_left),
            )

    def total(self, *earlier):
        if not self.ring:
            whole = tn(self.left, self.right).astype(BF)
            return lax.psum_scatter(whole, "dp", scatter_dimension=0, tiled=True)
        held = lax.optimization_barrier(self.near[2:] + self.late + earlier)
        right_b, left_a, right_a, left_b = held[:4]
        own = tn(self.left[:, : self.rows], self.right)
        from_left = jnp.concatenate([right_a, right_b]).astype(F32)
        from_right = jnp.concatenate([left_a, left_b]).astype(F32)
        return (own + from_left + from_right).astype(BF)


def rank_major(packed):
    return jnp.transpose(packed, (1, 0, 2)).reshape(-1, packed.shape[2])


def exchange(packed):
    return lax.all_to_all(packed, "seq", 0, 0, tiled=True)


def to_rows(mine, ranks):
    turned = lax.all_to_all(mine, "seq", 0, 0, tiled=True)
    return turned.reshape(ranks, -1, mine.shape[1])


def sum_everywhere(values):
    count = lax.axis_size("dp")
    ranks = lax.axis_size("seq")
    if count & (count - 1) or ranks & (ranks - 1):
        return lax.all_gather(lax.psum(values, "dp"), "seq", axis=0, tiled=True)
    step = 1
    while step < count:
        values = values + lax.ppermute(values, "dp", [(i, i ^ step) for i in range(count)])
        step *= 2
    rank = lax.axis_index("seq")
    held = values
    step = 1
    while step < ranks:
        other = lax.ppermute(held, "seq", [(i, i ^ step) for i in range(ranks)])
        upper = (rank & step) != 0
        held = jnp.concatenate([jnp.where(upper, other, held), jnp.where(upper, held, other)])
        step *= 2
    return held


class Pair:
    def __init__(self, value):
        self.value = value
        self.high = value.astype(BF)
        self.low = (value - self.high.astype(F32)).astype(BF)


def pair(value):
    return value if isinstance(value, Pair) else Pair(value)


NN = ((1,), (0,))
NT = ((1,), (1,))
TN = ((0,), (0,))


def dot(left, right, dims):
    a, b = pair(left), pair(right)
    return dot_f32(a.high, b.high, dims) + (
        dot_f32(a.high, b.low, dims) + dot_f32(a.low, b.high, dims)
    )


def stack(top, bottom):
    return jnp.concatenate([top, bottom], axis=0)


def grids(n):
    t = lax.broadcasted_iota(jnp.int32, (n, n), 0)
    s = lax.broadcasted_iota(jnp.int32, (n, n), 1)
    return t, s


def inverses(stricts, t, s):
    n = t.shape[0]
    eye = jnp.where(t == s, 1.0, 0.0).astype(F32)
    same = (t // 8) == (s // 8)
    small = [Pair(jnp.where(same, a, 0.0)) for a in stricts]
    square = [Pair(dot(a, a, NN)) for a in small]
    fourth = [dot(a, a, NN) for a in square]
    first = [eye - a.value for a in small]
    inv = [f + dot(f, a, NN) for f, a in zip(first, square)]
    inv = [f + dot(f, a, NN) for f, a in zip(inv, fourth)]
    size = 8
    while size < n:
        take = ((t // (2 * size)) == (s // (2 * size))) & ((t // size) != (s // size))
        held = [Pair(f) for f in inv]
        part = [dot(f, jnp.where(take, a, 0.0), NN) for f, a in zip(held, stricts)]
        inv = [f.value - dot(p, f, NN) for f, p in zip(held, part)]
        size *= 2
    return inv


def decays(cols, hp, t, s):
    n = t.shape[0]
    tri = jnp.where(t >= s, 1.0, 0.0).astype(F32)
    run = dot(tri, cols, NN)
    turned = jnp.transpose(run)
    offs = cols[:, 2 * hp : 2 * hp + 1]
    row = t[:, :1].astype(F32)
    gap = (t - s).astype(F32)
    same = (gap >= 0.0) & (offs >= gap)
    keep = offs[n - 1 : n, :] >= (n - 1.0) - row
    out = []
    for h in range(hp):
        g = run[:, h : h + 1]
        g_row = turned[h : h + 1, :]
        pairwise = jnp.where(same, jnp.exp(jnp.where(same, g - g_row, 0.0)), 0.0)
        start = jnp.where(offs > row, jnp.exp(g), 0.0)
        end = jnp.where(keep, jnp.exp(jnp.where(keep, g[n - 1 : n, :] - g, 0.0)), 0.0)
        out.append((pairwise, start, end, start[n - 1 : n, :], cols[:, hp + h : hp + h + 1]))
    return out


def lanes_of(hp, dk, dv):
    q = [slice(h * dk, (h + 1) * dk) for h in range(hp)]
    k = [slice((hp + h) * dk, (hp + h + 1) * dk) for h in range(hp)]
    v = [slice(2 * hp * dk + h * dv, 2 * hp * dk + (h + 1) * dv) for h in range(hp)]
    return q, k, v


def chunk_rows(c):
    return pl.ds(pl.multiple_of(c * CHUNK, CHUNK), CHUNK)


def chunk_cols(hp, rows, small_ref, rider_ref, const_ref):
    lane = lax.broadcasted_iota(jnp.int32, (CHUNK, LANES), 1)
    x = small_ref[rows, :]
    y = x + const_ref[1:2, :]
    logs = const_ref[0:1, :] * (jnp.maximum(y, 0.0) + jnp.log1p(jnp.exp(-jnp.abs(y))))
    beta = jax.nn.sigmoid(x)
    rider = rider_ref[rows, :].astype(F32)
    offs = rider[:, 0:1] * 64.0 + rider[:, 1:2]
    cols = jnp.where(lane < hp, logs, jnp.where(lane < 2 * hp, beta, 0.0))
    return jnp.where(lane == 2 * hp, offs, cols), offs


def conved_lanes(c, lanes, offs, pre_ref, taps_ref):
    rows = chunk_rows(c)
    above = pl.ds(pl.multiple_of(jnp.maximum(c * CHUNK - 16, 0), 16), 16)
    block = pre_ref[rows, lanes].astype(F32)
    ext = stack(pre_ref[above, lanes].astype(F32), block)
    total = taps_ref[0:1, lanes] * block
    for by in range(1, KERNEL):
        moved = pltpu.roll(ext, by, 0)[16:]
        total = total + taps_ref[by : by + 1, lanes] * jnp.where(offs >= by, moved, 0.0)
    return total


def unit_scale(u):
    return lax.rsqrt(jnp.sum(u * u, axis=1, keepdims=True) + 1e-06)


def fill_front(hp, dk, dv, c, pre_ref, small_ref, rider_ref, taps_ref, const_ref, qkv_ref, cols_ref, conv_ref):
    rows = chunk_rows(c)
    cols, offs = chunk_cols(hp, rows, small_ref, rider_ref, const_ref)
    cols_ref[rows, :] = cols
    for kind, slices in enumerate(lanes_of(hp, dk, dv)):
        for lanes in slices:
            conved = conved_lanes(c, lanes, offs, pre_ref, taps_ref)
            if conv_ref is not None:
                conv_ref[rows, lanes] = conved
            u = conved * jax.nn.sigmoid(conved)
            if kind == 0:
                u = u * (unit_scale(u) * dk ** (-0.5))
            elif kind == 1:
                u = u * unit_scale(u)
            qkv_ref[rows, lanes] = u


def fwd_kernel(
    hp, dk, dv, pre_ref, small_ref, rider_ref, taps_ref, const_ref,
    mixed_ref, state_ref, upd_ref, inv_ref, seen_ref,
    qkv_ref, cols_ref, p_ref, cur_ref,
):
    n = CHUNK
    chunks = pre_ref.shape[0] // n
    group = 2 if chunks % 2 == 0 else 1
    t, s = grids(n)
    q_at, k_at, v_at = lanes_of(hp, dk, dv)

    def prepare(step, carry):
        jobs = []
        for j in range(group):
            c = step * group + j
            fill_front(
                hp, dk, dv, c, pre_ref, small_ref, rider_ref, taps_ref, const_ref, qkv_ref, cols_ref, None
            )
            rows = chunk_rows(c)
            for h, d in enumerate(decays(cols_ref[rows, :], hp, t, s)):
                jobs.append((c, rows, h) + d)
        keys = [qkv_ref[r, k_at[h]] for _, r, h, *_ in jobs]
        both = [dot(stack(k, qkv_ref[job[1], q_at[job[2]]]), k, NT) for k, job in zip(keys, jobs)]
        strict = [jnp.where(t > s, job[3] * b[:n], 0.0) * job[7] for job, b in zip(jobs, both)]
        inv = [Pair(i) for i in inverses(strict, t, s)]
        for job, b, i, k in zip(jobs, both, inv, keys):
            c, r, h, pairwise, start, end, last, beta = job
            p_ref[c * hp + h] = pairwise * b[n:]
            inv_ref[c * hp + h] = i.value
            upd_ref[r, h * dv : (h + 1) * dv] = dot(i, beta * qkv_ref[r, v_at[h]], NN)
            seen_ref[r, h * dk : (h + 1) * dk] = dot(i, (beta * start) * k, NN)
        return carry

    lax.fori_loop(0, chunks // group, prepare, 0)
    cur_ref[...] = jnp.zeros_like(cur_ref)

    def advance(c, carry):
        rows = chunk_rows(c)
        for h, (pairwise, start, end, last, beta) in enumerate(decays(cols_ref[rows, :], hp, t, s)):
            vv = slice(h * dv, (h + 1) * dv)
            state = cur_ref[h]
            state_ref[c * hp + h] = state
            seen = seen_ref[rows, h * dk : (h + 1) * dk]
            both = dot(stack(seen, qkv_ref[rows, q_at[h]] * start), state, NN)
            update = Pair(upd_ref[rows, vv] - both[:n])
            upd_ref[rows, vv] = update.value
            mixed_ref[rows, vv] = both[n:] + dot(p_ref[c * hp + h], update, NN)
            cur_ref[h] = last * state + dot(qkv_ref[rows, k_at[h]] * end, update, TN)
        return carry

    lax.fori_loop(0, chunks, advance, 0)


def bwd_kernel(
    hp, dk, dv, pre_ref, small_ref, rider_ref, taps_ref, const_ref,
    state_ref, upd_ref, inv_ref, seen_ref, dm_ref, gain_ref,
    dpre_ref, dtaps_ref,
    qkv_ref, cols_ref, conv_ref, dcon_ref, dcols_ref, du_ref, ds_ref, cur_ref,
):
    n = CHUNK
    total = pre_ref.shape[0]
    chunks = total // n
    t, s = grids(n)
    q_at, k_at, v_at = lanes_of(hp, dk, dv)
    wide = 2 * hp * dk + hp * dv
    cur_ref[...] = jnp.zeros_like(cur_ref)
    dtaps_ref[...] = jnp.zeros_like(dtaps_ref)
    dtaps_ref[6:7, : gain_ref.shape[1]] = gain_ref[0:1, :]
    dcon_ref[total:, :] = jnp.zeros((dcon_ref.shape[0] - total, wide), F32)
    cols_ref[total:, :] = jnp.zeros((cols_ref.shape[0] - total, LANES), F32)

    def retreat(step, carry):
        c = chunks - 1 - step
        rows = chunk_rows(c)
        fill_front(
            hp, dk, dv, c, pre_ref, small_ref, rider_ref, taps_ref, const_ref, qkv_ref, cols_ref, conv_ref
        )
        for h, (pairwise, start, end, last, beta) in enumerate(decays(cols_ref[rows, :], hp, t, s)):
            vv = slice(h * dv, (h + 1) * dv)
            d_state = cur_ref[h]
            ds_ref[c * hp + h] = d_state
            dm = Pair(dm_ref[rows, vv])
            q, k = qkv_ref[rows, q_at[h]], qkv_ref[rows, k_at[h]]
            p = pairwise * dot(q, k, NT)
            du = dot(p, dm, TN) + dot(k * end, d_state, NN)
            du_ref[rows, vv] = du
            seen = seen_ref[rows, h * dk : (h + 1) * dk]
            cur_ref[h] = last * d_state + dot(q * start, dm, TN) - dot(seen, du, TN)
        return carry

    lax.fori_loop(0, chunks, retreat, 0)
    lane = lax.broadcasted_iota(jnp.int32, (n, LANES), 1)

    def through_silu(rows, lanes, dy, unit):
        conved = conv_ref[rows, lanes]
        sig = jax.nn.sigmoid(conved)
        if unit:
            u = conved * sig
            scale = unit_scale(u)
            dy = scale * dy - (scale * scale * scale) * u * jnp.sum(u * dy, axis=1, keepdims=True)
        dcon_ref[rows, lanes] = dy * (sig * (1.0 + conved * (1.0 - sig)))

    def finish(c, carry):
        rows = chunk_rows(c)
        d_cols = jnp.zeros((n, LANES), F32)
        for h, (pairwise, start, end, last, beta) in enumerate(decays(cols_ref[rows, :], hp, t, s)):
            vv = slice(h * dv, (h + 1) * dv)
            q, k, v = qkv_ref[rows, q_at[h]], qkv_ref[rows, k_at[h]], qkv_ref[rows, v_at[h]]
            dm = dm_ref[rows, vv]
            q_p, k_p, u_p = Pair(q), Pair(k), Pair(upd_ref[rows, vv])
            state = Pair(state_ref[c * hp + h])
            d_state = Pair(ds_ref[c * hp + h])
            w = dot(inv_ref[c * hp + h], du_ref[rows, vv], TN)
            scores = dot(stack(w, dm), u_p, NT)
            d_a = jnp.where(t > s, -scores[:n], 0.0)
            d_p = scores[n:]
            keys = dot(stack(k, q), k_p, NT)
            met = dot(stack(k, q), state, NN)
            r, qs = met[:n], met[n:]
            back = dot(stack(start * dm, -(beta * start) * w), state, NT)
            x = dot(u_p, d_state, NT)
            d_qk = pairwise * d_p
            d_kk = beta * (pairwise * d_a)
            d_query = back[:n] + dot(d_qk, k_p, NN)
            d_key = (
                back[n:]
                + dot(d_qk, q_p, TN)
                + dot(d_kk + jnp.transpose(d_kk), k_p, NN)
                + end * x
            )
            through_silu(rows, q_at[h], d_query * dk ** (-0.5), True)
            through_silu(rows, k_at[h], d_key, True)
            through_silu(rows, v_at[h], beta * w, False)
            inner = pairwise * d_a * keys[:n]
            d_beta = jnp.sum(w * (v - start * r), axis=1, keepdims=True) + jnp.sum(
                inner, axis=1, keepdims=True
            )
            d_start = jnp.sum(dm * qs, axis=1, keepdims=True) - beta * jnp.sum(
                w * r, axis=1, keepdims=True
            )
            e = pairwise * d_p * keys[n:] + beta * inner
            d_end = end * jnp.sum(k * x, axis=1, keepdims=True)
            d_g = (
                jnp.sum(e, axis=1, keepdims=True)
                - jnp.sum(jnp.transpose(e), axis=1, keepdims=True)
                + d_start * start
                - d_end
            )
            held = jnp.sum(
                jnp.sum(state.value * d_state.value, axis=1, keepdims=True), axis=0, keepdims=True
            )
            tail = jnp.sum(d_end, axis=0, keepdims=True) + last * held
            d_g = d_g + jnp.where(t[:, :1] == n - 1, tail, 0.0)
            d_cols = jnp.where(lane == h, d_g, d_cols)
            d_cols = jnp.where(lane == hp + h, d_beta, d_cols)
        tri = jnp.where(t >= s, 1.0, 0.0).astype(F32)
        dcols_ref[rows, :] = jnp.where(lane < hp, dot(tri, d_cols, TN), d_cols)
        return carry

    lax.fori_loop(0, chunks, finish, 0)

    def spread(c, carry):
        rows = chunk_rows(c)
        below = pl.ds(pl.multiple_of((c + 1) * n, n), 8)
        cols = cols_ref[rows, :]
        offs = cols[:, 2 * hp : 2 * hp + 1]
        offs_below = cols_ref[below, 2 * hp : 2 * hp + 1]
        for slices in (q_at, k_at, v_at):
            for lanes in slices:
                pre = pre_ref[rows, lanes].astype(F32)
                d_con = dcon_ref[rows, lanes]
                d_below = dcon_ref[below, lanes]
                out = taps_ref[0:1, lanes] * d_con
                dtaps_ref[0:1, lanes] += jnp.sum(pre * d_con, axis=0, keepdims=True)
                for by in range(1, KERNEL):
                    ext = stack(
                        jnp.where(offs >= by, d_con, 0.0), jnp.where(offs_below >= by, d_below, 0.0)
                    )
                    moved = pltpu.roll(ext, n + 8 - by, 0)[:n]
                    out = out + taps_ref[by : by + 1, lanes] * moved
                    dtaps_ref[by : by + 1, lanes] += jnp.sum(pre * moved, axis=0, keepdims=True)
                dpre_ref[rows, lanes] = out.astype(BF)
        d_cols = dcols_ref[rows, :]
        slope = const_ref[0:1, :] * jax.nn.sigmoid(small_ref[rows, :] + const_ref[1:2, :])
        d_small = jnp.where(lane < hp, d_cols * slope, d_cols * cols * (1.0 - cols))
        d_small = jnp.where(lane < 2 * hp, d_small, 0.0)
        dpre_ref[rows, wide:] = d_small.astype(BF)
        dtaps_ref[4:5, :LANES] += jnp.sum(d_small, axis=0, keepdims=True)
        dtaps_ref[5:6, :LANES] += jnp.sum(d_cols * cols, axis=0, keepdims=True)
        return carry

    lax.fori_loop(0, chunks, spread, 0)


def gate_kernel(hp, dv, mixed_ref, gate_ref, gain_ref, out_ref):
    for h in range(hp):
        at = slice(h * dv, (h + 1) * dv)
        mixed = mixed_ref[:, at]
        scale = lax.rsqrt(jnp.mean(mixed * mixed, axis=1, keepdims=True) + 1e-05)
        gate = gate_ref[:, at]
        out_ref[:, at] = (mixed * scale * gain_ref[0:1, :] * (gate * jax.nn.sigmoid(gate))).astype(BF)


def gate_back_kernel(hp, dv, d_ref, mixed_ref, gate_ref, gain_ref, dm_ref, dgate_ref, dgain_ref):
    @pl.when(pl.program_id(0) == 0)
    def _():
        dgain_ref[...] = jnp.zeros_like(dgain_ref)

    gain = gain_ref[0:1, :]
    for h in range(hp):
        at = slice(h * dv, (h + 1) * dv)
        mixed = mixed_ref[:, at]
        scale = lax.rsqrt(jnp.mean(mixed * mixed, axis=1, keepdims=True) + 1e-05)
        m = mixed * scale
        gate = gate_ref[:, at]
        sig = jax.nn.sigmoid(gate)
        through = d_ref[:, at] * (gate * sig)
        dgain_ref[0:1, :] += jnp.sum(through * m, axis=0, keepdims=True)
        em = through * gain
        dm_ref[:, at] = scale * (em - m * jnp.mean(em * m, axis=1, keepdims=True))
        slope = sig * (1.0 + gate * (1.0 - sig))
        dgate_ref[:, at] = (d_ref[:, at] * m * gain * slope).astype(BF)


def pack_kernel(ranks, *refs):
    *ins, out_ref = refs
    rows = ins[0].shape[0]
    parts = [ref[...].astype(F32) for ref in ins]
    for r in range(ranks):
        pieces = [p[:, r * (p.shape[1] // ranks) : (r + 1) * (p.shape[1] // ranks)] for p in parts]
        out_ref[r * rows : (r + 1) * rows, :] = jnp.concatenate(pieces, axis=1).astype(BF)


def unpack_kernel(ranks, in_ref, *outs):
    rows = outs[0].shape[0]
    for i, out_ref in enumerate(outs):
        size = out_ref.shape[1] // ranks
        pieces = [
            in_ref[r * rows : (r + 1) * rows, :].astype(F32)[:, i * size : (i + 1) * size]
            for r in range(ranks)
        ]
        out_ref[...] = jnp.concatenate(pieces, axis=1)


VMEM_LIMIT = 60 * 2**20


def shape_of(*dims, dtype=F32):
    return jax.ShapeDtypeStruct(dims, dtype)


def pack_even(ranks, *arrays):
    rows = arrays[0].shape[0]
    wide = sum(a.shape[1] for a in arrays) // ranks
    return pl.pallas_call(
        functools.partial(pack_kernel, ranks),
        out_shape=shape_of(ranks * rows, wide, dtype=BF),
        compiler_params=pltpu.CompilerParams(vmem_limit_bytes=VMEM_LIMIT),
        name="pack_even",
    )(*arrays)


def unpack_even(ranks, packed, count):
    rows = packed.shape[0] // ranks
    size = packed.shape[1] // count
    return pl.pallas_call(
        functools.partial(unpack_kernel, ranks),
        out_shape=(shape_of(rows, ranks * size),) * count,
        compiler_params=pltpu.CompilerParams(vmem_limit_bytes=VMEM_LIMIT),
        name="unpack_even",
    )(packed)


def delta_forward(pre, small, rider, taps, const, hp, dk, dv):
    total, wide = pre.shape
    jobs = total // CHUNK * hp
    return pl.pallas_call(
        functools.partial(fwd_kernel, hp, dk, dv),
        out_shape=(
            shape_of(total, hp * dv),
            shape_of(jobs, dk, dv),
            shape_of(total, hp * dv),
            shape_of(jobs, CHUNK, CHUNK),
            shape_of(total, hp * dk),
        ),
        scratch_shapes=[
            pltpu.VMEM((total, wide), F32),
            pltpu.VMEM((total, LANES), F32),
            pltpu.VMEM((jobs, CHUNK, CHUNK), F32),
            pltpu.VMEM((hp, dk, dv), F32),
        ],
        compiler_params=pltpu.CompilerParams(vmem_limit_bytes=VMEM_LIMIT),
        cost_estimate=pl.CostEstimate(
            flops=total * hp * 21_000_000,
            transcendentals=total * hp * CHUNK,
            bytes_accessed=total * wide * 16,
        ),
        name="delta_forward",
    )(pre, small, rider, taps, const)


def delta_backward(pre, small, rider, taps, const, saved, d_mixed, gain, hp, dk, dv):
    total, wide = pre.shape
    jobs = total // CHUNK * hp
    return pl.pallas_call(
        functools.partial(bwd_kernel, hp, dk, dv),
        out_shape=(
            shape_of(total, wide + LANES, dtype=BF),
            shape_of(8, wide),
        ),
        scratch_shapes=[
            pltpu.VMEM((total, wide), F32),
            pltpu.VMEM((total + 8, LANES), F32),
            pltpu.VMEM((total, wide), F32),
            pltpu.VMEM((total + 8, wide), F32),
            pltpu.VMEM((total, LANES), F32),
            pltpu.VMEM((total, hp * dv), F32),
            pltpu.VMEM((jobs, dk, dv), F32),
            pltpu.VMEM((hp, dk, dv), F32),
        ],
        compiler_params=pltpu.CompilerParams(vmem_limit_bytes=VMEM_LIMIT),
        cost_estimate=pl.CostEstimate(
            flops=total * hp * 34_000_000,
            transcendentals=total * hp * CHUNK,
            bytes_accessed=total * wide * 20,
        ),
        name="delta_backward",
    )(pre, small, rider, taps, const, *saved, d_mixed, gain)


GATE_ROWS = 256


def gate_forward(mixed, gate, gain, hp, dv):
    total, wide = mixed.shape
    rows = min(GATE_ROWS, total)
    block = pl.BlockSpec((rows, wide), lambda i: (i, 0))
    return pl.pallas_call(
        functools.partial(gate_kernel, hp, dv),
        grid=(total // rows,),
        in_specs=[block, block, pl.BlockSpec((1, dv), lambda i: (0, 0))],
        out_specs=block,
        out_shape=shape_of(total, wide, dtype=BF),
        name="gate_forward",
    )(mixed, gate, gain)


def gate_backward(d_gated, mixed, gate, gain, hp, dv):
    total, wide = mixed.shape
    rows = min(GATE_ROWS, total)
    block = pl.BlockSpec((rows, wide), lambda i: (i, 0))
    return pl.pallas_call(
        functools.partial(gate_back_kernel, hp, dv),
        grid=(total // rows,),
        in_specs=[block, block, block, pl.BlockSpec((1, dv), lambda i: (0, 0))],
        out_specs=(block, block, pl.BlockSpec((8, dv), lambda i: (0, 0))),
        out_shape=(
            shape_of(total, wide),
            shape_of(total, wide, dtype=BF),
            shape_of(8, dv),
        ),
        name="gate_backward",
    )(d_gated, mixed, gate, gain)


def local(
    tokens,
    attn_gain,
    w_query,
    w_key,
    w_value,
    w_decay,
    w_beta,
    w_gate,
    w_out,
    conv_query,
    conv_key,
    conv_value,
    decay_log,
    decay_bias,
    out_gain,
    mlp_gain,
    w_hidden,
    w_up,
    w_down,
    offsets,
    cotangent,
):
    ranks = lax.axis_size("seq")
    rank = lax.axis_index("seq")
    heads = decay_log.shape[0]
    width = tokens.shape[-1]
    tok = tokens.shape[1]
    length = tok * ranks
    plan = Plan(ranks, heads, w_query.shape[1] // heads, out_gain.shape[0], w_hidden.shape[1])
    hp, vs, dk, dv, ff = plan.hp, plan.vs, plan.key_dim, plan.dv, plan.ff
    rows = w_query.shape[0]

    own_tokens = to_ring(tokens[0])
    own_cot = to_ring(cotangent[0])
    rider = jnp.concatenate(
        [
            (offsets[0] // 64).astype(BF)[:, None],
            (offsets[0] % 64).astype(BF)[:, None],
            jnp.zeros((tok, LANES - 2), BF),
        ],
        axis=1,
    )
    small = jnp.concatenate(
        [
            plan.split_keys(w_decay),
            plan.split_keys(w_beta),
            jnp.broadcast_to(attn_gain[:, None, None], (rows, ranks, 1)),
            jnp.broadcast_to(mlp_gain[:, None, None], (rows, ranks, 1)),
            jnp.zeros((rows, ranks, LANES - 2 - 2 * hp), BF),
        ],
        axis=2,
    )
    mix_pack = rank_major(
        jnp.concatenate(
            [
                plan.split_keys(w_query),
                plan.split_keys(w_key),
                plan.split_even(w_value),
                small,
            ],
            axis=2,
        )
    )
    side_pack = rank_major(
        jnp.concatenate([plan.split_even(w_gate), plan.split_even(w_out)], axis=2)
    )
    mlp_pack = pack_even(ranks, w_hidden, w_up, w_down)
    mix_own = exchange(mix_pack)
    held = lax.optimization_barrier(
        (jnp.concatenate([own_tokens, rider], axis=1), side_pack, mlp_pack, mix_own)
    )
    gathered = lax.all_gather(held[0], "seq", axis=0, tiled=True)
    side_own = exchange(held[1])
    mix_own = held[3]
    w_mix = gather_end(mix_own, gather_start(mix_own))
    mlp_own_cols = exchange(after(held[2], side_own, gathered))
    side_own = after(side_own, w_mix)
    side_near = gather_start(side_own)

    at_k = hp * dk
    at_v = 2 * hp * dk
    at_s = at_v + hp * dv
    attn_gain_full = w_mix[:, at_s + 2 * hp].astype(F32)
    mlp_gain_full = w_mix[:, at_s + 2 * hp + 1].astype(F32)

    tokens_all = gathered[:, :width].astype(F32)
    normed_all = tokens_all * rms_scale(tokens_all)
    attn = (normed_all * attn_gain_full).astype(BF)
    pre = nn(attn, w_mix[:, :at_s]).astype(BF)
    pre_small = nn(attn, w_mix[:, at_s:])
    cot_all = lax.all_gather(after(own_cot, pre), "seq", axis=0, tiled=True)
    group = rank // vs
    taps_query = lax.dynamic_slice_in_dim(conv_query, group * hp * dk, hp * dk, 1)
    taps_key = lax.dynamic_slice_in_dim(conv_key, group * hp * dk, hp * dk, 1)
    taps_value = lax.dynamic_slice_in_dim(conv_value, rank * hp * dv, hp * dv, 1)
    own_log = lax.dynamic_slice_in_dim(decay_log, group * hp, hp, 0)
    own_bias = lax.dynamic_slice_in_dim(decay_bias, group * hp, hp, 0)
    own_gain = lax.dynamic_slice_in_dim(out_gain, (rank % vs) * dv, dv, 0)

    taps = jnp.concatenate([taps_query, taps_key, taps_value], axis=1)
    const = jnp.pad(jnp.stack([-jnp.exp(own_log), own_bias]), ((0, 0), (0, LANES - hp)))
    pre, pre_small = lax.optimization_barrier((pre, pre_small, side_own))[:2]
    rider_all = gathered[:, width:]
    mixed, *saved = delta_forward(pre, pre_small, rider_all, taps, const, hp, dk, dv)
    mixed, *side_near = lax.optimization_barrier((mixed,) + tuple(side_near))
    w_side = gather_end(side_own, side_near)
    gate_cols = w_side[:, : hp * dv]
    out_cols = w_side[:, hp * dv :]
    mlp_near = gather_start(after(mlp_own_cols, w_side))
    pre_gate = nn(attn, gate_cols)

    def by_head(array):
        return array.reshape(length, hp, -1)

    def gate_apply(mixed_in, gate_in, gain_in):
        m = by_head(mixed_in)
        square = plan.value_sum(jnp.sum(m * m, axis=-1, keepdims=True))
        scale = lax.rsqrt(square / plan.value_dim + 1e-05)
        return (m * scale * gain_in * silu(by_head(gate_in))).reshape(length, -1)

    def gate_apply_back(d_out, mixed_in, gate_in, gain_in):
        d, mixed_in, gate_in = by_head(d_out), by_head(mixed_in), by_head(gate_in)
        square = plan.value_sum(jnp.sum(mixed_in * mixed_in, axis=-1, keepdims=True))
        scale = lax.rsqrt(square / plan.value_dim + 1e-05)
        m = mixed_in * scale
        through = d * silu(gate_in)
        em = through * gain_in
        mean = plan.value_sum(jnp.sum(em * m, axis=-1, keepdims=True)) / plan.value_dim
        d_mix = scale * (em - m * mean)
        d_gt = d * m * gain_in * silu_slope(gate_in)
        return (
            d_mix.reshape(length, -1),
            d_gt.reshape(length, -1).astype(BF),
            jnp.sum(through * m, axis=(0, 1)),
        )

    if vs == 1:
        gated = gate_forward(mixed, pre_gate, own_gain[None], hp, dv)
    else:
        gated = gate_apply(mixed, pre_gate, own_gain).astype(BF)
    gated = after(gated, mlp_own_cols, cot_all)
    branch = lax.psum_scatter(
        nt(gated, out_cols).astype(BF), "seq", scatter_dimension=0, tiled=True
    )
    inputs = own_tokens.astype(F32)
    middle = inputs + branch.astype(F32)
    r2 = rms_scale(middle)
    n2 = middle * r2
    near_and_cot = lax.optimization_barrier(
        ((n2 * mlp_gain_full).astype(BF), cot_all) + tuple(mlp_near)
    )
    mlp_own, cot_all, mlp_near = near_and_cot[0], near_and_cot[1], near_and_cot[2:]
    mlp_cols = gather_end(mlp_own_cols, mlp_near)
    mlp_all = lax.all_gather(mlp_own, "seq", axis=0, tiled=True)
    both_w = mlp_cols[:, : 2 * ff]
    down_w = mlp_cols[:, 2 * ff :]
    d_product = nn(cot_all, down_w)
    both_pre = nn(mlp_all, both_w)
    hidden_pre = both_pre[:, :ff]
    up_pre = both_pre[:, ff:]
    sh = silu(hidden_pre)
    product = (sh * up_pre).astype(BF)
    d_both = jnp.concatenate(
        [
            (d_product * up_pre * silu_slope(hidden_pre)).astype(BF),
            (d_product * sh).astype(BF),
        ],
        axis=1,
    )
    d_mlp = lax.psum_scatter(
        nt(d_both, both_w).astype(BF), "seq", scatter_dimension=0, tiled=True
    ).astype(F32)
    d_output = own_cot.astype(F32)
    e2 = d_mlp * mlp_gain_full
    d_middle = d_output + r2 * (e2 - n2 * jnp.mean(e2 * n2, axis=-1, keepdims=True))
    both_sum = RingGrad(mlp_all, d_both)
    down_sum = RingGrad(cot_all, product)
    d_branch_own = after(d_middle.astype(BF), *both_sum.near, *down_sum.sent)
    both_sum.second(d_branch_own)
    d_branch_all = lax.all_gather(d_branch_own, "seq", axis=0, tiled=True)
    mlp_part = after(nt(product, down_w).astype(BF), d_branch_all)
    mlp_out = lax.psum_scatter(mlp_part, "seq", scatter_dimension=0, tiled=True)

    d_gated = nn(d_branch_all, out_cols)
    if vs == 1:
        d_mixed, d_gate, gain_part = gate_backward(
            d_gated, mixed, pre_gate, own_gain[None], hp, dv
        )
    else:
        d_mixed, d_gate, gain_part = gate_apply_back(d_gated, mixed, pre_gate, own_gain)
        gain_part = jnp.pad(gain_part[None], ((0, 7), (0, 0)))
    gate_sum = RingGrad(attn, d_gate)
    out_sum = RingGrad(d_branch_all, gated)
    d_attn_gate = nt(d_gate, gate_cols)
    down_sum.second(d_branch_all)
    d_mixed = after(
        d_mixed,
        *both_sum.late,
        *down_sum.late,
        *gate_sum.sent,
        *out_sum.sent,
        mlp_part,
        d_attn_gate,
    )
    mlp_rows = exchange(
        jnp.concatenate([both_sum.total(d_mixed), down_sum.total(d_mixed)], axis=1)
    )
    d_pre, d_sums = delta_backward(
        pre, pre_small, rider_all, taps, const, saved, d_mixed, gain_part, hp, dk, dv
    )
    d_pre, d_sums, mlp_out, mlp_rows = lax.optimization_barrier(
        (d_pre, d_sums, mlp_out, mlp_rows) + gate_sum.near + out_sum.near
    )[:4]
    mix_sum = RingGrad(attn, d_pre)
    gate_sum.second(d_pre)
    out_sum.second(d_pre)
    gate_rows = to_rows(gate_sum.total(), ranks)
    out_rows = to_rows(out_sum.total(), ranks)
    mix_sum.second()
    mix_rows = to_rows(mix_sum.total(), ranks)
    d_attn = lax.psum_scatter(
        (d_attn_gate + nt(d_pre, w_mix)).astype(BF), "seq", scatter_dimension=0, tiled=True
    ).astype(F32)

    output = from_ring((middle + mlp_out.astype(F32)).astype(BF))
    n = inputs * rms_scale(inputs)
    e = d_attn * attn_gain_full
    grad_tokens = from_ring(
        (d_middle + rms_scale(inputs) * (e - n * jnp.mean(e * n, axis=-1, keepdims=True))).astype(BF)
    )

    every = sum_everywhere(d_sums).reshape(ranks, 8, -1)

    def per_head(part, lead):
        part = part.reshape(ranks // vs, vs, lead, -1).sum(axis=1)
        return jnp.transpose(part, (1, 0, 2)).reshape(lead, -1)

    every_taps = every[:, :KERNEL]
    grad_conv_value = jnp.transpose(every_taps[:, :, at_v:], (1, 0, 2)).reshape(KERNEL, -1)
    gain_sum = every[:, 6, :dv].reshape(ranks // vs, vs, dv).sum(axis=0).reshape(-1)
    grad_query = plan.join_keys(mix_rows[:, :, :at_k])
    grad_key = plan.join_keys(mix_rows[:, :, at_k:at_v])
    grad_value = plan.join_even(mix_rows[:, :, at_v:at_s])
    grad_decay = plan.join_keys(mix_rows[:, :, at_s : at_s + hp])
    grad_beta = plan.join_keys(mix_rows[:, :, at_s + hp : at_s + 2 * hp])
    grad_gate = plan.join_even(gate_rows)
    grad_hidden, grad_up, grad_down = unpack_even(ranks, mlp_rows, 3)

    def gain_grad(gain, pairs):
        total = sum(jnp.sum(w.astype(F32) * g, axis=1) for w, g in pairs)
        return total / gain.astype(F32)

    return (
        output[None],
        grad_tokens[None],
        gain_grad(
            attn_gain,
            (
                (w_query, grad_query),
                (w_key, grad_key),
                (w_value, grad_value),
                (w_decay, grad_decay),
                (w_beta, grad_beta),
                (w_gate, grad_gate),
            ),
        ),
        grad_query,
        grad_key,
        grad_value,
        grad_decay,
        grad_beta,
        grad_gate,
        plan.join_even(out_rows),
        per_head(every_taps[:, :, :at_k], KERNEL),
        per_head(every_taps[:, :, at_k:at_v], KERNEL),
        grad_conv_value,
        per_head(every[:, 5, :hp], 1)[0],
        per_head(every[:, 4, :hp], 1)[0],
        gain_sum,
        gain_grad(mlp_gain, ((w_hidden, grad_hidden), (w_up, grad_up))),
        grad_hidden,
        grad_up,
        grad_down,
    )


def solution(mesh):
    flat = ("dp", "seq")
    tok_spec = P("dp", "seq", None)
    row_spec = P(flat, None)
    gain_spec = P(flat)
    in_specs = (
        (tok_spec, gain_spec)
        + (row_spec,) * 7
        + (P(),) * 6
        + (gain_spec,)
        + (row_spec,) * 3
        + (P("dp", "seq"), tok_spec)
    )
    out_specs = (
        (tok_spec, tok_spec, gain_spec)
        + (row_spec,) * 7
        + (P(),) * 6
        + (gain_spec,)
        + (row_spec,) * 3
    )
    return jax.shard_map(local, mesh=mesh, in_specs=in_specs, out_specs=out_specs, check_vma=False)
```

```python
import functools

import jax
import jax.numpy as jnp
from jax import lax
from jax.experimental import pallas as pl
from jax.experimental.pallas import tpu as pltpu
from jax.sharding import PartitionSpec as P

KERNEL = 4
LANES = 128
BF = jnp.bfloat16
F32 = jnp.float32
CHUNK = 128


def rms_scale(value):
    return lax.rsqrt(jnp.mean(value * value, axis=-1, keepdims=True) + 1e-05)


def dot_f32(left, right, dims):
    return lax.dot_general(left, right, (dims, ((), ())), preferred_element_type=F32)


def nn(left, right):
    return dot_f32(left, right, ((1,), (0,)))


def nt(left, right):
    return dot_f32(left, right, ((1,), (1,)))


def tn(left, right):
    return dot_f32(left, right, ((0,), (0,)))


def silu(value):
    return value * jax.nn.sigmoid(value)


def silu_slope(value):
    s = jax.nn.sigmoid(value)
    return s * (1.0 + value * (1.0 - s))


class Plan:
    def __init__(self, ranks, heads, key_dim, value_dim, hidden):
        self.ranks = ranks
        self.heads = heads
        self.key_dim = key_dim
        self.hp = max(1, heads // ranks)
        self.vs = max(1, ranks // heads)
        self.dv = value_dim // self.vs
        self.value_dim = value_dim
        self.ff = hidden // ranks

    def split_keys(self, array):
        rows = array.shape[0]
        grouped = array.reshape(rows, self.heads // self.hp, -1)
        return jnp.repeat(grouped, self.vs, axis=1) if self.vs > 1 else grouped

    def split_even(self, array):
        return array.reshape(array.shape[0], self.ranks, -1)

    def join_keys(self, array):
        ranks, rows, width = array.shape
        array = array.astype(F32)
        if self.vs > 1:
            array = array.reshape(ranks // self.vs, self.vs, rows, width).sum(axis=1)
        return jnp.transpose(array, (1, 0, 2)).reshape(rows, -1)

    def join_even(self, array):
        return jnp.transpose(array, (1, 0, 2)).reshape(array.shape[1], -1).astype(F32)

    def value_sum(self, array):
        step = 1
        while step < self.vs:
            pairs = [(i, i ^ step) for i in range(self.ranks)]
            array = array + lax.ppermute(array, "seq", pairs)
            step *= 2
        return array


def after(value, *earlier):
    return lax.optimization_barrier((value,) + earlier)[0]


def ring_order(count):
    return [0, 1, 3, 2] if count == 4 else list(range(count))


def ring_pairs(count):
    order = ring_order(count)
    right = [(order[i], order[(i + 1) % count]) for i in range(count)]
    return right, [(there, here) for here, there in right]


def ring_place():
    me = lax.axis_index("dp")
    return me ^ (me >> 1)


def swap_blocks(array):
    size = array.shape[1] // 4
    return jnp.concatenate(
        [array[:, : 2 * size], array[:, 3 * size :], array[:, 2 * size : 3 * size]], axis=1
    )


def to_ring(array):
    if lax.axis_size("dp") != 4:
        return array
    width = array.shape[1]
    turned = swap_blocks(array)
    twice = jnp.concatenate([turned, turned], axis=1)
    return lax.dynamic_slice_in_dim(twice, ring_place() * (width // 4), width, 1)


def from_ring(array):
    if lax.axis_size("dp") != 4:
        return array
    width = array.shape[1]
    twice = jnp.concatenate([array, array], axis=1)
    at = (4 - ring_place()) * (width // 4)
    return swap_blocks(lax.dynamic_slice_in_dim(twice, at, width, 1))


def gather_start(own):
    if lax.axis_size("dp") != 4:
        return ()
    right, left = ring_pairs(4)
    return lax.ppermute(own, "dp", right), lax.ppermute(own, "dp", left)


def gather_end(own, near):
    if lax.axis_size("dp") != 4:
        return lax.all_gather(own, "dp", axis=0, tiled=True)
    right, left = ring_pairs(4)
    half = own.shape[0] // 2
    from_left, from_right = near
    far_a = lax.ppermute(from_left[:half], "dp", right)
    far_b = lax.ppermute(from_right[half:], "dp", left)
    return jnp.concatenate([own, from_right, far_a, far_b, from_left])


class RingGrad:
    def __init__(self, left, right, kernel=True):
        self.ring = lax.axis_size("dp") == 4
        self.left, self.right, self.kernel = left, right, kernel
        rows = self.rows = left.shape[1] // lax.axis_size("dp")
        half = self.half = rows // 2
        self.sent, self.far, self.sums, self.near = (), (), (), ()
        if self.ring:
            to_right, to_left = ring_pairs(4)
            self.sent = self.products((2 * rows, half, ()), (2 * rows + half, half, ()))
            self.far = (
                lax.ppermute(self.sent[0], "dp", to_right),
                lax.ppermute(self.sent[1], "dp", to_left),
            )

    def products(self, *spans):
        if self.kernel:
            return tuple(grad_rows(self.left, self.right, spans))
        out = []
        for at, size, arrived in spans:
            total = tn(self.left[:, at : at + size], self.right)
            for array, row in arrived:
                rest = size - row - array.shape[0]
                total = total + jnp.pad(array.astype(F32), ((row, rest), (0, 0)))
            out.append(total.astype(BF))
        return tuple(out)

    def second(self, *earlier):
        if self.ring:
            to_right, to_left = ring_pairs(4)
            far_a, far_b = lax.optimization_barrier(self.far + earlier)[:2]
            rows, half = self.rows, self.half
            self.sums = self.products(
                (rows, rows, ((far_a, 0),)), (3 * rows, rows, ((far_b, half),))
            )
            self.near = (
                lax.ppermute(self.sums[0], "dp", to_right),
                lax.ppermute(self.sums[1], "dp", to_left),
            )

    def total(self, *earlier):
        if not self.ring:
            whole = tn(self.left, self.right).astype(BF)
            return lax.psum_scatter(whole, "dp", scatter_dimension=0, tiled=True)
        held = lax.optimization_barrier(self.near + earlier)
        return self.products((0, self.rows, ((held[0], 0), (held[1], 0))))[0]


class RingPair:
    def __init__(self, *pairs):
        self.ring = lax.axis_size("dp") == 4
        self.pairs = pairs
        rows = self.rows = pairs[0][0].shape[1] // lax.axis_size("dp")
        self.half = rows // 2
        self.sent, self.near, self.sums, self.late = (), (), (), ()
        if self.ring:
            to_right, to_left = ring_pairs(4)
            self.sent = self.blocks((4, 5, 3, 6))
            self.near = (
                lax.ppermute(self.sent[0], "dp", to_right),
                lax.ppermute(self.sent[1], "dp", to_left),
                lax.ppermute(self.sent[2], "dp", to_right),
                lax.ppermute(self.sent[3], "dp", to_left),
            )

    def blocks(self, which, *extra):
        return tuple(grad_blocks(self.half, which, self.pairs, *extra))

    def second(self, *earlier):
        if self.ring:
            to_right, to_left = ring_pairs(4)
            held = lax.optimization_barrier(self.near + earlier)
            far, self.near = held[:2], held[:4]
            self.sums = self.blocks((2, 7), far)
            self.late = (
                lax.ppermute(self.sums[0], "dp", to_right),
                lax.ppermute(self.sums[1], "dp", to_left),
            )

    def total(self, *earlier):
        if not self.ring:
            whole = jnp.concatenate([tn(a, b).astype(BF) for a, b in self.pairs], axis=1)
            return lax.psum_scatter(whole, "dp", scatter_dimension=0, tiled=True)
        held = lax.optimization_barrier(self.near[2:] + self.late + earlier)
        right_b, left_a, right_a, left_b = held[:4]
        return jnp.concatenate(self.blocks((0, 1), (right_a, right_b), (left_a, left_b)))


def rank_major(packed):
    return jnp.transpose(packed, (1, 0, 2)).reshape(-1, packed.shape[2])


def exchange(packed):
    return lax.all_to_all(packed, "seq", 0, 0, tiled=True)


def to_rows(mine, ranks):
    turned = lax.all_to_all(mine, "seq", 0, 0, tiled=True)
    return turned.reshape(ranks, -1, mine.shape[1])


def sum_everywhere(values):
    count = lax.axis_size("dp")
    ranks = lax.axis_size("seq")
    if count & (count - 1) or ranks & (ranks - 1):
        return lax.all_gather(lax.psum(values, "dp"), "seq", axis=0, tiled=True)
    step = 1
    while step < count:
        values = values + lax.ppermute(values, "dp", [(i, i ^ step) for i in range(count)])
        step *= 2
    rank = lax.axis_index("seq")
    held = values
    step = 1
    while step < ranks:
        other = lax.ppermute(held, "seq", [(i, i ^ step) for i in range(ranks)])
        upper = (rank & step) != 0
        held = jnp.concatenate([jnp.where(upper, other, held), jnp.where(upper, held, other)])
        step *= 2
    return held


class Pair:
    def __init__(self, value):
        self.value = value
        self.high = value.astype(BF)
        self.low = (value - self.high.astype(F32)).astype(BF)


def pair(value):
    return value if isinstance(value, Pair) else Pair(value)


NN = ((1,), (0,))
NT = ((1,), (1,))
TN = ((0,), (0,))


def dot(left, right, dims):
    a, b = pair(left), pair(right)
    return dot_f32(a.high, b.high, dims) + (
        dot_f32(a.high, b.low, dims) + dot_f32(a.low, b.high, dims)
    )


def stack(top, bottom):
    return jnp.concatenate([top, bottom], axis=0)


def grids(n):
    t = lax.broadcasted_iota(jnp.int32, (n, n), 0)
    s = lax.broadcasted_iota(jnp.int32, (n, n), 1)
    return t, s


def inverses(stricts, t, s):
    n = t.shape[0]
    eye = jnp.where(t == s, 1.0, 0.0).astype(F32)
    same = (t // 8) == (s // 8)
    small = [Pair(jnp.where(same, a, 0.0)) for a in stricts]
    square = [Pair(dot(a, a, NN)) for a in small]
    fourth = [dot(a, a, NN) for a in square]
    first = [eye - a.value for a in small]
    inv = [f + dot(f, a, NN) for f, a in zip(first, square)]
    inv = [f + dot(f, a, NN) for f, a in zip(inv, fourth)]
    size = 8
    while size < n:
        take = ((t // (2 * size)) == (s // (2 * size))) & ((t // size) != (s // size))
        held = [Pair(f) for f in inv]
        part = [dot(f, jnp.where(take, a, 0.0), NN) for f, a in zip(held, stricts)]
        inv = [f.value - dot(p, f, NN) for f, p in zip(held, part)]
        size *= 2
    return inv


def decays(cols, hp, t, s):
    n = t.shape[0]
    tri = jnp.where(t >= s, 1.0, 0.0).astype(F32)
    run = dot(tri, cols, NN)
    turned = jnp.transpose(run)
    offs = cols[:, 2 * hp : 2 * hp + 1]
    row = t[:, :1].astype(F32)
    gap = (t - s).astype(F32)
    same = (gap >= 0.0) & (offs >= gap)
    keep = offs[n - 1 : n, :] >= (n - 1.0) - row
    out = []
    for h in range(hp):
        g = run[:, h : h + 1]
        g_row = turned[h : h + 1, :]
        pairwise = jnp.where(same, jnp.exp(jnp.where(same, g - g_row, 0.0)), 0.0)
        start = jnp.where(offs > row, jnp.exp(g), 0.0)
        end = jnp.where(keep, jnp.exp(jnp.where(keep, g[n - 1 : n, :] - g, 0.0)), 0.0)
        out.append((pairwise, start, end, start[n - 1 : n, :], cols[:, hp + h : hp + h + 1]))
    return out


def lanes_of(hp, dk, dv):
    q = [slice(h * dk, (h + 1) * dk) for h in range(hp)]
    k = [slice((hp + h) * dk, (hp + h + 1) * dk) for h in range(hp)]
    v = [slice(2 * hp * dk + h * dv, 2 * hp * dk + (h + 1) * dv) for h in range(hp)]
    return q, k, v


def chunk_rows(c):
    return pl.ds(pl.multiple_of(c * CHUNK, CHUNK), CHUNK)


def chunk_cols(hp, rows, small_ref, rider_ref, const_ref):
    lane = lax.broadcasted_iota(jnp.int32, (CHUNK, LANES), 1)
    x = small_ref[rows, :]
    y = x + const_ref[1:2, :]
    logs = const_ref[0:1, :] * (jnp.maximum(y, 0.0) + jnp.log1p(jnp.exp(-jnp.abs(y))))
    beta = jax.nn.sigmoid(x)
    rider = rider_ref[rows, :].astype(F32)
    offs = rider[:, 0:1] * 64.0 + rider[:, 1:2]
    cols = jnp.where(lane < hp, logs, jnp.where(lane < 2 * hp, beta, 0.0))
    return jnp.where(lane == 2 * hp, offs, cols), offs


def conved_lanes(c, lanes, offs, pre_ref, taps_ref):
    rows = chunk_rows(c)
    above = pl.ds(pl.multiple_of(jnp.maximum(c * CHUNK - 16, 0), 16), 16)
    block = pre_ref[rows, lanes].astype(F32)
    ext = stack(pre_ref[above, lanes].astype(F32), block)
    total = taps_ref[0:1, lanes] * block
    for by in range(1, KERNEL):
        moved = pltpu.roll(ext, by, 0)[16:]
        total = total + taps_ref[by : by + 1, lanes] * jnp.where(offs >= by, moved, 0.0)
    return total


def unit_scale(u):
    return lax.rsqrt(jnp.sum(u * u, axis=1, keepdims=True) + 1e-06)


def fill_front(hp, dk, dv, c, pre_ref, small_ref, rider_ref, taps_ref, const_ref, qkv_ref, cols_ref, conv_ref):
    rows = chunk_rows(c)
    cols, offs = chunk_cols(hp, rows, small_ref, rider_ref, const_ref)
    cols_ref[rows, :] = cols
    for kind, slices in enumerate(lanes_of(hp, dk, dv)):
        for lanes in slices:
            conved = conved_lanes(c, lanes, offs, pre_ref, taps_ref)
            if conv_ref is not None:
                conv_ref[rows, lanes] = conved
            u = conved * jax.nn.sigmoid(conved)
            if kind == 0:
                u = u * (unit_scale(u) * dk ** (-0.5))
            elif kind == 1:
                u = u * unit_scale(u)
            qkv_ref[rows, lanes] = u


def fwd_kernel(
    hp, dk, dv, pre_ref, small_ref, rider_ref, taps_ref, const_ref,
    mixed_ref, state_ref, upd_ref, inv_ref, seen_ref,
    qkv_ref, cols_ref, p_ref, cur_ref,
):
    n = CHUNK
    chunks = pre_ref.shape[0] // n
    group = 2 if chunks % 2 == 0 else 1
    t, s = grids(n)
    q_at, k_at, v_at = lanes_of(hp, dk, dv)

    def prepare(step, carry):
        jobs = []
        for j in range(group):
            c = step * group + j
            fill_front(
                hp, dk, dv, c, pre_ref, small_ref, rider_ref, taps_ref, const_ref, qkv_ref, cols_ref, None
            )
            rows = chunk_rows(c)
            for h, d in enumerate(decays(cols_ref[rows, :], hp, t, s)):
                jobs.append((c, rows, h) + d)
        keys = [qkv_ref[r, k_at[h]] for _, r, h, *_ in jobs]
        both = [dot(stack(k, qkv_ref[job[1], q_at[job[2]]]), k, NT) for k, job in zip(keys, jobs)]
        strict = [jnp.where(t > s, job[3] * b[:n], 0.0) * job[7] for job, b in zip(jobs, both)]
        inv = [Pair(i) for i in inverses(strict, t, s)]
        for job, b, i, k in zip(jobs, both, inv, keys):
            c, r, h, pairwise, start, end, last, beta = job
            p_ref[c * hp + h] = pairwise * b[n:]
            inv_ref[c * hp + h] = i.value
            upd_ref[r, h * dv : (h + 1) * dv] = dot(i, beta * qkv_ref[r, v_at[h]], NN)
            seen_ref[r, h * dk : (h + 1) * dk] = dot(i, (beta * start) * k, NN)
        return carry

    lax.fori_loop(0, chunks // group, prepare, 0)
    cur_ref[...] = jnp.zeros_like(cur_ref)

    def advance(c, carry):
        rows = chunk_rows(c)
        for h, (pairwise, start, end, last, beta) in enumerate(decays(cols_ref[rows, :], hp, t, s)):
            vv = slice(h * dv, (h + 1) * dv)
            state = cur_ref[h]
            state_ref[c * hp + h] = state
            seen = seen_ref[rows, h * dk : (h + 1) * dk]
            both = dot(stack(seen, qkv_ref[rows, q_at[h]] * start), state, NN)
            update = Pair(upd_ref[rows, vv] - both[:n])
            upd_ref[rows, vv] = update.value
            mixed_ref[rows, vv] = both[n:] + dot(p_ref[c * hp + h], update, NN)
            cur_ref[h] = last * state + dot(qkv_ref[rows, k_at[h]] * end, update, TN)
        return carry

    lax.fori_loop(0, chunks, advance, 0)


def bwd_kernel(
    hp, dk, dv, pre_ref, small_ref, rider_ref, taps_ref, const_ref,
    state_ref, upd_ref, inv_ref, seen_ref, dm_ref, gain_ref,
    dpre_ref, dtaps_ref,
    qkv_ref, cols_ref, conv_ref, dcon_ref, dcols_ref, du_ref, ds_ref, cur_ref,
):
    n = CHUNK
    total = pre_ref.shape[0]
    chunks = total // n
    t, s = grids(n)
    q_at, k_at, v_at = lanes_of(hp, dk, dv)
    wide = 2 * hp * dk + hp * dv
    cur_ref[...] = jnp.zeros_like(cur_ref)
    dtaps_ref[...] = jnp.zeros_like(dtaps_ref)
    dtaps_ref[6:7, : gain_ref.shape[1]] = gain_ref[0:1, :]
    dcon_ref[total:, :] = jnp.zeros((dcon_ref.shape[0] - total, wide), F32)
    cols_ref[total:, :] = jnp.zeros((cols_ref.shape[0] - total, LANES), F32)

    def retreat(step, carry):
        c = chunks - 1 - step
        rows = chunk_rows(c)
        fill_front(
            hp, dk, dv, c, pre_ref, small_ref, rider_ref, taps_ref, const_ref, qkv_ref, cols_ref, conv_ref
        )
        for h, (pairwise, start, end, last, beta) in enumerate(decays(cols_ref[rows, :], hp, t, s)):
            vv = slice(h * dv, (h + 1) * dv)
            d_state = cur_ref[h]
            ds_ref[c * hp + h] = d_state
            dm = Pair(dm_ref[rows, vv])
            q, k = qkv_ref[rows, q_at[h]], qkv_ref[rows, k_at[h]]
            p = pairwise * dot(q, k, NT)
            du = dot(p, dm, TN) + dot(k * end, d_state, NN)
            du_ref[rows, vv] = du
            seen = seen_ref[rows, h * dk : (h + 1) * dk]
            cur_ref[h] = last * d_state + dot(q * start, dm, TN) - dot(seen, du, TN)
        return carry

    lax.fori_loop(0, chunks, retreat, 0)
    lane = lax.broadcasted_iota(jnp.int32, (n, LANES), 1)

    def through_silu(rows, lanes, dy, unit):
        conved = conv_ref[rows, lanes]
        sig = jax.nn.sigmoid(conved)
        if unit:
            u = conved * sig
            scale = unit_scale(u)
            dy = scale * dy - (scale * scale * scale) * u * jnp.sum(u * dy, axis=1, keepdims=True)
        dcon_ref[rows, lanes] = dy * (sig * (1.0 + conved * (1.0 - sig)))

    def finish(c, carry):
        rows = chunk_rows(c)
        d_cols = jnp.zeros((n, LANES), F32)
        for h, (pairwise, start, end, last, beta) in enumerate(decays(cols_ref[rows, :], hp, t, s)):
            vv = slice(h * dv, (h + 1) * dv)
            q, k, v = qkv_ref[rows, q_at[h]], qkv_ref[rows, k_at[h]], qkv_ref[rows, v_at[h]]
            dm = dm_ref[rows, vv]
            q_p, k_p, u_p = Pair(q), Pair(k), Pair(upd_ref[rows, vv])
            state = Pair(state_ref[c * hp + h])
            d_state = Pair(ds_ref[c * hp + h])
            w = dot(inv_ref[c * hp + h], du_ref[rows, vv], TN)
            scores = dot(stack(w, dm), u_p, NT)
            d_a = jnp.where(t > s, -scores[:n], 0.0)
            d_p = scores[n:]
            keys = dot(stack(k, q), k_p, NT)
            met = dot(stack(k, q), state, NN)
            r, qs = met[:n], met[n:]
            back = dot(stack(start * dm, -(beta * start) * w), state, NT)
            x = dot(u_p, d_state, NT)
            d_qk = pairwise * d_p
            d_kk = beta * (pairwise * d_a)
            d_query = back[:n] + dot(d_qk, k_p, NN)
            d_key = (
                back[n:]
                + dot(d_qk, q_p, TN)
                + dot(d_kk + jnp.transpose(d_kk), k_p, NN)
                + end * x
            )
            through_silu(rows, q_at[h], d_query * dk ** (-0.5), True)
            through_silu(rows, k_at[h], d_key, True)
            through_silu(rows, v_at[h], beta * w, False)
            inner = pairwise * d_a * keys[:n]
            d_beta = jnp.sum(w * (v - start * r), axis=1, keepdims=True) + jnp.sum(
                inner, axis=1, keepdims=True
            )
            d_start = jnp.sum(dm * qs, axis=1, keepdims=True) - beta * jnp.sum(
                w * r, axis=1, keepdims=True
            )
            e = pairwise * d_p * keys[n:] + beta * inner
            d_end = end * jnp.sum(k * x, axis=1, keepdims=True)
            d_g = (
                jnp.sum(e, axis=1, keepdims=True)
                - jnp.sum(jnp.transpose(e), axis=1, keepdims=True)
                + d_start * start
                - d_end
            )
            held = jnp.sum(
                jnp.sum(state.value * d_state.value, axis=1, keepdims=True), axis=0, keepdims=True
            )
            tail = jnp.sum(d_end, axis=0, keepdims=True) + last * held
            d_g = d_g + jnp.where(t[:, :1] == n - 1, tail, 0.0)
            d_cols = jnp.where(lane == h, d_g, d_cols)
            d_cols = jnp.where(lane == hp + h, d_beta, d_cols)
        tri = jnp.where(t >= s, 1.0, 0.0).astype(F32)
        dcols_ref[rows, :] = jnp.where(lane < hp, dot(tri, d_cols, TN), d_cols)
        return carry

    lax.fori_loop(0, chunks, finish, 0)

    def spread(c, carry):
        rows = chunk_rows(c)
        below = pl.ds(pl.multiple_of((c + 1) * n, n), 8)
        cols = cols_ref[rows, :]
        offs = cols[:, 2 * hp : 2 * hp + 1]
        offs_below = cols_ref[below, 2 * hp : 2 * hp + 1]
        for slices in (q_at, k_at, v_at):
            for lanes in slices:
                pre = pre_ref[rows, lanes].astype(F32)
                d_con = dcon_ref[rows, lanes]
                d_below = dcon_ref[below, lanes]
                out = taps_ref[0:1, lanes] * d_con
                dtaps_ref[0:1, lanes] += jnp.sum(pre * d_con, axis=0, keepdims=True)
                for by in range(1, KERNEL):
                    ext = stack(
                        jnp.where(offs >= by, d_con, 0.0), jnp.where(offs_below >= by, d_below, 0.0)
                    )
                    moved = pltpu.roll(ext, n + 8 - by, 0)[:n]
                    out = out + taps_ref[by : by + 1, lanes] * moved
                    dtaps_ref[by : by + 1, lanes] += jnp.sum(pre * moved, axis=0, keepdims=True)
                dpre_ref[rows, lanes] = out.astype(BF)
        d_cols = dcols_ref[rows, :]
        slope = const_ref[0:1, :] * jax.nn.sigmoid(small_ref[rows, :] + const_ref[1:2, :])
        d_small = jnp.where(lane < hp, d_cols * slope, d_cols * cols * (1.0 - cols))
        d_small = jnp.where(lane < 2 * hp, d_small, 0.0)
        dpre_ref[rows, wide:] = d_small.astype(BF)
        dtaps_ref[4:5, :LANES] += jnp.sum(d_small, axis=0, keepdims=True)
        dtaps_ref[5:6, :LANES] += jnp.sum(d_cols * cols, axis=0, keepdims=True)
        return carry

    lax.fori_loop(0, chunks, spread, 0)


def gate_kernel(hp, dv, mixed_ref, gate_ref, gain_ref, out_ref):
    for h in range(hp):
        at = slice(h * dv, (h + 1) * dv)
        mixed = mixed_ref[:, at]
        scale = lax.rsqrt(jnp.mean(mixed * mixed, axis=1, keepdims=True) + 1e-05)
        gate = gate_ref[:, at]
        out_ref[:, at] = (mixed * scale * gain_ref[0:1, :] * (gate * jax.nn.sigmoid(gate))).astype(BF)


def gate_back_kernel(hp, dv, d_ref, mixed_ref, gate_ref, gain_ref, dm_ref, dgate_ref, dgain_ref):
    @pl.when(pl.program_id(0) == 0)
    def _():
        dgain_ref[...] = jnp.zeros_like(dgain_ref)

    gain = gain_ref[0:1, :]
    for h in range(hp):
        at = slice(h * dv, (h + 1) * dv)
        mixed = mixed_ref[:, at]
        scale = lax.rsqrt(jnp.mean(mixed * mixed, axis=1, keepdims=True) + 1e-05)
        m = mixed * scale
        gate = gate_ref[:, at]
        sig = jax.nn.sigmoid(gate)
        through = d_ref[:, at] * (gate * sig)
        dgain_ref[0:1, :] += jnp.sum(through * m, axis=0, keepdims=True)
        em = through * gain
        dm_ref[:, at] = scale * (em - m * jnp.mean(em * m, axis=1, keepdims=True))
        slope = sig * (1.0 + gate * (1.0 - sig))
        dgate_ref[:, at] = (d_ref[:, at] * m * gain * slope).astype(BF)


def pack_kernel(ranks, *refs):
    *ins, out_ref = refs
    rows = ins[0].shape[0]
    parts = [ref[...].astype(F32) for ref in ins]
    for r in range(ranks):
        pieces = [p[:, r * (p.shape[1] // ranks) : (r + 1) * (p.shape[1] // ranks)] for p in parts]
        out_ref[r * rows : (r + 1) * rows, :] = jnp.concatenate(pieces, axis=1).astype(BF)


def unpack_kernel(ranks, in_ref, *outs):
    rows = outs[0].shape[0]
    for i, out_ref in enumerate(outs):
        size = out_ref.shape[1] // ranks
        pieces = [
            in_ref[r * rows : (r + 1) * rows, :].astype(F32)[:, i * size : (i + 1) * size]
            for r in range(ranks)
        ]
        out_ref[...] = jnp.concatenate(pieces, axis=1)


def grad_kernel(spans, left_ref, right_ref, *refs):
    adds, outs = refs[: -len(spans)], refs[-len(spans) :]
    taken = 0
    for (at, size, places), out_ref in zip(spans, outs):
        for row in range(0, size, 256):
            high = min(256, size - row)
            piece = dot_f32(left_ref[:, at + row : at + row + high], right_ref[...], TN)
            for k, (first, rows) in enumerate(places):
                if first <= row < first + rows:
                    piece = piece + adds[taken + k][row - first : row - first + high, :].astype(F32)
            out_ref[row : row + high, :] = piece.astype(BF)
        taken += len(places)


def block_kernel(half, blocks, pairs, extra, *refs):
    lefts, rights = refs[:pairs], refs[pairs : 2 * pairs]
    adds, outs = refs[2 * pairs : -len(blocks)], refs[-len(blocks) :]
    for i, block in enumerate(blocks):
        lane = 0
        for left_ref, right_ref in zip(lefts, rights):
            wide = right_ref.shape[1]
            at = slice(lane, lane + wide)
            piece = dot_f32(left_ref[:, block * half : (block + 1) * half], right_ref[...], TN)
            for k in range(extra):
                piece = piece + adds[k * len(blocks) + i][:, at].astype(F32)
            outs[i][:, at] = piece.astype(BF)
            lane += wide


VMEM_LIMIT = 60 * 2**20


def shape_of(*dims, dtype=F32):
    return jax.ShapeDtypeStruct(dims, dtype)


def grad_rows(left, right, spans):
    wide = right.shape[1]
    rows = sum(size for _, size, _ in spans)
    fixed = tuple(
        (at, size, tuple((row, x.shape[0]) for x, row in arrived)) for at, size, arrived in spans
    )
    return pl.pallas_call(
        functools.partial(grad_kernel, fixed),
        out_shape=tuple(shape_of(size, wide, dtype=BF) for _, size, _ in spans),
        compiler_params=pltpu.CompilerParams(vmem_limit_bytes=VMEM_LIMIT),
        cost_estimate=pl.CostEstimate(
            flops=2 * rows * wide * left.shape[0],
            transcendentals=0,
            bytes_accessed=2 * (left.size + right.size + rows * wide),
        ),
        name="grad_rows",
    )(left, right, *(x for _, _, arrived in spans for x, _ in arrived))


def grad_blocks(half, blocks, pairs, *extra):
    wide = sum(b.shape[1] for _, b in pairs)
    arrays = [a for a, _ in pairs] + [b for _, b in pairs] + [x for xs in extra for x in xs]
    return pl.pallas_call(
        functools.partial(block_kernel, half, blocks, len(pairs), len(extra)),
        out_shape=(shape_of(half, wide, dtype=BF),) * len(blocks),
        compiler_params=pltpu.CompilerParams(vmem_limit_bytes=VMEM_LIMIT),
        cost_estimate=pl.CostEstimate(
            flops=half * len(blocks) * wide * pairs[0][0].shape[0] // 8,
            transcendentals=0,
            bytes_accessed=half * len(blocks) * wide,
        ),
        name="grad_blocks",
    )(*arrays)


def back_kernel(pairs, *refs):
    total = dot_f32(refs[0][...], refs[pairs][...], NT)
    for i in range(1, pairs):
        total = total + dot_f32(refs[i][...], refs[pairs + i][...], NT)
    refs[-1][...] = total.astype(BF)


def back_product(*pairs):
    total, wide = pairs[0][0].shape[0], pairs[0][1].shape[0]
    rows = 256
    lefts = [a for a, _ in pairs]
    rights = [b for _, b in pairs]
    return pl.pallas_call(
        functools.partial(back_kernel, len(pairs)),
        grid=(total // rows,),
        in_specs=[pl.BlockSpec((rows, a.shape[1]), lambda i: (i, 0)) for a in lefts]
        + [pl.BlockSpec(b.shape, lambda i: (0, 0)) for b in rights],
        out_specs=pl.BlockSpec((rows, wide), lambda i: (i, 0)),
        out_shape=shape_of(total, wide, dtype=BF),
        compiler_params=pltpu.CompilerParams(vmem_limit_bytes=VMEM_LIMIT),
        cost_estimate=pl.CostEstimate(
            flops=total * wide * 256, transcendentals=0, bytes_accessed=total * wide
        ),
        name="back_product",
    )(*lefts, *rights)


def pack_even(ranks, *arrays):
    rows = arrays[0].shape[0]
    wide = sum(a.shape[1] for a in arrays) // ranks
    return pl.pallas_call(
        functools.partial(pack_kernel, ranks),
        out_shape=shape_of(ranks * rows, wide, dtype=BF),
        compiler_params=pltpu.CompilerParams(vmem_limit_bytes=VMEM_LIMIT),
        name="pack_even",
    )(*arrays)


def unpack_even(ranks, packed, count):
    rows = packed.shape[0] // ranks
    size = packed.shape[1] // count
    return pl.pallas_call(
        functools.partial(unpack_kernel, ranks),
        out_shape=(shape_of(rows, ranks * size),) * count,
        compiler_params=pltpu.CompilerParams(vmem_limit_bytes=VMEM_LIMIT),
        name="unpack_even",
    )(packed)


def delta_forward(pre, small, rider, taps, const, hp, dk, dv):
    total, wide = pre.shape
    jobs = total // CHUNK * hp
    return pl.pallas_call(
        functools.partial(fwd_kernel, hp, dk, dv),
        out_shape=(
            shape_of(total, hp * dv),
            shape_of(jobs, dk, dv),
            shape_of(total, hp * dv),
            shape_of(jobs, CHUNK, CHUNK),
            shape_of(total, hp * dk),
        ),
        scratch_shapes=[
            pltpu.VMEM((total, wide), F32),
            pltpu.VMEM((total, LANES), F32),
            pltpu.VMEM((jobs, CHUNK, CHUNK), F32),
            pltpu.VMEM((hp, dk, dv), F32),
        ],
        compiler_params=pltpu.CompilerParams(vmem_limit_bytes=VMEM_LIMIT),
        cost_estimate=pl.CostEstimate(
            flops=total * hp * 21_000_000,
            transcendentals=total * hp * CHUNK,
            bytes_accessed=total * wide * 16,
        ),
        name="delta_forward",
    )(pre, small, rider, taps, const)


def delta_backward(pre, small, rider, taps, const, saved, d_mixed, gain, hp, dk, dv):
    total, wide = pre.shape
    jobs = total // CHUNK * hp
    return pl.pallas_call(
        functools.partial(bwd_kernel, hp, dk, dv),
        out_shape=(
            shape_of(total, wide + LANES, dtype=BF),
            shape_of(8, wide),
        ),
        scratch_shapes=[
            pltpu.VMEM((total, wide), F32),
            pltpu.VMEM((total + 8, LANES), F32),
            pltpu.VMEM((total, wide), F32),
            pltpu.VMEM((total + 8, wide), F32),
            pltpu.VMEM((total, LANES), F32),
            pltpu.VMEM((total, hp * dv), F32),
            pltpu.VMEM((jobs, dk, dv), F32),
            pltpu.VMEM((hp, dk, dv), F32),
        ],
        compiler_params=pltpu.CompilerParams(vmem_limit_bytes=VMEM_LIMIT),
        cost_estimate=pl.CostEstimate(
            flops=total * hp * 5_000_000,
            transcendentals=total * hp * CHUNK,
            bytes_accessed=total * wide * 20,
        ),
        name="delta_backward",
    )(pre, small, rider, taps, const, *saved, d_mixed, gain)


GATE_ROWS = 256


def gate_forward(mixed, gate, gain, hp, dv):
    total, wide = mixed.shape
    rows = min(GATE_ROWS, total)
    block = pl.BlockSpec((rows, wide), lambda i: (i, 0))
    return pl.pallas_call(
        functools.partial(gate_kernel, hp, dv),
        grid=(total // rows,),
        in_specs=[block, block, pl.BlockSpec((1, dv), lambda i: (0, 0))],
        out_specs=block,
        out_shape=shape_of(total, wide, dtype=BF),
        name="gate_forward",
    )(mixed, gate, gain)


def gate_backward(d_gated, mixed, gate, gain, hp, dv):
    total, wide = mixed.shape
    rows = min(GATE_ROWS, total)
    block = pl.BlockSpec((rows, wide), lambda i: (i, 0))
    return pl.pallas_call(
        functools.partial(gate_back_kernel, hp, dv),
        grid=(total // rows,),
        in_specs=[block, block, block, pl.BlockSpec((1, dv), lambda i: (0, 0))],
        out_specs=(block, block, pl.BlockSpec((8, dv), lambda i: (0, 0))),
        out_shape=(
            shape_of(total, wide),
            shape_of(total, wide, dtype=BF),
            shape_of(8, dv),
        ),
        name="gate_backward",
    )(d_gated, mixed, gate, gain)


def local(
    tokens,
    attn_gain,
    w_query,
    w_key,
    w_value,
    w_decay,
    w_beta,
    w_gate,
    w_out,
    conv_query,
    conv_key,
    conv_value,
    decay_log,
    decay_bias,
    out_gain,
    mlp_gain,
    w_hidden,
    w_up,
    w_down,
    offsets,
    cotangent,
):
    ranks = lax.axis_size("seq")
    rank = lax.axis_index("seq")
    heads = decay_log.shape[0]
    width = tokens.shape[-1]
    tok = tokens.shape[1]
    length = tok * ranks
    plan = Plan(ranks, heads, w_query.shape[1] // heads, out_gain.shape[0], w_hidden.shape[1])
    hp, vs, dk, dv, ff = plan.hp, plan.vs, plan.key_dim, plan.dv, plan.ff
    rows = w_query.shape[0]

    own_tokens = to_ring(tokens[0])
    own_cot = to_ring(cotangent[0])
    rider = jnp.concatenate(
        [
            (offsets[0] // 64).astype(BF)[:, None],
            (offsets[0] % 64).astype(BF)[:, None],
            jnp.zeros((tok, LANES - 2), BF),
        ],
        axis=1,
    )
    small = jnp.concatenate(
        [
            plan.split_keys(w_decay),
            plan.split_keys(w_beta),
            jnp.broadcast_to(attn_gain[:, None, None], (rows, ranks, 1)),
            jnp.broadcast_to(mlp_gain[:, None, None], (rows, ranks, 1)),
            jnp.zeros((rows, ranks, LANES - 2 - 2 * hp), BF),
        ],
        axis=2,
    )
    mix_pack = rank_major(
        jnp.concatenate(
            [
                plan.split_keys(w_query),
                plan.split_keys(w_key),
                plan.split_even(w_value),
                small,
            ],
            axis=2,
        )
    )
    side_pack = rank_major(
        jnp.concatenate([plan.split_even(w_gate), plan.split_even(w_out)], axis=2)
    )
    mlp_pack = pack_even(ranks, w_hidden, w_up, w_down)
    mix_own = exchange(mix_pack)
    held = lax.optimization_barrier(
        (jnp.concatenate([own_tokens, rider], axis=1), side_pack, mlp_pack, mix_own)
    )
    gathered = lax.all_gather(held[0], "seq", axis=0, tiled=True)
    side_own = exchange(held[1])
    mix_own = held[3]
    w_mix = gather_end(mix_own, gather_start(mix_own))
    mlp_own_cols = exchange(after(held[2], side_own, gathered))
    side_own = after(side_own, w_mix)
    side_near = gather_start(side_own)

    at_k = hp * dk
    at_v = 2 * hp * dk
    at_s = at_v + hp * dv
    attn_gain_full = w_mix[:, at_s + 2 * hp].astype(F32)
    mlp_gain_full = w_mix[:, at_s + 2 * hp + 1].astype(F32)

    tokens_all = gathered[:, :width].astype(F32)
    normed_all = tokens_all * rms_scale(tokens_all)
    attn = (normed_all * attn_gain_full).astype(BF)
    pre = nn(attn, w_mix[:, :at_s]).astype(BF)
    pre_small = nn(attn, w_mix[:, at_s:])
    cot_all = lax.all_gather(after(own_cot, pre), "seq", axis=0, tiled=True)
    group = rank // vs
    taps_query = lax.dynamic_slice_in_dim(conv_query, group * hp * dk, hp * dk, 1)
    taps_key = lax.dynamic_slice_in_dim(conv_key, group * hp * dk, hp * dk, 1)
    taps_value = lax.dynamic_slice_in_dim(conv_value, rank * hp * dv, hp * dv, 1)
    own_log = lax.dynamic_slice_in_dim(decay_log, group * hp, hp, 0)
    own_bias = lax.dynamic_slice_in_dim(decay_bias, group * hp, hp, 0)
    own_gain = lax.dynamic_slice_in_dim(out_gain, (rank % vs) * dv, dv, 0)

    taps = jnp.concatenate([taps_query, taps_key, taps_value], axis=1)
    const = jnp.pad(jnp.stack([-jnp.exp(own_log), own_bias]), ((0, 0), (0, LANES - hp)))
    pre, pre_small = lax.optimization_barrier((pre, pre_small, side_own))[:2]
    rider_all = gathered[:, width:]
    mixed, *saved = delta_forward(pre, pre_small, rider_all, taps, const, hp, dk, dv)
    mixed, *side_near = lax.optimization_barrier((mixed,) + tuple(side_near))
    w_side = gather_end(side_own, side_near)
    gate_cols = w_side[:, : hp * dv]
    out_cols = w_side[:, hp * dv :]
    mlp_near = gather_start(after(mlp_own_cols, w_side))
    pre_gate = nn(attn, gate_cols)

    def by_head(array):
        return array.reshape(length, hp, -1)

    def gate_apply(mixed_in, gate_in, gain_in):
        m = by_head(mixed_in)
        square = plan.value_sum(jnp.sum(m * m, axis=-1, keepdims=True))
        scale = lax.rsqrt(square / plan.value_dim + 1e-05)
        return (m * scale * gain_in * silu(by_head(gate_in))).reshape(length, -1)

    def gate_apply_back(d_out, mixed_in, gate_in, gain_in):
        d, mixed_in, gate_in = by_head(d_out), by_head(mixed_in), by_head(gate_in)
        square = plan.value_sum(jnp.sum(mixed_in * mixed_in, axis=-1, keepdims=True))
        scale = lax.rsqrt(square / plan.value_dim + 1e-05)
        m = mixed_in * scale
        through = d * silu(gate_in)
        em = through * gain_in
        mean = plan.value_sum(jnp.sum(em * m, axis=-1, keepdims=True)) / plan.value_dim
        d_mix = scale * (em - m * mean)
        d_gt = d * m * gain_in * silu_slope(gate_in)
        return (
            d_mix.reshape(length, -1),
            d_gt.reshape(length, -1).astype(BF),
            jnp.sum(through * m, axis=(0, 1)),
        )

    if vs == 1:
        gated = gate_forward(mixed, pre_gate, own_gain[None], hp, dv)
    else:
        gated = gate_apply(mixed, pre_gate, own_gain).astype(BF)
    gated = after(gated, mlp_own_cols, cot_all)
    branch = lax.psum_scatter(
        nt(gated, out_cols).astype(BF), "seq", scatter_dimension=0, tiled=True
    )
    inputs = own_tokens.astype(F32)
    middle = inputs + branch.astype(F32)
    r2 = rms_scale(middle)
    n2 = middle * r2
    near_and_cot = lax.optimization_barrier(
        ((n2 * mlp_gain_full).astype(BF), cot_all) + tuple(mlp_near)
    )
    mlp_own, cot_all, mlp_near = near_and_cot[0], near_and_cot[1], near_and_cot[2:]
    mlp_cols = gather_end(mlp_own_cols, mlp_near)
    mlp_all = lax.all_gather(mlp_own, "seq", axis=0, tiled=True)
    both_w = mlp_cols[:, : 2 * ff]
    down_w = mlp_cols[:, 2 * ff :]
    d_product = nn(cot_all, down_w)
    both_pre = nn(mlp_all, both_w)
    hidden_pre = both_pre[:, :ff]
    up_pre = both_pre[:, ff:]
    sh = silu(hidden_pre)
    product = (sh * up_pre).astype(BF)
    d_both = jnp.concatenate(
        [
            (d_product * up_pre * silu_slope(hidden_pre)).astype(BF),
            (d_product * sh).astype(BF),
        ],
        axis=1,
    )
    d_mlp = lax.psum_scatter(
        nt(d_both, both_w).astype(BF), "seq", scatter_dimension=0, tiled=True
    ).astype(F32)
    d_output = own_cot.astype(F32)
    e2 = d_mlp * mlp_gain_full
    d_middle = d_output + r2 * (e2 - n2 * jnp.mean(e2 * n2, axis=-1, keepdims=True))
    down_sum = RingGrad(cot_all, product, kernel=False)
    both_sum = RingGrad(mlp_all, d_both, kernel=False)
    mlp_part = nt(product, down_w).astype(BF)
    down_sum.second(mlp_part)
    both_sum.second(mlp_part)
    d_branch_own = after(d_middle.astype(BF), *both_sum.sums, *down_sum.sums)
    d_branch_all = lax.all_gather(d_branch_own, "seq", axis=0, tiled=True)
    mlp_mine = jnp.concatenate([both_sum.total(d_branch_own), down_sum.total(d_branch_own)], axis=1)
    mlp_rows = exchange(mlp_mine)
    d_branch_all = after(d_branch_all, mlp_mine)
    mlp_out = lax.psum_scatter(
        after(mlp_part, d_branch_all), "seq", scatter_dimension=0, tiled=True
    )

    d_gated = nn(d_branch_all, out_cols)
    if vs == 1:
        d_mixed, d_gate, gain_part = gate_backward(
            d_gated, mixed, pre_gate, own_gain[None], hp, dv
        )
    else:
        d_mixed, d_gate, gain_part = gate_apply_back(d_gated, mixed, pre_gate, own_gain)
        gain_part = jnp.pad(gain_part[None], ((0, 7), (0, 0)))
    side_sum = RingPair((attn, d_gate), (d_branch_all, gated))
    d_mixed = after(d_mixed, *side_sum.sent)
    d_pre, d_sums = delta_backward(
        pre, pre_small, rider_all, taps, const, saved, d_mixed, gain_part, hp, dk, dv
    )
    held = lax.optimization_barrier((d_pre, d_sums, mlp_rows) + side_sum.near)
    d_pre, d_sums, mlp_rows = held[:3]
    side_sum.near = held[3:]
    d_attn_part = back_product((d_pre, w_mix), (d_gate, gate_cols))
    d_attn = lax.psum_scatter(d_attn_part, "seq", scatter_dimension=0, tiled=True).astype(F32)
    side_sum.second(d_attn_part)
    mix_sum = RingGrad(attn, after(d_pre, d_attn_part))
    every = sum_everywhere(after(d_sums, d_attn_part))
    mlp_out, every, *held = lax.optimization_barrier(
        (mlp_out, every) + side_sum.late + mix_sum.far
    )
    count = len(side_sum.late)
    side_sum.late, mix_sum.far = tuple(held[:count]), tuple(held[count:])
    mix_sum.second()
    side_mine = side_sum.total(*mix_sum.sums)
    side_rows = to_rows(side_mine, ranks)
    every = every.reshape(ranks, 8, -1)
    held = lax.optimization_barrier((mlp_rows, mlp_out, side_rows) + mix_sum.near)
    mlp_rows, mlp_out, side_rows = held[:3]
    mix_sum.near = held[3:]
    mix_rows = to_rows(mix_sum.total(), ranks)
    grad_hidden, grad_up, grad_down = unpack_even(ranks, mlp_rows, 3)

    output = from_ring((middle + mlp_out.astype(F32)).astype(BF))
    n = inputs * rms_scale(inputs)
    e = d_attn * attn_gain_full
    grad_tokens = from_ring(
        (d_middle + rms_scale(inputs) * (e - n * jnp.mean(e * n, axis=-1, keepdims=True))).astype(BF)
    )

    def per_head(part, lead):
        part = part.reshape(ranks // vs, vs, lead, -1).sum(axis=1)
        return jnp.transpose(part, (1, 0, 2)).reshape(lead, -1)

    every_taps = every[:, :KERNEL]
    grad_conv_value = jnp.transpose(every_taps[:, :, at_v:], (1, 0, 2)).reshape(KERNEL, -1)
    gain_sum = every[:, 6, :dv].reshape(ranks // vs, vs, dv).sum(axis=0).reshape(-1)
    grad_query = plan.join_keys(mix_rows[:, :, :at_k])
    grad_key = plan.join_keys(mix_rows[:, :, at_k:at_v])
    grad_value = plan.join_even(mix_rows[:, :, at_v:at_s])
    grad_decay = plan.join_keys(mix_rows[:, :, at_s : at_s + hp])
    grad_beta = plan.join_keys(mix_rows[:, :, at_s + hp : at_s + 2 * hp])
    grad_gate = plan.join_even(side_rows[:, :, : hp * dv])

    def gain_grad(gain, pairs):
        total = sum(jnp.sum(w.astype(F32) * g, axis=1) for w, g in pairs)
        return total / gain.astype(F32)

    return (
        output[None],
        grad_tokens[None],
        gain_grad(
            attn_gain,
            (
                (w_query, grad_query),
                (w_key, grad_key),
                (w_value, grad_value),
                (w_decay, grad_decay),
                (w_beta, grad_beta),
                (w_gate, grad_gate),
            ),
        ),
        grad_query,
        grad_key,
        grad_value,
        grad_decay,
        grad_beta,
        grad_gate,
        plan.join_even(side_rows[:, :, hp * dv :]),
        per_head(every_taps[:, :, :at_k], KERNEL),
        per_head(every_taps[:, :, at_k:at_v], KERNEL),
        grad_conv_value,
        per_head(every[:, 5, :hp], 1)[0],
        per_head(every[:, 4, :hp], 1)[0],
        gain_sum,
        gain_grad(mlp_gain, ((w_hidden, grad_hidden), (w_up, grad_up))),
        grad_hidden,
        grad_up,
        grad_down,
    )


def solution(mesh):
    flat = ("dp", "seq")
    tok_spec = P("dp", "seq", None)
    row_spec = P(flat, None)
    gain_spec = P(flat)
    in_specs = (
        (tok_spec, gain_spec)
        + (row_spec,) * 7
        + (P(),) * 6
        + (gain_spec,)
        + (row_spec,) * 3
        + (P("dp", "seq"), tok_spec)
    )
    out_specs = (
        (tok_spec, tok_spec, gain_spec)
        + (row_spec,) * 7
        + (P(),) * 6
        + (gain_spec,)
        + (row_spec,) * 3
    )
    return jax.shard_map(local, mesh=mesh, in_specs=in_specs, out_specs=out_specs, check_vma=False)
```

```python
import functools

import jax
import jax.numpy as jnp
from jax import lax
from jax.experimental import pallas as pl
from jax.experimental.pallas import tpu as pltpu
from jax.sharding import PartitionSpec as P

KERNEL = 4
LANES = 128
BF = jnp.bfloat16
F32 = jnp.float32
CHUNK = 128


def rms_scale(value):
    return lax.rsqrt(jnp.mean(value * value, axis=-1, keepdims=True) + 1e-05)


def dot_f32(left, right, dims):
    return lax.dot_general(left, right, (dims, ((), ())), preferred_element_type=F32)


def nn(left, right):
    return dot_f32(left, right, ((1,), (0,)))


def nt(left, right):
    return dot_f32(left, right, ((1,), (1,)))


def tn(left, right):
    return dot_f32(left, right, ((0,), (0,)))


def silu(value):
    return value * jax.nn.sigmoid(value)


def silu_slope(value):
    s = jax.nn.sigmoid(value)
    return s * (1.0 + value * (1.0 - s))


class Plan:
    def __init__(self, ranks, heads, key_dim, value_dim, hidden):
        self.ranks = ranks
        self.heads = heads
        self.key_dim = key_dim
        self.hp = max(1, heads // ranks)
        self.vs = max(1, ranks // heads)
        self.dv = value_dim // self.vs
        self.value_dim = value_dim
        self.ff = hidden // ranks

    def split_keys(self, array):
        rows = array.shape[0]
        grouped = array.reshape(rows, self.heads // self.hp, -1)
        return jnp.repeat(grouped, self.vs, axis=1) if self.vs > 1 else grouped

    def split_even(self, array):
        return array.reshape(array.shape[0], self.ranks, -1)

    def join_keys(self, array):
        ranks, rows, width = array.shape
        array = array.astype(F32)
        if self.vs > 1:
            array = array.reshape(ranks // self.vs, self.vs, rows, width).sum(axis=1)
        return jnp.transpose(array, (1, 0, 2)).reshape(rows, -1)

    def join_even(self, array):
        return jnp.transpose(array, (1, 0, 2)).reshape(array.shape[1], -1).astype(F32)

    def value_sum(self, array):
        step = 1
        while step < self.vs:
            pairs = [(i, i ^ step) for i in range(self.ranks)]
            array = array + lax.ppermute(array, "seq", pairs)
            step *= 2
        return array


def after(value, *earlier):
    return lax.optimization_barrier((value,) + earlier)[0]


def ring_order(count):
    return [0, 1, 3, 2] if count == 4 else list(range(count))


def ring_pairs(count):
    order = ring_order(count)
    right = [(order[i], order[(i + 1) % count]) for i in range(count)]
    return right, [(there, here) for here, there in right]


def ring_place():
    me = lax.axis_index("dp")
    return me ^ (me >> 1)


def swap_blocks(array):
    size = array.shape[1] // 4
    return jnp.concatenate(
        [array[:, : 2 * size], array[:, 3 * size :], array[:, 2 * size : 3 * size]], axis=1
    )


def to_ring(array):
    if lax.axis_size("dp") != 4:
        return array
    width = array.shape[1]
    turned = swap_blocks(array)
    twice = jnp.concatenate([turned, turned], axis=1)
    return lax.dynamic_slice_in_dim(twice, ring_place() * (width // 4), width, 1)


def from_ring(array):
    if lax.axis_size("dp") != 4:
        return array
    width = array.shape[1]
    twice = jnp.concatenate([array, array], axis=1)
    at = (4 - ring_place()) * (width // 4)
    return swap_blocks(lax.dynamic_slice_in_dim(twice, at, width, 1))


def gather_start(own):
    if lax.axis_size("dp") != 4:
        return ()
    right, left = ring_pairs(4)
    return lax.ppermute(own, "dp", right), lax.ppermute(own, "dp", left)


def gather_end(own, near):
    if lax.axis_size("dp") != 4:
        return lax.all_gather(own, "dp", axis=0, tiled=True)
    right, left = ring_pairs(4)
    half = own.shape[0] // 2
    from_left, from_right = near
    far_a = lax.ppermute(from_left[:half], "dp", right)
    far_b = lax.ppermute(from_right[half:], "dp", left)
    return jnp.concatenate([own, from_right, far_a, far_b, from_left])


class RingGrad:
    def __init__(self, left, right, kernel=True):
        self.ring = lax.axis_size("dp") == 4
        self.left, self.right, self.kernel = left, right, kernel
        rows = self.rows = left.shape[1] // lax.axis_size("dp")
        half = self.half = rows // 2
        self.sent, self.far, self.sums, self.near = (), (), (), ()
        if self.ring:
            to_right, to_left = ring_pairs(4)
            self.sent = self.products((2 * rows, half, ()), (2 * rows + half, half, ()))
            self.far = (
                lax.ppermute(self.sent[0], "dp", to_right),
                lax.ppermute(self.sent[1], "dp", to_left),
            )

    def products(self, *spans):
        if self.kernel:
            return tuple(grad_rows(self.left, self.right, spans))
        out = []
        for at, size, arrived in spans:
            total = tn(self.left[:, at : at + size], self.right)
            for array, row in arrived:
                rest = size - row - array.shape[0]
                total = total + jnp.pad(array.astype(F32), ((row, rest), (0, 0)))
            out.append(total.astype(BF))
        return tuple(out)

    def second(self, *earlier):
        if self.ring:
            to_right, to_left = ring_pairs(4)
            far_a, far_b = lax.optimization_barrier(self.far + earlier)[:2]
            rows, half = self.rows, self.half
            self.sums = self.products(
                (rows, rows, ((far_a, 0),)), (3 * rows, rows, ((far_b, half),))
            )
            self.near = (
                lax.ppermute(self.sums[0], "dp", to_right),
                lax.ppermute(self.sums[1], "dp", to_left),
            )

    def total(self, *earlier):
        if not self.ring:
            whole = tn(self.left, self.right).astype(BF)
            return lax.psum_scatter(whole, "dp", scatter_dimension=0, tiled=True)
        held = lax.optimization_barrier(self.near + earlier)
        return self.products((0, self.rows, ((held[0], 0), (held[1], 0))))[0]


class RingPair:
    def __init__(self, *pairs):
        self.ring = lax.axis_size("dp") == 4
        self.pairs = pairs
        rows = self.rows = pairs[0][0].shape[1] // lax.axis_size("dp")
        self.half = rows // 2
        self.sent, self.near, self.sums, self.late = (), (), (), ()
        if self.ring:
            to_right, to_left = ring_pairs(4)
            self.sent = self.blocks((4, 5, 3, 6))
            self.near = (
                lax.ppermute(self.sent[0], "dp", to_right),
                lax.ppermute(self.sent[1], "dp", to_left),
                lax.ppermute(self.sent[2], "dp", to_right),
                lax.ppermute(self.sent[3], "dp", to_left),
            )

    def blocks(self, which, *extra):
        return tuple(grad_blocks(self.half, which, self.pairs, *extra))

    def second(self, *earlier):
        if self.ring:
            to_right, to_left = ring_pairs(4)
            held = lax.optimization_barrier(self.near + earlier)
            far, self.near = held[:2], held[:4]
            self.sums = self.blocks((2, 7), far)
            self.late = (
                lax.ppermute(self.sums[0], "dp", to_right),
                lax.ppermute(self.sums[1], "dp", to_left),
            )

    def total(self, *earlier):
        if not self.ring:
            whole = jnp.concatenate([tn(a, b).astype(BF) for a, b in self.pairs], axis=1)
            return lax.psum_scatter(whole, "dp", scatter_dimension=0, tiled=True)
        held = lax.optimization_barrier(self.near[2:] + self.late + earlier)
        right_b, left_a, right_a, left_b = held[:4]
        return jnp.concatenate(self.blocks((0, 1), (right_a, right_b), (left_a, left_b)))


def rank_major(packed):
    return jnp.transpose(packed, (1, 0, 2)).reshape(-1, packed.shape[2])


def exchange(packed):
    return lax.all_to_all(packed, "seq", 0, 0, tiled=True)


def to_rows(mine, ranks):
    turned = lax.all_to_all(mine, "seq", 0, 0, tiled=True)
    return turned.reshape(ranks, -1, mine.shape[1])


def sum_dp(values):
    count = lax.axis_size("dp")
    if count & (count - 1):
        return lax.psum(values, "dp")
    step = 1
    while step < count:
        values = values + lax.ppermute(values, "dp", [(i, i ^ step) for i in range(count)])
        step *= 2
    return values


def gather_small(values):
    ranks = lax.axis_size("seq")
    if ranks & (ranks - 1):
        return lax.all_gather(values, "seq", axis=0, tiled=True)
    rank = lax.axis_index("seq")
    step = 1
    while step < ranks:
        other = lax.ppermute(values, "seq", [(i, i ^ step) for i in range(ranks)])
        upper = (rank & step) != 0
        values = jnp.concatenate(
            [jnp.where(upper, other, values), jnp.where(upper, values, other)]
        )
        step *= 2
    return values


class Pair:
    def __init__(self, value):
        self.value = value
        self.high = value.astype(BF)
        self.low = (value - self.high.astype(F32)).astype(BF)


def pair(value):
    return value if isinstance(value, Pair) else Pair(value)


NN = ((1,), (0,))
NT = ((1,), (1,))
TN = ((0,), (0,))


def dot(left, right, dims):
    a, b = pair(left), pair(right)
    return dot_f32(a.high, b.high, dims) + (
        dot_f32(a.high, b.low, dims) + dot_f32(a.low, b.high, dims)
    )


def stack(top, bottom):
    return jnp.concatenate([top, bottom], axis=0)


def grids(n):
    t = lax.broadcasted_iota(jnp.int32, (n, n), 0)
    s = lax.broadcasted_iota(jnp.int32, (n, n), 1)
    return t, s


def inverses(stricts, t, s):
    n = t.shape[0]
    eye = jnp.where(t == s, 1.0, 0.0).astype(F32)
    same = (t // 8) == (s // 8)
    small = [Pair(jnp.where(same, a, 0.0)) for a in stricts]
    square = [Pair(dot(a, a, NN)) for a in small]
    fourth = [dot(a, a, NN) for a in square]
    first = [eye - a.value for a in small]
    inv = [f + dot(f, a, NN) for f, a in zip(first, square)]
    inv = [f + dot(f, a, NN) for f, a in zip(inv, fourth)]
    size = 8
    while size < n:
        take = ((t // (2 * size)) == (s // (2 * size))) & ((t // size) != (s // size))
        held = [Pair(f) for f in inv]
        part = [dot(f, jnp.where(take, a, 0.0), NN) for f, a in zip(held, stricts)]
        inv = [f.value - dot(p, f, NN) for f, p in zip(held, part)]
        size *= 2
    return inv


def decays(cols, hp, t, s):
    n = t.shape[0]
    tri = jnp.where(t >= s, 1.0, 0.0).astype(F32)
    run = dot(tri, cols, NN)
    turned = jnp.transpose(run)
    offs = cols[:, 2 * hp : 2 * hp + 1]
    row = t[:, :1].astype(F32)
    gap = (t - s).astype(F32)
    same = (gap >= 0.0) & (offs >= gap)
    keep = offs[n - 1 : n, :] >= (n - 1.0) - row
    out = []
    for h in range(hp):
        g = run[:, h : h + 1]
        g_row = turned[h : h + 1, :]
        pairwise = jnp.where(same, jnp.exp(jnp.where(same, g - g_row, 0.0)), 0.0)
        start = jnp.where(offs > row, jnp.exp(g), 0.0)
        end = jnp.where(keep, jnp.exp(jnp.where(keep, g[n - 1 : n, :] - g, 0.0)), 0.0)
        out.append((pairwise, start, end, start[n - 1 : n, :], cols[:, hp + h : hp + h + 1]))
    return out


def lanes_of(hp, dk, dv):
    q = [slice(h * dk, (h + 1) * dk) for h in range(hp)]
    k = [slice((hp + h) * dk, (hp + h + 1) * dk) for h in range(hp)]
    v = [slice(2 * hp * dk + h * dv, 2 * hp * dk + (h + 1) * dv) for h in range(hp)]
    return q, k, v


def chunk_rows(c):
    return pl.ds(pl.multiple_of(c * CHUNK, CHUNK), CHUNK)


def chunk_cols(hp, rows, small_ref, rider_ref, const_ref):
    lane = lax.broadcasted_iota(jnp.int32, (CHUNK, LANES), 1)
    x = small_ref[rows, :]
    y = x + const_ref[1:2, :]
    logs = const_ref[0:1, :] * (jnp.maximum(y, 0.0) + jnp.log1p(jnp.exp(-jnp.abs(y))))
    beta = jax.nn.sigmoid(x)
    offs = rider_ref[rows, 0:1]
    cols = jnp.where(lane < hp, logs, jnp.where(lane < 2 * hp, beta, 0.0))
    return jnp.where(lane == 2 * hp, offs, cols), offs


def conved_lanes(c, lanes, offs, pre_ref, taps_ref):
    rows = chunk_rows(c)
    above = pl.ds(pl.multiple_of(jnp.maximum(c * CHUNK - 16, 0), 16), 16)
    block = pre_ref[rows, lanes].astype(F32)
    ext = stack(pre_ref[above, lanes].astype(F32), block)
    total = taps_ref[0:1, lanes] * block
    for by in range(1, KERNEL):
        moved = pltpu.roll(ext, by, 0)[16:]
        total = total + taps_ref[by : by + 1, lanes] * jnp.where(offs >= by, moved, 0.0)
    return total


def unit_scale(u):
    return lax.rsqrt(jnp.sum(u * u, axis=1, keepdims=True) + 1e-06)


def fill_front(hp, dk, dv, c, pre_ref, small_ref, rider_ref, taps_ref, const_ref, qkv_ref, cols_ref, conv_ref):
    rows = chunk_rows(c)
    cols, offs = chunk_cols(hp, rows, small_ref, rider_ref, const_ref)
    cols_ref[rows, :] = cols
    for kind, slices in enumerate(lanes_of(hp, dk, dv)):
        for lanes in slices:
            conved = conved_lanes(c, lanes, offs, pre_ref, taps_ref)
            if conv_ref is not None:
                conv_ref[rows, lanes] = conved
            u = conved * jax.nn.sigmoid(conved)
            if kind == 0:
                u = u * (unit_scale(u) * dk ** (-0.5))
            elif kind == 1:
                u = u * unit_scale(u)
            qkv_ref[rows, lanes] = u


def fwd_kernel(
    hp, dk, dv, pre_ref, small_ref, rider_ref, taps_ref, const_ref,
    mixed_ref, state_ref, upd_ref, inv_ref, seen_ref,
    qkv_ref, cols_ref, p_ref, cur_ref,
):
    n = CHUNK
    chunks = pre_ref.shape[0] // n
    group = 2 if chunks % 2 == 0 else 1
    t, s = grids(n)
    q_at, k_at, v_at = lanes_of(hp, dk, dv)

    def prepare(step, carry):
        jobs = []
        for j in range(group):
            c = step * group + j
            fill_front(
                hp, dk, dv, c, pre_ref, small_ref, rider_ref, taps_ref, const_ref, qkv_ref, cols_ref, None
            )
            rows = chunk_rows(c)
            for h, d in enumerate(decays(cols_ref[rows, :], hp, t, s)):
                jobs.append((c, rows, h) + d)
        keys = [qkv_ref[r, k_at[h]] for _, r, h, *_ in jobs]
        both = [dot(stack(k, qkv_ref[job[1], q_at[job[2]]]), k, NT) for k, job in zip(keys, jobs)]
        strict = [jnp.where(t > s, job[3] * b[:n], 0.0) * job[7] for job, b in zip(jobs, both)]
        inv = [Pair(i) for i in inverses(strict, t, s)]
        for job, b, i, k in zip(jobs, both, inv, keys):
            c, r, h, pairwise, start, end, last, beta = job
            p_ref[c * hp + h] = pairwise * b[n:]
            inv_ref[c * hp + h] = i.value
            upd_ref[r, h * dv : (h + 1) * dv] = dot(i, beta * qkv_ref[r, v_at[h]], NN)
            seen_ref[r, h * dk : (h + 1) * dk] = dot(i, (beta * start) * k, NN)
        return carry

    lax.fori_loop(0, chunks // group, prepare, 0)
    cur_ref[...] = jnp.zeros_like(cur_ref)

    def advance(c, carry):
        rows = chunk_rows(c)
        for h, (pairwise, start, end, last, beta) in enumerate(decays(cols_ref[rows, :], hp, t, s)):
            vv = slice(h * dv, (h + 1) * dv)
            state = cur_ref[h]
            state_ref[c * hp + h] = state
            seen = seen_ref[rows, h * dk : (h + 1) * dk]
            both = dot(stack(seen, qkv_ref[rows, q_at[h]] * start), state, NN)
            update = Pair(upd_ref[rows, vv] - both[:n])
            upd_ref[rows, vv] = update.value
            mixed_ref[rows, vv] = both[n:] + dot(p_ref[c * hp + h], update, NN)
            cur_ref[h] = last * state + dot(qkv_ref[rows, k_at[h]] * end, update, TN)
        return carry

    lax.fori_loop(0, chunks, advance, 0)


def bwd_kernel(
    hp, dk, dv, pre_ref, small_ref, rider_ref, taps_ref, const_ref,
    state_ref, upd_ref, inv_ref, seen_ref, dm_ref, gain_ref,
    dpre_ref, dtaps_ref,
    qkv_ref, cols_ref, conv_ref, dcon_ref, dcols_ref, du_ref, ds_ref, cur_ref,
):
    n = CHUNK
    total = pre_ref.shape[0]
    chunks = total // n
    t, s = grids(n)
    q_at, k_at, v_at = lanes_of(hp, dk, dv)
    wide = 2 * hp * dk + hp * dv
    cur_ref[...] = jnp.zeros_like(cur_ref)
    dtaps_ref[...] = jnp.zeros_like(dtaps_ref)
    dtaps_ref[6:7, : gain_ref.shape[1]] = gain_ref[0:1, :]
    dcon_ref[total:, :] = jnp.zeros((dcon_ref.shape[0] - total, wide), F32)
    cols_ref[total:, :] = jnp.zeros((cols_ref.shape[0] - total, LANES), F32)

    def retreat(step, carry):
        c = chunks - 1 - step
        rows = chunk_rows(c)
        fill_front(
            hp, dk, dv, c, pre_ref, small_ref, rider_ref, taps_ref, const_ref, qkv_ref, cols_ref, conv_ref
        )
        for h, (pairwise, start, end, last, beta) in enumerate(decays(cols_ref[rows, :], hp, t, s)):
            vv = slice(h * dv, (h + 1) * dv)
            d_state = cur_ref[h]
            ds_ref[c * hp + h] = d_state
            dm = Pair(dm_ref[rows, vv])
            q, k = qkv_ref[rows, q_at[h]], qkv_ref[rows, k_at[h]]
            p = pairwise * dot(q, k, NT)
            du = dot(p, dm, TN) + dot(k * end, d_state, NN)
            du_ref[rows, vv] = du
            seen = seen_ref[rows, h * dk : (h + 1) * dk]
            cur_ref[h] = last * d_state + dot(q * start, dm, TN) - dot(seen, du, TN)
        return carry

    lax.fori_loop(0, chunks, retreat, 0)
    lane = lax.broadcasted_iota(jnp.int32, (n, LANES), 1)

    def through_silu(rows, lanes, dy, unit):
        conved = conv_ref[rows, lanes]
        sig = jax.nn.sigmoid(conved)
        if unit:
            u = conved * sig
            scale = unit_scale(u)
            dy = scale * dy - (scale * scale * scale) * u * jnp.sum(u * dy, axis=1, keepdims=True)
        dcon_ref[rows, lanes] = dy * (sig * (1.0 + conved * (1.0 - sig)))

    def finish(c, carry):
        rows = chunk_rows(c)
        d_cols = jnp.zeros((n, LANES), F32)
        for h, (pairwise, start, end, last, beta) in enumerate(decays(cols_ref[rows, :], hp, t, s)):
            vv = slice(h * dv, (h + 1) * dv)
            q, k, v = qkv_ref[rows, q_at[h]], qkv_ref[rows, k_at[h]], qkv_ref[rows, v_at[h]]
            dm = dm_ref[rows, vv]
            q_p, k_p, u_p = Pair(q), Pair(k), Pair(upd_ref[rows, vv])
            state = Pair(state_ref[c * hp + h])
            d_state = Pair(ds_ref[c * hp + h])
            w = dot(inv_ref[c * hp + h], du_ref[rows, vv], TN)
            scores = dot(stack(w, dm), u_p, NT)
            d_a = jnp.where(t > s, -scores[:n], 0.0)
            d_p = scores[n:]
            keys = dot(stack(k, q), k_p, NT)
            met = dot(stack(k, q), state, NN)
            r, qs = met[:n], met[n:]
            back = dot(stack(start * dm, -(beta * start) * w), state, NT)
            x = dot(u_p, d_state, NT)
            d_qk = pairwise * d_p
            d_kk = beta * (pairwise * d_a)
            d_query = back[:n] + dot(d_qk, k_p, NN)
            d_key = (
                back[n:]
                + dot(d_qk, q_p, TN)
                + dot(d_kk + jnp.transpose(d_kk), k_p, NN)
                + end * x
            )
            through_silu(rows, q_at[h], d_query * dk ** (-0.5), True)
            through_silu(rows, k_at[h], d_key, True)
            through_silu(rows, v_at[h], beta * w, False)
            inner = pairwise * d_a * keys[:n]
            d_beta = jnp.sum(w * (v - start * r), axis=1, keepdims=True) + jnp.sum(
                inner, axis=1, keepdims=True
            )
            d_start = jnp.sum(dm * qs, axis=1, keepdims=True) - beta * jnp.sum(
                w * r, axis=1, keepdims=True
            )
            e = pairwise * d_p * keys[n:] + beta * inner
            d_end = end * jnp.sum(k * x, axis=1, keepdims=True)
            d_g = (
                jnp.sum(e, axis=1, keepdims=True)
                - jnp.sum(jnp.transpose(e), axis=1, keepdims=True)
                + d_start * start
                - d_end
            )
            held = jnp.sum(
                jnp.sum(state.value * d_state.value, axis=1, keepdims=True), axis=0, keepdims=True
            )
            tail = jnp.sum(d_end, axis=0, keepdims=True) + last * held
            d_g = d_g + jnp.where(t[:, :1] == n - 1, tail, 0.0)
            d_cols = jnp.where(lane == h, d_g, d_cols)
            d_cols = jnp.where(lane == hp + h, d_beta, d_cols)
        tri = jnp.where(t >= s, 1.0, 0.0).astype(F32)
        dcols_ref[rows, :] = jnp.where(lane < hp, dot(tri, d_cols, TN), d_cols)
        return carry

    lax.fori_loop(0, chunks, finish, 0)

    def spread(c, carry):
        rows = chunk_rows(c)
        below = pl.ds(pl.multiple_of((c + 1) * n, n), 8)
        cols = cols_ref[rows, :]
        offs = cols[:, 2 * hp : 2 * hp + 1]
        offs_below = cols_ref[below, 2 * hp : 2 * hp + 1]
        for slices in (q_at, k_at, v_at):
            for lanes in slices:
                pre = pre_ref[rows, lanes].astype(F32)
                d_con = dcon_ref[rows, lanes]
                d_below = dcon_ref[below, lanes]
                out = taps_ref[0:1, lanes] * d_con
                dtaps_ref[0:1, lanes] += jnp.sum(pre * d_con, axis=0, keepdims=True)
                for by in range(1, KERNEL):
                    ext = stack(
                        jnp.where(offs >= by, d_con, 0.0), jnp.where(offs_below >= by, d_below, 0.0)
                    )
                    moved = pltpu.roll(ext, n + 8 - by, 0)[:n]
                    out = out + taps_ref[by : by + 1, lanes] * moved
                    dtaps_ref[by : by + 1, lanes] += jnp.sum(pre * moved, axis=0, keepdims=True)
                dpre_ref[rows, lanes] = out.astype(BF)
        d_cols = dcols_ref[rows, :]
        slope = const_ref[0:1, :] * jax.nn.sigmoid(small_ref[rows, :] + const_ref[1:2, :])
        d_small = jnp.where(lane < hp, d_cols * slope, d_cols * cols * (1.0 - cols))
        d_small = jnp.where(lane < 2 * hp, d_small, 0.0)
        dpre_ref[rows, wide:] = d_small.astype(BF)
        dtaps_ref[4:5, :LANES] += jnp.sum(d_small, axis=0, keepdims=True)
        dtaps_ref[5:6, :LANES] += jnp.sum(d_cols * cols, axis=0, keepdims=True)
        return carry

    lax.fori_loop(0, chunks, spread, 0)


def gate_kernel(hp, dv, mixed_ref, gate_ref, gain_ref, out_ref):
    for h in range(hp):
        at = slice(h * dv, (h + 1) * dv)
        mixed = mixed_ref[:, at]
        scale = lax.rsqrt(jnp.mean(mixed * mixed, axis=1, keepdims=True) + 1e-05)
        gate = gate_ref[:, at]
        out_ref[:, at] = (mixed * scale * gain_ref[0:1, :] * (gate * jax.nn.sigmoid(gate))).astype(BF)


def gate_back_kernel(hp, dv, d_ref, mixed_ref, gate_ref, gain_ref, dm_ref, dgate_ref, dgain_ref):
    @pl.when(pl.program_id(0) == 0)
    def _():
        dgain_ref[...] = jnp.zeros_like(dgain_ref)

    gain = gain_ref[0:1, :]
    for h in range(hp):
        at = slice(h * dv, (h + 1) * dv)
        mixed = mixed_ref[:, at]
        scale = lax.rsqrt(jnp.mean(mixed * mixed, axis=1, keepdims=True) + 1e-05)
        m = mixed * scale
        gate = gate_ref[:, at]
        sig = jax.nn.sigmoid(gate)
        through = d_ref[:, at] * (gate * sig)
        dgain_ref[0:1, :] += jnp.sum(through * m, axis=0, keepdims=True)
        em = through * gain
        dm_ref[:, at] = scale * (em - m * jnp.mean(em * m, axis=1, keepdims=True))
        slope = sig * (1.0 + gate * (1.0 - sig))
        dgate_ref[:, at] = (d_ref[:, at] * m * gain * slope).astype(BF)


def pack_kernel(ranks, *refs):
    *ins, out_ref = refs
    rows = ins[0].shape[0]
    parts = [ref[...].astype(F32) for ref in ins]
    for r in range(ranks):
        pieces = [p[:, r * (p.shape[1] // ranks) : (r + 1) * (p.shape[1] // ranks)] for p in parts]
        out_ref[r * rows : (r + 1) * rows, :] = jnp.concatenate(pieces, axis=1).astype(BF)


def unpack_kernel(ranks, in_ref, *outs):
    rows = outs[0].shape[0]
    for i, out_ref in enumerate(outs):
        size = out_ref.shape[1] // ranks
        pieces = [
            in_ref[r * rows : (r + 1) * rows, :].astype(F32)[:, i * size : (i + 1) * size]
            for r in range(ranks)
        ]
        out_ref[...] = jnp.concatenate(pieces, axis=1)


def grad_kernel(spans, left_ref, right_ref, *refs):
    adds, outs = refs[: -len(spans)], refs[-len(spans) :]
    taken = 0
    for (at, size, places), out_ref in zip(spans, outs):
        for row in range(0, size, 256):
            high = min(256, size - row)
            piece = dot_f32(left_ref[:, at + row : at + row + high], right_ref[...], TN)
            for k, (first, rows) in enumerate(places):
                if first <= row < first + rows:
                    piece = piece + adds[taken + k][row - first : row - first + high, :].astype(F32)
            out_ref[row : row + high, :] = piece.astype(BF)
        taken += len(places)


def block_kernel(half, blocks, pairs, extra, *refs):
    lefts, rights = refs[:pairs], refs[pairs : 2 * pairs]
    adds, outs = refs[2 * pairs : -len(blocks)], refs[-len(blocks) :]
    for i, block in enumerate(blocks):
        lane = 0
        for left_ref, right_ref in zip(lefts, rights):
            wide = right_ref.shape[1]
            at = slice(lane, lane + wide)
            piece = dot_f32(left_ref[:, block * half : (block + 1) * half], right_ref[...], TN)
            for k in range(extra):
                piece = piece + adds[k * len(blocks) + i][:, at].astype(F32)
            outs[i][:, at] = piece.astype(BF)
            lane += wide


VMEM_LIMIT = 60 * 2**20


def shape_of(*dims, dtype=F32):
    return jax.ShapeDtypeStruct(dims, dtype)


def grad_rows(left, right, spans):
    wide = right.shape[1]
    rows = sum(size for _, size, _ in spans)
    fixed = tuple(
        (at, size, tuple((row, x.shape[0]) for x, row in arrived)) for at, size, arrived in spans
    )
    return pl.pallas_call(
        functools.partial(grad_kernel, fixed),
        out_shape=tuple(shape_of(size, wide, dtype=BF) for _, size, _ in spans),
        compiler_params=pltpu.CompilerParams(vmem_limit_bytes=VMEM_LIMIT),
        cost_estimate=pl.CostEstimate(
            flops=2 * rows * wide * left.shape[0],
            transcendentals=0,
            bytes_accessed=2 * (left.size + right.size + rows * wide),
        ),
        name="grad_rows",
    )(left, right, *(x for _, _, arrived in spans for x, _ in arrived))


def grad_blocks(half, blocks, pairs, *extra):
    wide = sum(b.shape[1] for _, b in pairs)
    arrays = [a for a, _ in pairs] + [b for _, b in pairs] + [x for xs in extra for x in xs]
    return pl.pallas_call(
        functools.partial(block_kernel, half, blocks, len(pairs), len(extra)),
        out_shape=(shape_of(half, wide, dtype=BF),) * len(blocks),
        compiler_params=pltpu.CompilerParams(vmem_limit_bytes=VMEM_LIMIT),
        cost_estimate=pl.CostEstimate(
            flops=half * len(blocks) * wide * pairs[0][0].shape[0] // 8,
            transcendentals=0,
            bytes_accessed=half * len(blocks) * wide,
        ),
        name="grad_blocks",
    )(*arrays)


def back_kernel(pairs, *refs):
    total = dot_f32(refs[0][...], refs[pairs][...], NT)
    for i in range(1, pairs):
        total = total + dot_f32(refs[i][...], refs[pairs + i][...], NT)
    refs[-1][...] = total.astype(BF)


def back_product(*pairs):
    total, wide = pairs[0][0].shape[0], pairs[0][1].shape[0]
    rows = 256
    lefts = [a for a, _ in pairs]
    rights = [b for _, b in pairs]
    return pl.pallas_call(
        functools.partial(back_kernel, len(pairs)),
        grid=(total // rows,),
        in_specs=[pl.BlockSpec((rows, a.shape[1]), lambda i: (i, 0)) for a in lefts]
        + [pl.BlockSpec(b.shape, lambda i: (0, 0)) for b in rights],
        out_specs=pl.BlockSpec((rows, wide), lambda i: (i, 0)),
        out_shape=shape_of(total, wide, dtype=BF),
        compiler_params=pltpu.CompilerParams(vmem_limit_bytes=VMEM_LIMIT),
        cost_estimate=pl.CostEstimate(
            flops=total * wide * 256, transcendentals=0, bytes_accessed=total * wide
        ),
        name="back_product",
    )(*lefts, *rights)


def pack_even(ranks, *arrays):
    rows = arrays[0].shape[0]
    wide = sum(a.shape[1] for a in arrays) // ranks
    return pl.pallas_call(
        functools.partial(pack_kernel, ranks),
        out_shape=shape_of(ranks * rows, wide, dtype=BF),
        compiler_params=pltpu.CompilerParams(vmem_limit_bytes=VMEM_LIMIT),
        name="pack_even",
    )(*arrays)


def unpack_even(ranks, packed, count):
    rows = packed.shape[0] // ranks
    size = packed.shape[1] // count
    return pl.pallas_call(
        functools.partial(unpack_kernel, ranks),
        out_shape=(shape_of(rows, ranks * size),) * count,
        compiler_params=pltpu.CompilerParams(vmem_limit_bytes=VMEM_LIMIT),
        name="unpack_even",
    )(packed)


def delta_forward(pre, small, rider, taps, const, hp, dk, dv):
    total, wide = pre.shape
    jobs = total // CHUNK * hp
    return pl.pallas_call(
        functools.partial(fwd_kernel, hp, dk, dv),
        out_shape=(
            shape_of(total, hp * dv),
            shape_of(jobs, dk, dv),
            shape_of(total, hp * dv),
            shape_of(jobs, CHUNK, CHUNK),
            shape_of(total, hp * dk),
        ),
        scratch_shapes=[
            pltpu.VMEM((total, wide), F32),
            pltpu.VMEM((total, LANES), F32),
            pltpu.VMEM((jobs, CHUNK, CHUNK), F32),
            pltpu.VMEM((hp, dk, dv), F32),
        ],
        compiler_params=pltpu.CompilerParams(vmem_limit_bytes=VMEM_LIMIT),
        cost_estimate=pl.CostEstimate(
            flops=total * hp * 21_000_000,
            transcendentals=total * hp * CHUNK,
            bytes_accessed=total * wide * 16,
        ),
        name="delta_forward",
    )(pre, small, rider, taps, const)


def delta_backward(pre, small, rider, taps, const, saved, d_mixed, gain, hp, dk, dv):
    total, wide = pre.shape
    jobs = total // CHUNK * hp
    return pl.pallas_call(
        functools.partial(bwd_kernel, hp, dk, dv),
        out_shape=(
            shape_of(total, wide + LANES, dtype=BF),
            shape_of(8, wide),
        ),
        scratch_shapes=[
            pltpu.VMEM((total, wide), F32),
            pltpu.VMEM((total + 8, LANES), F32),
            pltpu.VMEM((total, wide), F32),
            pltpu.VMEM((total + 8, wide), F32),
            pltpu.VMEM((total, LANES), F32),
            pltpu.VMEM((total, hp * dv), F32),
            pltpu.VMEM((jobs, dk, dv), F32),
            pltpu.VMEM((hp, dk, dv), F32),
        ],
        compiler_params=pltpu.CompilerParams(vmem_limit_bytes=VMEM_LIMIT),
        cost_estimate=pl.CostEstimate(
            flops=total * hp * 5_000_000,
            transcendentals=total * hp * CHUNK,
            bytes_accessed=total * wide * 20,
        ),
        name="delta_backward",
    )(pre, small, rider, taps, const, *saved, d_mixed, gain)


GATE_ROWS = 256


def gate_forward(mixed, gate, gain, hp, dv):
    total, wide = mixed.shape
    rows = min(GATE_ROWS, total)
    block = pl.BlockSpec((rows, wide), lambda i: (i, 0))
    return pl.pallas_call(
        functools.partial(gate_kernel, hp, dv),
        grid=(total // rows,),
        in_specs=[block, block, pl.BlockSpec((1, dv), lambda i: (0, 0))],
        out_specs=block,
        out_shape=shape_of(total, wide, dtype=BF),
        name="gate_forward",
    )(mixed, gate, gain)


def gate_backward(d_gated, mixed, gate, gain, hp, dv):
    total, wide = mixed.shape
    rows = min(GATE_ROWS, total)
    block = pl.BlockSpec((rows, wide), lambda i: (i, 0))
    return pl.pallas_call(
        functools.partial(gate_back_kernel, hp, dv),
        grid=(total // rows,),
        in_specs=[block, block, block, pl.BlockSpec((1, dv), lambda i: (0, 0))],
        out_specs=(block, block, pl.BlockSpec((8, dv), lambda i: (0, 0))),
        out_shape=(
            shape_of(total, wide),
            shape_of(total, wide, dtype=BF),
            shape_of(8, dv),
        ),
        name="gate_backward",
    )(d_gated, mixed, gate, gain)


def local(
    tokens,
    attn_gain,
    w_query,
    w_key,
    w_value,
    w_decay,
    w_beta,
    w_gate,
    w_out,
    conv_query,
    conv_key,
    conv_value,
    decay_log,
    decay_bias,
    out_gain,
    mlp_gain,
    w_hidden,
    w_up,
    w_down,
    offsets,
    cotangent,
):
    ranks = lax.axis_size("seq")
    rank = lax.axis_index("seq")
    heads = decay_log.shape[0]
    width = tokens.shape[-1]
    tok = tokens.shape[1]
    length = tok * ranks
    plan = Plan(ranks, heads, w_query.shape[1] // heads, out_gain.shape[0], w_hidden.shape[1])
    hp, vs, dk, dv, ff = plan.hp, plan.vs, plan.key_dim, plan.dv, plan.ff
    rows = w_query.shape[0]

    own_tokens = to_ring(tokens[0])
    own_cot = to_ring(cotangent[0])
    small = jnp.concatenate(
        [
            plan.split_keys(w_decay),
            plan.split_keys(w_beta),
            jnp.broadcast_to(attn_gain[:, None, None], (rows, ranks, 1)),
            jnp.broadcast_to(mlp_gain[:, None, None], (rows, ranks, 1)),
            jnp.zeros((rows, ranks, LANES - 2 - 2 * hp), BF),
        ],
        axis=2,
    )
    mix_pack = rank_major(
        jnp.concatenate(
            [
                plan.split_keys(w_query),
                plan.split_keys(w_key),
                plan.split_even(w_value),
                small,
            ],
            axis=2,
        )
    )
    side_pack = rank_major(
        jnp.concatenate([plan.split_even(w_gate), plan.split_even(w_out)], axis=2)
    )
    mlp_pack = pack_even(ranks, w_hidden, w_up, w_down)
    mix_own = exchange(mix_pack)
    row_offsets = gather_small(offsets.astype(F32))
    held = lax.optimization_barrier(
        (own_tokens, side_pack, mlp_pack, mix_own, row_offsets)
    )
    gathered = lax.all_gather(held[0], "seq", axis=0, tiled=True)
    side_own = exchange(held[1])
    mix_own, row_offsets = held[3], held[4]
    w_mix = gather_end(mix_own, gather_start(mix_own))
    mlp_own_cols = exchange(after(held[2], side_own, gathered))
    side_own = after(side_own, w_mix)
    side_near = gather_start(side_own)

    at_k = hp * dk
    at_v = 2 * hp * dk
    at_s = at_v + hp * dv
    attn_gain_full = w_mix[:, at_s + 2 * hp].astype(F32)
    mlp_gain_full = w_mix[:, at_s + 2 * hp + 1].astype(F32)

    tokens_all = gathered.astype(F32)
    normed_all = tokens_all * rms_scale(tokens_all)
    attn = (normed_all * attn_gain_full).astype(BF)
    pre = nn(attn, w_mix[:, :at_s]).astype(BF)
    pre_small = nn(attn, w_mix[:, at_s:])
    cot_all = lax.all_gather(after(own_cot, pre), "seq", axis=0, tiled=True)
    group = rank // vs
    taps_query = lax.dynamic_slice_in_dim(conv_query, group * hp * dk, hp * dk, 1)
    taps_key = lax.dynamic_slice_in_dim(conv_key, group * hp * dk, hp * dk, 1)
    taps_value = lax.dynamic_slice_in_dim(conv_value, rank * hp * dv, hp * dv, 1)
    own_log = lax.dynamic_slice_in_dim(decay_log, group * hp, hp, 0)
    own_bias = lax.dynamic_slice_in_dim(decay_bias, group * hp, hp, 0)
    own_gain = lax.dynamic_slice_in_dim(out_gain, (rank % vs) * dv, dv, 0)

    taps = jnp.concatenate([taps_query, taps_key, taps_value], axis=1)
    const = jnp.pad(jnp.stack([-jnp.exp(own_log), own_bias]), ((0, 0), (0, LANES - hp)))
    pre, pre_small = lax.optimization_barrier((pre, pre_small, side_own))[:2]
    rider_all = jnp.pad(row_offsets.reshape(length, 1), ((0, 0), (0, LANES - 1)))
    mixed, *saved = delta_forward(pre, pre_small, rider_all, taps, const, hp, dk, dv)
    mixed, *side_near = lax.optimization_barrier((mixed,) + tuple(side_near))
    w_side = gather_end(side_own, side_near)
    gate_cols = w_side[:, : hp * dv]
    out_cols = w_side[:, hp * dv :]
    mlp_near = gather_start(after(mlp_own_cols, w_side))
    pre_gate = nn(attn, gate_cols)

    def by_head(array):
        return array.reshape(length, hp, -1)

    def gate_apply(mixed_in, gate_in, gain_in):
        m = by_head(mixed_in)
        square = plan.value_sum(jnp.sum(m * m, axis=-1, keepdims=True))
        scale = lax.rsqrt(square / plan.value_dim + 1e-05)
        return (m * scale * gain_in * silu(by_head(gate_in))).reshape(length, -1)

    def gate_apply_back(d_out, mixed_in, gate_in, gain_in):
        d, mixed_in, gate_in = by_head(d_out), by_head(mixed_in), by_head(gate_in)
        square = plan.value_sum(jnp.sum(mixed_in * mixed_in, axis=-1, keepdims=True))
        scale = lax.rsqrt(square / plan.value_dim + 1e-05)
        m = mixed_in * scale
        through = d * silu(gate_in)
        em = through * gain_in
        mean = plan.value_sum(jnp.sum(em * m, axis=-1, keepdims=True)) / plan.value_dim
        d_mix = scale * (em - m * mean)
        d_gt = d * m * gain_in * silu_slope(gate_in)
        return (
            d_mix.reshape(length, -1),
            d_gt.reshape(length, -1).astype(BF),
            jnp.sum(through * m, axis=(0, 1)),
        )

    if vs == 1:
        gated = gate_forward(mixed, pre_gate, own_gain[None], hp, dv)
    else:
        gated = gate_apply(mixed, pre_gate, own_gain).astype(BF)
    gated = after(gated, mlp_own_cols, cot_all)
    branch = lax.psum_scatter(
        nt(gated, out_cols).astype(BF), "seq", scatter_dimension=0, tiled=True
    )
    inputs = own_tokens.astype(F32)
    middle = inputs + branch.astype(F32)
    r2 = rms_scale(middle)
    n2 = middle * r2
    near_and_cot = lax.optimization_barrier(
        ((n2 * mlp_gain_full).astype(BF), cot_all) + tuple(mlp_near)
    )
    mlp_own, cot_all, mlp_near = near_and_cot[0], near_and_cot[1], near_and_cot[2:]
    mlp_cols = gather_end(mlp_own_cols, mlp_near)
    mlp_all = lax.all_gather(mlp_own, "seq", axis=0, tiled=True)
    both_w = mlp_cols[:, : 2 * ff]
    down_w = mlp_cols[:, 2 * ff :]
    d_product = nn(cot_all, down_w)
    both_pre = nn(mlp_all, both_w)
    hidden_pre = both_pre[:, :ff]
    up_pre = both_pre[:, ff:]
    sh = silu(hidden_pre)
    product = (sh * up_pre).astype(BF)
    d_both = jnp.concatenate(
        [
            (d_product * up_pre * silu_slope(hidden_pre)).astype(BF),
            (d_product * sh).astype(BF),
        ],
        axis=1,
    )
    d_mlp = lax.psum_scatter(
        nt(d_both, both_w).astype(BF), "seq", scatter_dimension=0, tiled=True
    ).astype(F32)
    d_output = own_cot.astype(F32)
    e2 = d_mlp * mlp_gain_full
    d_middle = d_output + r2 * (e2 - n2 * jnp.mean(e2 * n2, axis=-1, keepdims=True))
    down_sum = RingGrad(cot_all, product, kernel=False)
    both_sum = RingGrad(mlp_all, d_both, kernel=False)
    mlp_part = nt(product, down_w).astype(BF)
    down_sum.second(mlp_part)
    both_sum.second(mlp_part)
    d_branch_own = after(d_middle.astype(BF), *both_sum.sums, *down_sum.sums)
    d_branch_all = lax.all_gather(d_branch_own, "seq", axis=0, tiled=True)
    mlp_mine = jnp.concatenate([both_sum.total(d_branch_own), down_sum.total(d_branch_own)], axis=1)
    mlp_rows = exchange(mlp_mine)
    d_branch_all = after(d_branch_all, mlp_mine)
    mlp_out = lax.psum_scatter(
        after(mlp_part, d_branch_all), "seq", scatter_dimension=0, tiled=True
    )

    d_gated = nn(d_branch_all, out_cols)
    if vs == 1:
        d_mixed, d_gate, gain_part = gate_backward(
            d_gated, mixed, pre_gate, own_gain[None], hp, dv
        )
    else:
        d_mixed, d_gate, gain_part = gate_apply_back(d_gated, mixed, pre_gate, own_gain)
        gain_part = jnp.pad(gain_part[None], ((0, 7), (0, 0)))
    side_sum = RingPair((attn, d_gate), (d_branch_all, gated))
    d_mixed = after(d_mixed, *side_sum.sent)
    d_pre, d_sums = delta_backward(
        pre, pre_small, rider_all, taps, const, saved, d_mixed, gain_part, hp, dk, dv
    )
    held = lax.optimization_barrier((d_pre, d_sums) + side_sum.near)
    d_pre, d_sums = held[:2]
    side_sum.near = held[2:]
    side_sum.second()
    d_sums = sum_dp(d_sums)
    held = lax.optimization_barrier((d_pre, d_sums, mlp_rows) + side_sum.sums)
    d_pre, d_sums, mlp_rows = held[:3]
    d_attn_part = back_product((d_pre, w_mix), (d_gate, gate_cols))
    d_attn = lax.psum_scatter(d_attn_part, "seq", scatter_dimension=0, tiled=True).astype(F32)
    mix_sum = RingGrad(attn, after(d_pre, d_attn_part))
    every = gather_small(after(d_sums, d_attn_part))
    mlp_out, every, *held = lax.optimization_barrier(
        (mlp_out, every) + side_sum.late + mix_sum.far
    )
    count = len(side_sum.late)
    side_sum.late, mix_sum.far = tuple(held[:count]), tuple(held[count:])
    mix_sum.second()
    side_mine = side_sum.total(*mix_sum.sums)
    side_rows = to_rows(side_mine, ranks)
    every = every.reshape(ranks, 8, -1)
    held = lax.optimization_barrier((mlp_rows, mlp_out, side_rows) + mix_sum.near)
    mlp_rows, mlp_out, side_rows = held[:3]
    mix_sum.near = held[3:]
    mix_rows = to_rows(mix_sum.total(), ranks)
    grad_hidden, grad_up, grad_down = unpack_even(ranks, mlp_rows, 3)

    output = from_ring((middle + mlp_out.astype(F32)).astype(BF))
    n = inputs * rms_scale(inputs)
    e = d_attn * attn_gain_full
    grad_tokens = from_ring(
        (d_middle + rms_scale(inputs) * (e - n * jnp.mean(e * n, axis=-1, keepdims=True))).astype(BF)
    )

    def per_head(part, lead):
        part = part.reshape(ranks // vs, vs, lead, -1).sum(axis=1)
        return jnp.transpose(part, (1, 0, 2)).reshape(lead, -1)

    every_taps = every[:, :KERNEL]
    grad_conv_value = jnp.transpose(every_taps[:, :, at_v:], (1, 0, 2)).reshape(KERNEL, -1)
    gain_sum = every[:, 6, :dv].reshape(ranks // vs, vs, dv).sum(axis=0).reshape(-1)
    grad_query = plan.join_keys(mix_rows[:, :, :at_k])
    grad_key = plan.join_keys(mix_rows[:, :, at_k:at_v])
    grad_value = plan.join_even(mix_rows[:, :, at_v:at_s])
    grad_decay = plan.join_keys(mix_rows[:, :, at_s : at_s + hp])
    grad_beta = plan.join_keys(mix_rows[:, :, at_s + hp : at_s + 2 * hp])
    grad_gate = plan.join_even(side_rows[:, :, : hp * dv])

    def gain_grad(gain, pairs):
        total = sum(jnp.sum(w.astype(F32) * g, axis=1) for w, g in pairs)
        return total / gain.astype(F32)

    return (
        output[None],
        grad_tokens[None],
        gain_grad(
            attn_gain,
            (
                (w_query, grad_query),
                (w_key, grad_key),
                (w_value, grad_value),
                (w_decay, grad_decay),
                (w_beta, grad_beta),
                (w_gate, grad_gate),
            ),
        ),
        grad_query,
        grad_key,
        grad_value,
        grad_decay,
        grad_beta,
        grad_gate,
        plan.join_even(side_rows[:, :, hp * dv :]),
        per_head(every_taps[:, :, :at_k], KERNEL),
        per_head(every_taps[:, :, at_k:at_v], KERNEL),
        grad_conv_value,
        per_head(every[:, 5, :hp], 1)[0],
        per_head(every[:, 4, :hp], 1)[0],
        gain_sum,
        gain_grad(mlp_gain, ((w_hidden, grad_hidden), (w_up, grad_up))),
        grad_hidden,
        grad_up,
        grad_down,
    )


def solution(mesh):
    flat = ("dp", "seq")
    tok_spec = P("dp", "seq", None)
    row_spec = P(flat, None)
    gain_spec = P(flat)
    in_specs = (
        (tok_spec, gain_spec)
        + (row_spec,) * 7
        + (P(),) * 6
        + (gain_spec,)
        + (row_spec,) * 3
        + (P("dp", "seq"), tok_spec)
    )
    out_specs = (
        (tok_spec, tok_spec, gain_spec)
        + (row_spec,) * 7
        + (P(),) * 6
        + (gain_spec,)
        + (row_spec,) * 3
    )
    return jax.shard_map(local, mesh=mesh, in_specs=in_specs, out_specs=out_specs, check_vma=False)
```

```python
import functools

import jax
import jax.numpy as jnp
from jax import lax
from jax.experimental import pallas as pl
from jax.experimental.pallas import tpu as pltpu
from jax.sharding import PartitionSpec as P

KERNEL = 4
LANES = 128
BF = jnp.bfloat16
F32 = jnp.float32
CHUNK = 128


def rms_scale(value):
    return lax.rsqrt(jnp.mean(value * value, axis=-1, keepdims=True) + 1e-05)


def dot_f32(left, right, dims):
    return lax.dot_general(left, right, (dims, ((), ())), preferred_element_type=F32)


def nn(left, right):
    return dot_f32(left, right, ((1,), (0,)))


def nt(left, right):
    return dot_f32(left, right, ((1,), (1,)))


def tn(left, right):
    return dot_f32(left, right, ((0,), (0,)))


def silu(value):
    return value * jax.nn.sigmoid(value)


def silu_slope(value):
    s = jax.nn.sigmoid(value)
    return s * (1.0 + value * (1.0 - s))


class Plan:
    def __init__(self, ranks, heads, key_dim, value_dim, hidden):
        self.ranks = ranks
        self.heads = heads
        self.key_dim = key_dim
        self.hp = max(1, heads // ranks)
        self.vs = max(1, ranks // heads)
        self.dv = value_dim // self.vs
        self.value_dim = value_dim
        self.ff = hidden // ranks

    def split_keys(self, array):
        rows = array.shape[0]
        grouped = array.reshape(rows, self.heads // self.hp, -1)
        return jnp.repeat(grouped, self.vs, axis=1) if self.vs > 1 else grouped

    def split_even(self, array):
        return array.reshape(array.shape[0], self.ranks, -1)

    def join_keys(self, array):
        ranks, rows, width = array.shape
        array = array.astype(F32)
        if self.vs > 1:
            array = array.reshape(ranks // self.vs, self.vs, rows, width).sum(axis=1)
        return jnp.transpose(array, (1, 0, 2)).reshape(rows, -1)

    def join_even(self, array):
        return jnp.transpose(array, (1, 0, 2)).reshape(array.shape[1], -1).astype(F32)

    def value_sum(self, array):
        step = 1
        while step < self.vs:
            pairs = [(i, i ^ step) for i in range(self.ranks)]
            array = array + lax.ppermute(array, "seq", pairs)
            step *= 2
        return array


def after(value, *earlier):
    return lax.optimization_barrier((value,) + earlier)[0]


def ring_order(count):
    return [0, 1, 3, 2] if count == 4 else list(range(count))


def ring_pairs(count):
    order = ring_order(count)
    right = [(order[i], order[(i + 1) % count]) for i in range(count)]
    return right, [(there, here) for here, there in right]


def ring_place():
    me = lax.axis_index("dp")
    return me ^ (me >> 1)


def swap_blocks(array):
    size = array.shape[1] // 4
    return jnp.concatenate(
        [array[:, : 2 * size], array[:, 3 * size :], array[:, 2 * size : 3 * size]], axis=1
    )


def to_ring(array):
    if lax.axis_size("dp") != 4:
        return array
    width = array.shape[1]
    turned = swap_blocks(array)
    twice = jnp.concatenate([turned, turned], axis=1)
    return lax.dynamic_slice_in_dim(twice, ring_place() * (width // 4), width, 1)


def from_ring(array):
    if lax.axis_size("dp") != 4:
        return array
    width = array.shape[1]
    twice = jnp.concatenate([array, array], axis=1)
    at = (4 - ring_place()) * (width // 4)
    return swap_blocks(lax.dynamic_slice_in_dim(twice, at, width, 1))


def gather_start(own):
    if lax.axis_size("dp") != 4:
        return ()
    right, left = ring_pairs(4)
    return lax.ppermute(own, "dp", right), lax.ppermute(own, "dp", left)


def gather_end(own, near):
    if lax.axis_size("dp") != 4:
        return lax.all_gather(own, "dp", axis=0, tiled=True)
    right, left = ring_pairs(4)
    half = own.shape[0] // 2
    from_left, from_right = near
    far_a = lax.ppermute(from_left[:half], "dp", right)
    far_b = lax.ppermute(from_right[half:], "dp", left)
    return jnp.concatenate([own, from_right, far_a, far_b, from_left])


class RingGrad:
    def __init__(self, left, right, kernel=True):
        self.ring = lax.axis_size("dp") == 4
        self.left, self.right, self.kernel = left, right, kernel
        rows = self.rows = left.shape[1] // lax.axis_size("dp")
        half = self.half = rows // 2
        self.sent, self.far, self.sums, self.near = (), (), (), ()
        if self.ring:
            to_right, to_left = ring_pairs(4)
            self.sent = self.products((2 * rows, half, ()), (2 * rows + half, half, ()))
            self.far = (
                lax.ppermute(self.sent[0], "dp", to_right),
                lax.ppermute(self.sent[1], "dp", to_left),
            )

    def products(self, *spans):
        if self.kernel:
            return tuple(grad_rows(self.left, self.right, spans))
        out = []
        for at, size, arrived in spans:
            total = tn(self.left[:, at : at + size], self.right)
            for array, row in arrived:
                rest = size - row - array.shape[0]
                total = total + jnp.pad(array.astype(F32), ((row, rest), (0, 0)))
            out.append(total.astype(BF))
        return tuple(out)

    def second(self, *earlier):
        if self.ring:
            to_right, to_left = ring_pairs(4)
            far_a, far_b = lax.optimization_barrier(self.far + earlier)[:2]
            rows, half = self.rows, self.half
            self.sums = self.products(
                (rows, rows, ((far_a, 0),)), (3 * rows, rows, ((far_b, half),))
            )
            self.near = (
                lax.ppermute(self.sums[0], "dp", to_right),
                lax.ppermute(self.sums[1], "dp", to_left),
            )

    def total(self, *earlier):
        if not self.ring:
            whole = tn(self.left, self.right).astype(BF)
            return lax.psum_scatter(whole, "dp", scatter_dimension=0, tiled=True)
        held = lax.optimization_barrier(self.near + earlier)
        return self.products((0, self.rows, ((held[0], 0), (held[1], 0))))[0]


class RingPair:
    def __init__(self, *pairs):
        self.ring = lax.axis_size("dp") == 4
        self.pairs = pairs
        rows = self.rows = pairs[0][0].shape[1] // lax.axis_size("dp")
        self.half = rows // 2
        self.sent, self.near, self.sums, self.late = (), (), (), ()
        if self.ring:
            to_right, to_left = ring_pairs(4)
            self.sent = self.blocks((4, 5, 3, 6))
            self.near = (
                lax.ppermute(self.sent[0], "dp", to_right),
                lax.ppermute(self.sent[1], "dp", to_left),
                lax.ppermute(self.sent[2], "dp", to_right),
                lax.ppermute(self.sent[3], "dp", to_left),
            )

    def blocks(self, which, *extra):
        return tuple(grad_blocks(self.half, which, self.pairs, *extra))

    def second(self, *earlier):
        if self.ring:
            to_right, to_left = ring_pairs(4)
            held = lax.optimization_barrier(self.near + earlier)
            far, self.near = held[:2], held[:4]
            self.sums = self.blocks((2, 7), far)
            self.late = (
                lax.ppermute(self.sums[0], "dp", to_right),
                lax.ppermute(self.sums[1], "dp", to_left),
            )

    def total(self, *earlier):
        if not self.ring:
            whole = jnp.concatenate([tn(a, b).astype(BF) for a, b in self.pairs], axis=1)
            return lax.psum_scatter(whole, "dp", scatter_dimension=0, tiled=True)
        held = lax.optimization_barrier(self.near[2:] + self.late + earlier)
        right_b, left_a, right_a, left_b = held[:4]
        return jnp.concatenate(self.blocks((0, 1), (right_a, right_b), (left_a, left_b)))


def rank_major(packed):
    return jnp.transpose(packed, (1, 0, 2)).reshape(-1, packed.shape[2])


def exchange(packed):
    return lax.all_to_all(packed, "seq", 0, 0, tiled=True)


def to_rows(mine, ranks):
    turned = lax.all_to_all(mine, "seq", 0, 0, tiled=True)
    return turned.reshape(ranks, -1, mine.shape[1])


def sum_dp(values):
    count = lax.axis_size("dp")
    if count & (count - 1):
        return lax.psum(values, "dp")
    step = 1
    while step < count:
        values = values + lax.ppermute(values, "dp", [(i, i ^ step) for i in range(count)])
        step *= 2
    return values


def gather_small(values):
    ranks = lax.axis_size("seq")
    if ranks & (ranks - 1):
        return lax.all_gather(values, "seq", axis=0, tiled=True)
    rank = lax.axis_index("seq")
    step = 1
    while step < ranks:
        other = lax.ppermute(values, "seq", [(i, i ^ step) for i in range(ranks)])
        upper = (rank & step) != 0
        values = jnp.concatenate(
            [jnp.where(upper, other, values), jnp.where(upper, values, other)]
        )
        step *= 2
    return values


class Pair:
    def __init__(self, value):
        self.value = value
        self.high = value.astype(BF)
        self.low = (value - self.high.astype(F32)).astype(BF)


def pair(value):
    return value if isinstance(value, Pair) else Pair(value)


NN = ((1,), (0,))
NT = ((1,), (1,))
TN = ((0,), (0,))


def dot(left, right, dims):
    a, b = pair(left), pair(right)
    return dot_f32(a.high, b.high, dims) + (
        dot_f32(a.high, b.low, dims) + dot_f32(a.low, b.high, dims)
    )


def stack(top, bottom):
    return jnp.concatenate([top, bottom], axis=0)


def grids(n):
    t = lax.broadcasted_iota(jnp.int32, (n, n), 0)
    s = lax.broadcasted_iota(jnp.int32, (n, n), 1)
    return t, s


def inverses(stricts, t, s):
    n = t.shape[0]
    eye = jnp.where(t == s, 1.0, 0.0).astype(F32)
    same = (t // 8) == (s // 8)
    small = [Pair(jnp.where(same, a, 0.0)) for a in stricts]
    square = [Pair(dot(a, a, NN)) for a in small]
    fourth = [dot(a, a, NN) for a in square]
    first = [eye - a.value for a in small]
    inv = [f + dot(f, a, NN) for f, a in zip(first, square)]
    inv = [f + dot(f, a, NN) for f, a in zip(inv, fourth)]
    size = 8
    while size < n:
        take = ((t // (2 * size)) == (s // (2 * size))) & ((t // size) != (s // size))
        held = [Pair(f) for f in inv]
        part = [dot(f, jnp.where(take, a, 0.0), NN) for f, a in zip(held, stricts)]
        inv = [f.value - dot(p, f, NN) for f, p in zip(held, part)]
        size *= 2
    return inv


def decays(cols, hp, t, s):
    n = t.shape[0]
    tri = jnp.where(t >= s, 1.0, 0.0).astype(F32)
    run = dot(tri, cols, NN)
    turned = jnp.transpose(run)
    offs = cols[:, 2 * hp : 2 * hp + 1]
    row = t[:, :1].astype(F32)
    gap = (t - s).astype(F32)
    same = (gap >= 0.0) & (offs >= gap)
    keep = offs[n - 1 : n, :] >= (n - 1.0) - row
    out = []
    for h in range(hp):
        g = run[:, h : h + 1]
        g_row = turned[h : h + 1, :]
        pairwise = jnp.where(same, jnp.exp(jnp.where(same, g - g_row, 0.0)), 0.0)
        start = jnp.where(offs > row, jnp.exp(g), 0.0)
        end = jnp.where(keep, jnp.exp(jnp.where(keep, g[n - 1 : n, :] - g, 0.0)), 0.0)
        out.append((pairwise, start, end, start[n - 1 : n, :], cols[:, hp + h : hp + h + 1]))
    return out


def lanes_of(hp, dk, dv):
    q = [slice(h * dk, (h + 1) * dk) for h in range(hp)]
    k = [slice((hp + h) * dk, (hp + h + 1) * dk) for h in range(hp)]
    v = [slice(2 * hp * dk + h * dv, 2 * hp * dk + (h + 1) * dv) for h in range(hp)]
    return q, k, v


def chunk_rows(c):
    return pl.ds(pl.multiple_of(c * CHUNK, CHUNK), CHUNK)


def chunk_cols(hp, rows, small_ref, rider_ref, const_ref):
    lane = lax.broadcasted_iota(jnp.int32, (CHUNK, LANES), 1)
    x = small_ref[rows, :]
    y = x + const_ref[1:2, :]
    logs = const_ref[0:1, :] * (jnp.maximum(y, 0.0) + jnp.log1p(jnp.exp(-jnp.abs(y))))
    beta = jax.nn.sigmoid(x)
    offs = rider_ref[rows, 0:1]
    cols = jnp.where(lane < hp, logs, jnp.where(lane < 2 * hp, beta, 0.0))
    return jnp.where(lane == 2 * hp, offs, cols), offs


def conved_lanes(c, lanes, offs, pre_ref, taps_ref):
    rows = chunk_rows(c)
    above = pl.ds(pl.multiple_of(jnp.maximum(c * CHUNK - 16, 0), 16), 16)
    block = pre_ref[rows, lanes].astype(F32)
    ext = stack(pre_ref[above, lanes].astype(F32), block)
    total = taps_ref[0:1, lanes] * block
    for by in range(1, KERNEL):
        moved = pltpu.roll(ext, by, 0)[16:]
        total = total + taps_ref[by : by + 1, lanes] * jnp.where(offs >= by, moved, 0.0)
    return total


def unit_scale(u):
    return lax.rsqrt(jnp.sum(u * u, axis=1, keepdims=True) + 1e-06)


def fill_front(hp, dk, dv, c, pre_ref, small_ref, rider_ref, taps_ref, const_ref, qkv_ref, cols_ref, conv_ref):
    rows = chunk_rows(c)
    cols, offs = chunk_cols(hp, rows, small_ref, rider_ref, const_ref)
    cols_ref[rows, :] = cols
    for kind, slices in enumerate(lanes_of(hp, dk, dv)):
        for lanes in slices:
            conved = conved_lanes(c, lanes, offs, pre_ref, taps_ref)
            if conv_ref is not None:
                conv_ref[rows, lanes] = conved
            u = conved * jax.nn.sigmoid(conved)
            if kind == 0:
                u = u * (unit_scale(u) * dk ** (-0.5))
            elif kind == 1:
                u = u * unit_scale(u)
            qkv_ref[rows, lanes] = u


def fwd_kernel(
    hp, dk, dv, pre_ref, small_ref, rider_ref, taps_ref, const_ref,
    mixed_ref, state_ref, upd_ref, inv_ref, seen_ref,
    qkv_ref, cols_ref, p_ref, cur_ref,
):
    n = CHUNK
    chunks = pre_ref.shape[0] // n
    group = 2 if chunks % 2 == 0 else 1
    t, s = grids(n)
    q_at, k_at, v_at = lanes_of(hp, dk, dv)

    def prepare(step, carry):
        jobs = []
        for j in range(group):
            c = step * group + j
            fill_front(
                hp, dk, dv, c, pre_ref, small_ref, rider_ref, taps_ref, const_ref, qkv_ref, cols_ref, None
            )
            rows = chunk_rows(c)
            for h, d in enumerate(decays(cols_ref[rows, :], hp, t, s)):
                jobs.append((c, rows, h) + d)
        keys = [qkv_ref[r, k_at[h]] for _, r, h, *_ in jobs]
        both = [dot(stack(k, qkv_ref[job[1], q_at[job[2]]]), k, NT) for k, job in zip(keys, jobs)]
        strict = [jnp.where(t > s, job[3] * b[:n], 0.0) * job[7] for job, b in zip(jobs, both)]
        inv = [Pair(i) for i in inverses(strict, t, s)]
        for job, b, i, k in zip(jobs, both, inv, keys):
            c, r, h, pairwise, start, end, last, beta = job
            p_ref[c * hp + h] = pairwise * b[n:]
            inv_ref[c * hp + h] = i.value
            upd_ref[r, h * dv : (h + 1) * dv] = dot(i, beta * qkv_ref[r, v_at[h]], NN)
            seen_ref[r, h * dk : (h + 1) * dk] = dot(i, (beta * start) * k, NN)
        return carry

    lax.fori_loop(0, chunks // group, prepare, 0)
    cur_ref[...] = jnp.zeros_like(cur_ref)

    def advance(c, carry):
        rows = chunk_rows(c)
        for h, (pairwise, start, end, last, beta) in enumerate(decays(cols_ref[rows, :], hp, t, s)):
            vv = slice(h * dv, (h + 1) * dv)
            state = cur_ref[h]
            state_ref[c * hp + h] = state
            seen = seen_ref[rows, h * dk : (h + 1) * dk]
            both = dot(stack(seen, qkv_ref[rows, q_at[h]] * start), state, NN)
            update = Pair(upd_ref[rows, vv] - both[:n])
            upd_ref[rows, vv] = update.value
            mixed_ref[rows, vv] = both[n:] + dot(p_ref[c * hp + h], update, NN)
            cur_ref[h] = last * state + dot(qkv_ref[rows, k_at[h]] * end, update, TN)
        return carry

    lax.fori_loop(0, chunks, advance, 0)


def bwd_kernel(
    hp, dk, dv, pre_ref, small_ref, rider_ref, taps_ref, const_ref,
    state_ref, upd_ref, inv_ref, seen_ref, dm_ref, gain_ref,
    dpre_ref, dtaps_ref,
    qkv_ref, cols_ref, conv_ref, dcon_ref, dcols_ref, du_ref, ds_ref, cur_ref,
):
    n = CHUNK
    total = pre_ref.shape[0]
    chunks = total // n
    t, s = grids(n)
    q_at, k_at, v_at = lanes_of(hp, dk, dv)
    wide = 2 * hp * dk + hp * dv
    cur_ref[...] = jnp.zeros_like(cur_ref)
    dtaps_ref[...] = jnp.zeros_like(dtaps_ref)
    dtaps_ref[6:7, : gain_ref.shape[1]] = gain_ref[0:1, :]
    dcon_ref[total:, :] = jnp.zeros((dcon_ref.shape[0] - total, wide), F32)
    cols_ref[total:, :] = jnp.zeros((cols_ref.shape[0] - total, LANES), F32)

    def retreat(step, carry):
        c = chunks - 1 - step
        rows = chunk_rows(c)
        fill_front(
            hp, dk, dv, c, pre_ref, small_ref, rider_ref, taps_ref, const_ref, qkv_ref, cols_ref, conv_ref
        )
        for h, (pairwise, start, end, last, beta) in enumerate(decays(cols_ref[rows, :], hp, t, s)):
            vv = slice(h * dv, (h + 1) * dv)
            d_state = cur_ref[h]
            ds_ref[c * hp + h] = d_state
            dm = Pair(dm_ref[rows, vv])
            q, k = qkv_ref[rows, q_at[h]], qkv_ref[rows, k_at[h]]
            p = pairwise * dot(q, k, NT)
            du = dot(p, dm, TN) + dot(k * end, d_state, NN)
            du_ref[rows, vv] = du
            seen = seen_ref[rows, h * dk : (h + 1) * dk]
            cur_ref[h] = last * d_state + dot(q * start, dm, TN) - dot(seen, du, TN)
        return carry

    lax.fori_loop(0, chunks, retreat, 0)
    lane = lax.broadcasted_iota(jnp.int32, (n, LANES), 1)

    def through_silu(rows, lanes, dy, unit):
        conved = conv_ref[rows, lanes]
        sig = jax.nn.sigmoid(conved)
        if unit:
            u = conved * sig
            scale = unit_scale(u)
            dy = scale * dy - (scale * scale * scale) * u * jnp.sum(u * dy, axis=1, keepdims=True)
        dcon_ref[rows, lanes] = dy * (sig * (1.0 + conved * (1.0 - sig)))

    def finish(c, carry):
        rows = chunk_rows(c)
        d_cols = jnp.zeros((n, LANES), F32)
        for h, (pairwise, start, end, last, beta) in enumerate(decays(cols_ref[rows, :], hp, t, s)):
            vv = slice(h * dv, (h + 1) * dv)
            q, k, v = qkv_ref[rows, q_at[h]], qkv_ref[rows, k_at[h]], qkv_ref[rows, v_at[h]]
            dm = dm_ref[rows, vv]
            q_p, k_p, u_p = Pair(q), Pair(k), Pair(upd_ref[rows, vv])
            state = Pair(state_ref[c * hp + h])
            d_state = Pair(ds_ref[c * hp + h])
            w = dot(inv_ref[c * hp + h], du_ref[rows, vv], TN)
            scores = dot(stack(w, dm), u_p, NT)
            d_a = jnp.where(t > s, -scores[:n], 0.0)
            d_p = scores[n:]
            keys = dot(stack(k, q), k_p, NT)
            met = dot(stack(k, q), state, NN)
            r, qs = met[:n], met[n:]
            back = dot(stack(start * dm, -(beta * start) * w), state, NT)
            x = dot(u_p, d_state, NT)
            d_qk = pairwise * d_p
            d_kk = beta * (pairwise * d_a)
            d_query = back[:n] + dot(d_qk, k_p, NN)
            d_key = (
                back[n:]
                + dot(d_qk, q_p, TN)
                + dot(d_kk + jnp.transpose(d_kk), k_p, NN)
                + end * x
            )
            through_silu(rows, q_at[h], d_query * dk ** (-0.5), True)
            through_silu(rows, k_at[h], d_key, True)
            through_silu(rows, v_at[h], beta * w, False)
            inner = pairwise * d_a * keys[:n]
            d_beta = jnp.sum(w * (v - start * r), axis=1, keepdims=True) + jnp.sum(
                inner, axis=1, keepdims=True
            )
            d_start = jnp.sum(dm * qs, axis=1, keepdims=True) - beta * jnp.sum(
                w * r, axis=1, keepdims=True
            )
            e = pairwise * d_p * keys[n:] + beta * inner
            d_end = end * jnp.sum(k * x, axis=1, keepdims=True)
            d_g = (
                jnp.sum(e, axis=1, keepdims=True)
                - jnp.sum(jnp.transpose(e), axis=1, keepdims=True)
                + d_start * start
                - d_end
            )
            held = jnp.sum(
                jnp.sum(state.value * d_state.value, axis=1, keepdims=True), axis=0, keepdims=True
            )
            tail = jnp.sum(d_end, axis=0, keepdims=True) + last * held
            d_g = d_g + jnp.where(t[:, :1] == n - 1, tail, 0.0)
            d_cols = jnp.where(lane == h, d_g, d_cols)
            d_cols = jnp.where(lane == hp + h, d_beta, d_cols)
        tri = jnp.where(t >= s, 1.0, 0.0).astype(F32)
        dcols_ref[rows, :] = jnp.where(lane < hp, dot(tri, d_cols, TN), d_cols)
        return carry

    lax.fori_loop(0, chunks, finish, 0)

    def spread(c, carry):
        rows = chunk_rows(c)
        below = pl.ds(pl.multiple_of((c + 1) * n, n), 8)
        cols = cols_ref[rows, :]
        offs = cols[:, 2 * hp : 2 * hp + 1]
        offs_below = cols_ref[below, 2 * hp : 2 * hp + 1]
        for slices in (q_at, k_at, v_at):
            for lanes in slices:
                pre = pre_ref[rows, lanes].astype(F32)
                d_con = dcon_ref[rows, lanes]
                d_below = dcon_ref[below, lanes]
                out = taps_ref[0:1, lanes] * d_con
                dtaps_ref[0:1, lanes] += jnp.sum(pre * d_con, axis=0, keepdims=True)
                for by in range(1, KERNEL):
                    ext = stack(
                        jnp.where(offs >= by, d_con, 0.0), jnp.where(offs_below >= by, d_below, 0.0)
                    )
                    moved = pltpu.roll(ext, n + 8 - by, 0)[:n]
                    out = out + taps_ref[by : by + 1, lanes] * moved
                    dtaps_ref[by : by + 1, lanes] += jnp.sum(pre * moved, axis=0, keepdims=True)
                dpre_ref[rows, lanes] = out.astype(BF)
        d_cols = dcols_ref[rows, :]
        slope = const_ref[0:1, :] * jax.nn.sigmoid(small_ref[rows, :] + const_ref[1:2, :])
        d_small = jnp.where(lane < hp, d_cols * slope, d_cols * cols * (1.0 - cols))
        d_small = jnp.where(lane < 2 * hp, d_small, 0.0)
        dpre_ref[rows, wide:] = d_small.astype(BF)
        dtaps_ref[4:5, :LANES] += jnp.sum(d_small, axis=0, keepdims=True)
        dtaps_ref[5:6, :LANES] += jnp.sum(d_cols * cols, axis=0, keepdims=True)
        return carry

    lax.fori_loop(0, chunks, spread, 0)


def gate_kernel(hp, dv, mixed_ref, gate_ref, gain_ref, out_ref):
    for h in range(hp):
        at = slice(h * dv, (h + 1) * dv)
        mixed = mixed_ref[:, at]
        scale = lax.rsqrt(jnp.mean(mixed * mixed, axis=1, keepdims=True) + 1e-05)
        gate = gate_ref[:, at]
        out_ref[:, at] = (mixed * scale * gain_ref[0:1, :] * (gate * jax.nn.sigmoid(gate))).astype(BF)


def gate_back_kernel(hp, dv, d_ref, mixed_ref, gate_ref, gain_ref, dm_ref, dgate_ref, dgain_ref):
    @pl.when(pl.program_id(0) == 0)
    def _():
        dgain_ref[...] = jnp.zeros_like(dgain_ref)

    gain = gain_ref[0:1, :]
    for h in range(hp):
        at = slice(h * dv, (h + 1) * dv)
        mixed = mixed_ref[:, at]
        scale = lax.rsqrt(jnp.mean(mixed * mixed, axis=1, keepdims=True) + 1e-05)
        m = mixed * scale
        gate = gate_ref[:, at]
        sig = jax.nn.sigmoid(gate)
        through = d_ref[:, at] * (gate * sig)
        dgain_ref[0:1, :] += jnp.sum(through * m, axis=0, keepdims=True)
        em = through * gain
        dm_ref[:, at] = scale * (em - m * jnp.mean(em * m, axis=1, keepdims=True))
        slope = sig * (1.0 + gate * (1.0 - sig))
        dgate_ref[:, at] = (d_ref[:, at] * m * gain * slope).astype(BF)


def pack_kernel(ranks, *refs):
    *ins, out_ref = refs
    rows = ins[0].shape[0]
    parts = [ref[...].astype(F32) for ref in ins]
    for r in range(ranks):
        pieces = [p[:, r * (p.shape[1] // ranks) : (r + 1) * (p.shape[1] // ranks)] for p in parts]
        out_ref[r * rows : (r + 1) * rows, :] = jnp.concatenate(pieces, axis=1).astype(BF)


def mix_pack_kernel(ranks, hp, vs, q_ref, k_ref, v_ref, decay_ref, beta_ref, gain_ref, out_ref):
    rows = q_ref.shape[0]
    groups = ranks // vs
    k_wide, v_wide = q_ref.shape[1] // groups, v_ref.shape[1] // ranks
    lane = lax.broadcasted_iota(jnp.int32, (rows, LANES), 1)
    decay, beta = decay_ref[...].astype(F32), beta_ref[...].astype(F32)
    gain = gain_ref[...].astype(F32)
    for r in range(ranks):
        at, g = slice(r * rows, (r + 1) * rows), r // vs
        out_ref[at, :k_wide] = q_ref[:, g * k_wide : (g + 1) * k_wide]
        out_ref[at, k_wide : 2 * k_wide] = k_ref[:, g * k_wide : (g + 1) * k_wide]
        out_ref[at, 2 * k_wide : 2 * k_wide + v_wide] = v_ref[:, r * v_wide : (r + 1) * v_wide]
        small = jnp.zeros((rows, LANES), F32)
        for j in range(hp):
            small = jnp.where(lane == j, decay[:, g * hp + j : g * hp + j + 1], small)
            small = jnp.where(lane == hp + j, beta[:, g * hp + j : g * hp + j + 1], small)
        small = jnp.where(lane == 2 * hp, gain[:, 0:1], small)
        small = jnp.where(lane == 2 * hp + 1, gain[:, 1:2], small)
        out_ref[at, 2 * k_wide + v_wide :] = small.astype(BF)


def unpack_kernel(ranks, in_ref, *outs):
    rows = outs[0].shape[0]
    for i, out_ref in enumerate(outs):
        size = out_ref.shape[1] // ranks
        pieces = [
            in_ref[r * rows : (r + 1) * rows, :].astype(F32)[:, i * size : (i + 1) * size]
            for r in range(ranks)
        ]
        out_ref[...] = jnp.concatenate(pieces, axis=1)


def grad_kernel(spans, left_ref, right_ref, *refs):
    adds, outs = refs[: -len(spans)], refs[-len(spans) :]
    taken = 0
    for (at, size, places), out_ref in zip(spans, outs):
        for row in range(0, size, 256):
            high = min(256, size - row)
            piece = dot_f32(left_ref[:, at + row : at + row + high], right_ref[...], TN)
            for k, (first, rows) in enumerate(places):
                if first <= row < first + rows:
                    piece = piece + adds[taken + k][row - first : row - first + high, :].astype(F32)
            out_ref[row : row + high, :] = piece.astype(BF)
        taken += len(places)


def block_kernel(half, blocks, pairs, extra, *refs):
    lefts, rights = refs[:pairs], refs[pairs : 2 * pairs]
    adds, outs = refs[2 * pairs : -len(blocks)], refs[-len(blocks) :]
    for i, block in enumerate(blocks):
        lane = 0
        for left_ref, right_ref in zip(lefts, rights):
            wide = right_ref.shape[1]
            at = slice(lane, lane + wide)
            piece = dot_f32(left_ref[:, block * half : (block + 1) * half], right_ref[...], TN)
            for k in range(extra):
                piece = piece + adds[k * len(blocks) + i][:, at].astype(F32)
            outs[i][:, at] = piece.astype(BF)
            lane += wide


VMEM_LIMIT = 60 * 2**20


def shape_of(*dims, dtype=F32):
    return jax.ShapeDtypeStruct(dims, dtype)


def grad_rows(left, right, spans):
    wide = right.shape[1]
    rows = sum(size for _, size, _ in spans)
    fixed = tuple(
        (at, size, tuple((row, x.shape[0]) for x, row in arrived)) for at, size, arrived in spans
    )
    return pl.pallas_call(
        functools.partial(grad_kernel, fixed),
        out_shape=tuple(shape_of(size, wide, dtype=BF) for _, size, _ in spans),
        compiler_params=pltpu.CompilerParams(vmem_limit_bytes=VMEM_LIMIT),
        cost_estimate=pl.CostEstimate(
            flops=2 * rows * wide * left.shape[0],
            transcendentals=0,
            bytes_accessed=2 * (left.size + right.size + rows * wide),
        ),
        name="grad_rows",
    )(left, right, *(x for _, _, arrived in spans for x, _ in arrived))


def grad_blocks(half, blocks, pairs, *extra):
    wide = sum(b.shape[1] for _, b in pairs)
    arrays = [a for a, _ in pairs] + [b for _, b in pairs] + [x for xs in extra for x in xs]
    return pl.pallas_call(
        functools.partial(block_kernel, half, blocks, len(pairs), len(extra)),
        out_shape=(shape_of(half, wide, dtype=BF),) * len(blocks),
        compiler_params=pltpu.CompilerParams(vmem_limit_bytes=VMEM_LIMIT),
        cost_estimate=pl.CostEstimate(
            flops=half * len(blocks) * wide * pairs[0][0].shape[0] // 8,
            transcendentals=0,
            bytes_accessed=half * len(blocks) * wide,
        ),
        name="grad_blocks",
    )(*arrays)


def back_kernel(pairs, *refs):
    total = dot_f32(refs[0][...], refs[pairs][...], NT)
    for i in range(1, pairs):
        total = total + dot_f32(refs[i][...], refs[pairs + i][...], NT)
    refs[-1][...] = total.astype(BF)


def column_block(at):
    return lambda i: (0, at)


def back_product(*terms):
    total, wide = terms[0][0].shape[0], terms[0][1].shape[0]
    rows = 256
    return pl.pallas_call(
        functools.partial(back_kernel, len(terms)),
        grid=(total // rows,),
        in_specs=[pl.BlockSpec((rows, a.shape[1]), lambda i: (i, 0)) for a, _, _ in terms]
        + [pl.BlockSpec((wide, a.shape[1]), column_block(at)) for a, _, at in terms],
        out_specs=pl.BlockSpec((rows, wide), lambda i: (i, 0)),
        out_shape=shape_of(total, wide, dtype=BF),
        compiler_params=pltpu.CompilerParams(vmem_limit_bytes=VMEM_LIMIT),
        cost_estimate=pl.CostEstimate(
            flops=total * wide * 256, transcendentals=0, bytes_accessed=total * wide
        ),
        name="back_product",
    )(*(a for a, _, _ in terms), *(b for _, b, _ in terms))


def pack_even(ranks, *arrays):
    rows = arrays[0].shape[0]
    wide = sum(a.shape[1] for a in arrays) // ranks
    return pl.pallas_call(
        functools.partial(pack_kernel, ranks),
        out_shape=shape_of(ranks * rows, wide, dtype=BF),
        compiler_params=pltpu.CompilerParams(vmem_limit_bytes=VMEM_LIMIT),
        name="pack_even",
    )(*arrays)


def pack_mix(ranks, hp, vs, w_query, w_key, w_value, *smalls):
    rows = w_query.shape[0]
    wide = 2 * w_query.shape[1] * vs // ranks + w_value.shape[1] // ranks + LANES
    return pl.pallas_call(
        functools.partial(mix_pack_kernel, ranks, hp, vs),
        out_shape=shape_of(ranks * rows, wide, dtype=BF),
        compiler_params=pltpu.CompilerParams(vmem_limit_bytes=VMEM_LIMIT),
        name="pack_mix",
    )(w_query, w_key, w_value, *smalls)


def unpack_even(ranks, packed, count):
    rows = packed.shape[0] // ranks
    size = packed.shape[1] // count
    return pl.pallas_call(
        functools.partial(unpack_kernel, ranks),
        out_shape=(shape_of(rows, ranks * size),) * count,
        compiler_params=pltpu.CompilerParams(vmem_limit_bytes=VMEM_LIMIT),
        name="unpack_even",
    )(packed)


def delta_forward(pre, small, rider, taps, const, hp, dk, dv):
    total, wide = pre.shape
    jobs = total // CHUNK * hp
    return pl.pallas_call(
        functools.partial(fwd_kernel, hp, dk, dv),
        out_shape=(
            shape_of(total, hp * dv),
            shape_of(jobs, dk, dv),
            shape_of(total, hp * dv),
            shape_of(jobs, CHUNK, CHUNK),
            shape_of(total, hp * dk),
        ),
        scratch_shapes=[
            pltpu.VMEM((total, wide), F32),
            pltpu.VMEM((total, LANES), F32),
            pltpu.VMEM((jobs, CHUNK, CHUNK), F32),
            pltpu.VMEM((hp, dk, dv), F32),
        ],
        compiler_params=pltpu.CompilerParams(vmem_limit_bytes=VMEM_LIMIT),
        cost_estimate=pl.CostEstimate(
            flops=total * hp * 21_000_000,
            transcendentals=total * hp * CHUNK,
            bytes_accessed=total * wide * 16,
        ),
        name="delta_forward",
    )(pre, small, rider, taps, const)


def delta_backward(pre, small, rider, taps, const, saved, d_mixed, gain, hp, dk, dv):
    total, wide = pre.shape
    jobs = total // CHUNK * hp
    return pl.pallas_call(
        functools.partial(bwd_kernel, hp, dk, dv),
        out_shape=(
            shape_of(total, wide + LANES, dtype=BF),
            shape_of(8, wide),
        ),
        scratch_shapes=[
            pltpu.VMEM((total, wide), F32),
            pltpu.VMEM((total + 8, LANES), F32),
            pltpu.VMEM((total, wide), F32),
            pltpu.VMEM((total + 8, wide), F32),
            pltpu.VMEM((total, LANES), F32),
            pltpu.VMEM((total, hp * dv), F32),
            pltpu.VMEM((jobs, dk, dv), F32),
            pltpu.VMEM((hp, dk, dv), F32),
        ],
        compiler_params=pltpu.CompilerParams(vmem_limit_bytes=VMEM_LIMIT),
        cost_estimate=pl.CostEstimate(
            flops=total * hp * 5_000_000,
            transcendentals=total * hp * CHUNK,
            bytes_accessed=total * wide * 20,
        ),
        name="delta_backward",
    )(pre, small, rider, taps, const, *saved, d_mixed, gain)


GATE_ROWS = 256


def gate_forward(mixed, gate, gain, hp, dv):
    total, wide = mixed.shape
    rows = min(GATE_ROWS, total)
    block = pl.BlockSpec((rows, wide), lambda i: (i, 0))
    return pl.pallas_call(
        functools.partial(gate_kernel, hp, dv),
        grid=(total // rows,),
        in_specs=[block, block, pl.BlockSpec((1, dv), lambda i: (0, 0))],
        out_specs=block,
        out_shape=shape_of(total, wide, dtype=BF),
        name="gate_forward",
    )(mixed, gate, gain)


def gate_backward(d_gated, mixed, gate, gain, hp, dv):
    total, wide = mixed.shape
    rows = min(GATE_ROWS, total)
    block = pl.BlockSpec((rows, wide), lambda i: (i, 0))
    return pl.pallas_call(
        functools.partial(gate_back_kernel, hp, dv),
        grid=(total // rows,),
        in_specs=[block, block, block, pl.BlockSpec((1, dv), lambda i: (0, 0))],
        out_specs=(block, block, pl.BlockSpec((8, dv), lambda i: (0, 0))),
        out_shape=(
            shape_of(total, wide),
            shape_of(total, wide, dtype=BF),
            shape_of(8, dv),
        ),
        name="gate_backward",
    )(d_gated, mixed, gate, gain)


def local(
    tokens,
    attn_gain,
    w_query,
    w_key,
    w_value,
    w_decay,
    w_beta,
    w_gate,
    w_out,
    conv_query,
    conv_key,
    conv_value,
    decay_log,
    decay_bias,
    out_gain,
    mlp_gain,
    w_hidden,
    w_up,
    w_down,
    offsets,
    cotangent,
):
    ranks = lax.axis_size("seq")
    rank = lax.axis_index("seq")
    heads = decay_log.shape[0]
    width = tokens.shape[-1]
    tok = tokens.shape[1]
    length = tok * ranks
    plan = Plan(ranks, heads, w_query.shape[1] // heads, out_gain.shape[0], w_hidden.shape[1])
    hp, vs, dk, dv, ff = plan.hp, plan.vs, plan.key_dim, plan.dv, plan.ff
    rows = w_query.shape[0]

    own_tokens = to_ring(tokens[0])
    own_cot = to_ring(cotangent[0])
    gains = jnp.stack([attn_gain, mlp_gain], axis=1)
    mix_pack = pack_mix(ranks, hp, vs, w_query, w_key, w_value, w_decay, w_beta, gains)
    side_pack = rank_major(
        jnp.concatenate([plan.split_even(w_gate), plan.split_even(w_out)], axis=2)
    )
    mlp_pack = pack_even(ranks, w_hidden, w_up, w_down)
    mix_own = exchange(mix_pack)
    row_offsets = gather_small(offsets.astype(F32))
    held = lax.optimization_barrier(
        (own_tokens, side_pack, mlp_pack, mix_own, row_offsets)
    )
    gathered = lax.all_gather(held[0], "seq", axis=0, tiled=True)
    side_own = exchange(held[1])
    mix_own, row_offsets = held[3], held[4]
    w_mix = gather_end(mix_own, gather_start(mix_own))
    mlp_own_cols = exchange(after(held[2], side_own, gathered))
    side_own = after(side_own, w_mix)
    side_near = gather_start(side_own)

    at_k = hp * dk
    at_v = 2 * hp * dk
    at_s = at_v + hp * dv
    attn_gain_full = w_mix[:, at_s + 2 * hp].astype(F32)
    mlp_gain_full = w_mix[:, at_s + 2 * hp + 1].astype(F32)

    tokens_all = gathered.astype(F32)
    normed_all = tokens_all * rms_scale(tokens_all)
    attn = (normed_all * attn_gain_full).astype(BF)
    pre = nn(attn, w_mix[:, :at_s]).astype(BF)
    pre_small = nn(attn, w_mix[:, at_s:])
    cot_all = lax.all_gather(after(own_cot, pre), "seq", axis=0, tiled=True)
    group = rank // vs
    taps_query = lax.dynamic_slice_in_dim(conv_query, group * hp * dk, hp * dk, 1)
    taps_key = lax.dynamic_slice_in_dim(conv_key, group * hp * dk, hp * dk, 1)
    taps_value = lax.dynamic_slice_in_dim(conv_value, rank * hp * dv, hp * dv, 1)
    own_log = lax.dynamic_slice_in_dim(decay_log, group * hp, hp, 0)
    own_bias = lax.dynamic_slice_in_dim(decay_bias, group * hp, hp, 0)
    own_gain = lax.dynamic_slice_in_dim(out_gain, (rank % vs) * dv, dv, 0)

    taps = jnp.concatenate([taps_query, taps_key, taps_value], axis=1)
    const = jnp.pad(jnp.stack([-jnp.exp(own_log), own_bias]), ((0, 0), (0, LANES - hp)))
    pre, pre_small = lax.optimization_barrier((pre, pre_small, side_own))[:2]
    rider_all = jnp.pad(row_offsets.reshape(length, 1), ((0, 0), (0, LANES - 1)))
    mixed, *saved = delta_forward(pre, pre_small, rider_all, taps, const, hp, dk, dv)
    mixed, *side_near = lax.optimization_barrier((mixed,) + tuple(side_near))
    w_side = gather_end(side_own, side_near)
    gate_cols = w_side[:, : hp * dv]
    out_cols = w_side[:, hp * dv :]
    mlp_near = gather_start(after(mlp_own_cols, w_side))
    pre_gate = nn(attn, gate_cols)

    def by_head(array):
        return array.reshape(length, hp, -1)

    def gate_apply(mixed_in, gate_in, gain_in):
        m = by_head(mixed_in)
        square = plan.value_sum(jnp.sum(m * m, axis=-1, keepdims=True))
        scale = lax.rsqrt(square / plan.value_dim + 1e-05)
        return (m * scale * gain_in * silu(by_head(gate_in))).reshape(length, -1)

    def gate_apply_back(d_out, mixed_in, gate_in, gain_in):
        d, mixed_in, gate_in = by_head(d_out), by_head(mixed_in), by_head(gate_in)
        square = plan.value_sum(jnp.sum(mixed_in * mixed_in, axis=-1, keepdims=True))
        scale = lax.rsqrt(square / plan.value_dim + 1e-05)
        m = mixed_in * scale
        through = d * silu(gate_in)
        em = through * gain_in
        mean = plan.value_sum(jnp.sum(em * m, axis=-1, keepdims=True)) / plan.value_dim
        d_mix = scale * (em - m * mean)
        d_gt = d * m * gain_in * silu_slope(gate_in)
        return (
            d_mix.reshape(length, -1),
            d_gt.reshape(length, -1).astype(BF),
            jnp.sum(through * m, axis=(0, 1)),
        )

    if vs == 1:
        gated = gate_forward(mixed, pre_gate, own_gain[None], hp, dv)
    else:
        gated = gate_apply(mixed, pre_gate, own_gain).astype(BF)
    branch = lax.psum_scatter(
        after(nt(gated, out_cols).astype(BF), mlp_own_cols, cot_all), "seq", scatter_dimension=0, tiled=True
    )
    inputs = own_tokens.astype(F32)
    middle = inputs + branch.astype(F32)
    r2 = rms_scale(middle)
    n2 = middle * r2
    near_and_cot = lax.optimization_barrier(
        ((n2 * mlp_gain_full).astype(BF), cot_all) + tuple(mlp_near)
    )
    mlp_own, cot_all, mlp_near = near_and_cot[0], near_and_cot[1], near_and_cot[2:]
    mlp_cols = gather_end(mlp_own_cols, mlp_near)
    mlp_all = lax.all_gather(mlp_own, "seq", axis=0, tiled=True)
    both_w = mlp_cols[:, : 2 * ff]
    down_w = mlp_cols[:, 2 * ff :]
    d_product = nn(cot_all, down_w)
    both_pre = nn(mlp_all, both_w)
    hidden_pre = both_pre[:, :ff]
    up_pre = both_pre[:, ff:]
    sh = silu(hidden_pre)
    product = (sh * up_pre).astype(BF)
    d_both = jnp.concatenate(
        [
            (d_product * up_pre * silu_slope(hidden_pre)).astype(BF),
            (d_product * sh).astype(BF),
        ],
        axis=1,
    )
    d_mlp = lax.psum_scatter(
        nt(d_both, both_w).astype(BF), "seq", scatter_dimension=0, tiled=True
    ).astype(F32)
    d_output = own_cot.astype(F32)
    e2 = d_mlp * mlp_gain_full
    d_middle = d_output + r2 * (e2 - n2 * jnp.mean(e2 * n2, axis=-1, keepdims=True))
    down_sum = RingGrad(cot_all, product, kernel=False)
    both_sum = RingGrad(mlp_all, d_both, kernel=False)
    mlp_part = nt(product, down_w).astype(BF)
    down_sum.second(mlp_part)
    both_sum.second(mlp_part)
    d_branch_own = after(d_middle.astype(BF), *both_sum.sums, *down_sum.sums)
    d_branch_all = lax.all_gather(d_branch_own, "seq", axis=0, tiled=True)
    mlp_mine = jnp.concatenate([both_sum.total(d_branch_own), down_sum.total(d_branch_own)], axis=1)
    mlp_rows = exchange(mlp_mine)
    d_branch_all = after(d_branch_all, mlp_mine)
    mlp_out = lax.psum_scatter(
        after(mlp_part, d_branch_all), "seq", scatter_dimension=0, tiled=True
    )

    d_gated = nn(d_branch_all, out_cols)
    if vs == 1:
        d_mixed, d_gate, gain_part = gate_backward(
            d_gated, mixed, pre_gate, own_gain[None], hp, dv
        )
    else:
        d_mixed, d_gate, gain_part = gate_apply_back(d_gated, mixed, pre_gate, own_gain)
        gain_part = jnp.pad(gain_part[None], ((0, 7), (0, 0)))
    side_sum = RingPair((attn, d_gate), (d_branch_all, gated))
    d_mixed = after(d_mixed, *side_sum.sent)
    d_pre, d_sums = delta_backward(
        pre, pre_small, rider_all, taps, const, saved, d_mixed, gain_part, hp, dk, dv
    )
    held = lax.optimization_barrier((d_pre, d_sums) + side_sum.near)
    d_pre, d_sums = held[:2]
    side_sum.near = held[2:]
    side_sum.second()
    d_sums = sum_dp(d_sums)
    held = lax.optimization_barrier((d_pre, d_sums, mlp_rows) + side_sum.sums)
    d_pre, d_sums, mlp_rows = held[:3]
    d_attn_part = back_product((d_pre, w_mix, 0), (d_gate, w_side, 0))
    d_attn = lax.psum_scatter(d_attn_part, "seq", scatter_dimension=0, tiled=True).astype(F32)
    mix_sum = RingGrad(attn, after(d_pre, d_attn_part))
    every = gather_small(after(d_sums, d_attn_part))
    mlp_out, every, *held = lax.optimization_barrier(
        (mlp_out, every) + side_sum.late + mix_sum.far
    )
    count = len(side_sum.late)
    side_sum.late, mix_sum.far = tuple(held[:count]), tuple(held[count:])
    mix_sum.second()
    side_mine = side_sum.total(*mix_sum.sums)
    side_rows = to_rows(side_mine, ranks)
    every = every.reshape(ranks, 8, -1)
    held = lax.optimization_barrier((mlp_rows, mlp_out, side_rows) + mix_sum.near)
    mlp_rows, mlp_out, side_rows = held[:3]
    mix_sum.near = held[3:]
    mix_rows = to_rows(mix_sum.total(), ranks)
    grad_hidden, grad_up, grad_down = unpack_even(ranks, mlp_rows, 3)

    output = from_ring((middle + mlp_out.astype(F32)).astype(BF))
    n = inputs * rms_scale(inputs)
    e = d_attn * attn_gain_full
    grad_tokens = from_ring(
        (d_middle + rms_scale(inputs) * (e - n * jnp.mean(e * n, axis=-1, keepdims=True))).astype(BF)
    )

    def per_head(part, lead):
        part = part.reshape(ranks // vs, vs, lead, -1).sum(axis=1)
        return jnp.transpose(part, (1, 0, 2)).reshape(lead, -1)

    every_taps = every[:, :KERNEL]
    grad_conv_value = jnp.transpose(every_taps[:, :, at_v:], (1, 0, 2)).reshape(KERNEL, -1)
    gain_sum = every[:, 6, :dv].reshape(ranks // vs, vs, dv).sum(axis=0).reshape(-1)
    grad_query = plan.join_keys(mix_rows[:, :, :at_k])
    grad_key = plan.join_keys(mix_rows[:, :, at_k:at_v])
    grad_value = plan.join_even(mix_rows[:, :, at_v:at_s])
    grad_decay = plan.join_keys(mix_rows[:, :, at_s : at_s + hp])
    grad_beta = plan.join_keys(mix_rows[:, :, at_s + hp : at_s + 2 * hp])
    grad_gate = plan.join_even(side_rows[:, :, : hp * dv])

    def gain_grad(gain, pairs):
        total = sum(jnp.sum(w.astype(F32) * g, axis=1) for w, g in pairs)
        return total / gain.astype(F32)

    return (
        output[None],
        grad_tokens[None],
        gain_grad(
            attn_gain,
            (
                (w_query, grad_query),
                (w_key, grad_key),
                (w_value, grad_value),
                (w_decay, grad_decay),
                (w_beta, grad_beta),
                (w_gate, grad_gate),
            ),
        ),
        grad_query,
        grad_key,
        grad_value,
        grad_decay,
        grad_beta,
        grad_gate,
        plan.join_even(side_rows[:, :, hp * dv :]),
        per_head(every_taps[:, :, :at_k], KERNEL),
        per_head(every_taps[:, :, at_k:at_v], KERNEL),
        grad_conv_value,
        per_head(every[:, 5, :hp], 1)[0],
        per_head(every[:, 4, :hp], 1)[0],
        gain_sum,
        gain_grad(mlp_gain, ((w_hidden, grad_hidden), (w_up, grad_up))),
        grad_hidden,
        grad_up,
        grad_down,
    )


def solution(mesh):
    flat = ("dp", "seq")
    tok_spec = P("dp", "seq", None)
    row_spec = P(flat, None)
    gain_spec = P(flat)
    in_specs = (
        (tok_spec, gain_spec)
        + (row_spec,) * 7
        + (P(),) * 6
        + (gain_spec,)
        + (row_spec,) * 3
        + (P("dp", "seq"), tok_spec)
    )
    out_specs = (
        (tok_spec, tok_spec, gain_spec)
        + (row_spec,) * 7
        + (P(),) * 6
        + (gain_spec,)
        + (row_spec,) * 3
    )
    return jax.shard_map(local, mesh=mesh, in_specs=in_specs, out_specs=out_specs, check_vma=False)
```

```python
import functools

import jax
import jax.numpy as jnp
from jax import lax
from jax.experimental import pallas as pl
from jax.experimental.pallas import tpu as pltpu
from jax.sharding import PartitionSpec as P

KERNEL = 4
LANES = 128
BF = jnp.bfloat16
F32 = jnp.float32
CHUNK = 128


def rms_scale(value):
    return lax.rsqrt(jnp.mean(value * value, axis=-1, keepdims=True) + 1e-05)


def dot_f32(left, right, dims):
    return lax.dot_general(left, right, (dims, ((), ())), preferred_element_type=F32)


def nn(left, right):
    return dot_f32(left, right, ((1,), (0,)))


def nt(left, right):
    return dot_f32(left, right, ((1,), (1,)))


def tn(left, right):
    return dot_f32(left, right, ((0,), (0,)))


def silu(value):
    return value * jax.nn.sigmoid(value)


def silu_slope(value):
    s = jax.nn.sigmoid(value)
    return s * (1.0 + value * (1.0 - s))


class Plan:
    def __init__(self, ranks, heads, key_dim, value_dim, hidden):
        self.ranks = ranks
        self.heads = heads
        self.key_dim = key_dim
        self.hp = max(1, heads // ranks)
        self.vs = max(1, ranks // heads)
        self.dv = value_dim // self.vs
        self.value_dim = value_dim
        self.ff = hidden // ranks

    def split_keys(self, array):
        rows = array.shape[0]
        grouped = array.reshape(rows, self.heads // self.hp, -1)
        return jnp.repeat(grouped, self.vs, axis=1) if self.vs > 1 else grouped

    def split_even(self, array):
        return array.reshape(array.shape[0], self.ranks, -1)

    def join_keys(self, array):
        ranks, rows, width = array.shape
        array = array.astype(F32)
        if self.vs > 1:
            array = array.reshape(ranks // self.vs, self.vs, rows, width).sum(axis=1)
        return jnp.transpose(array, (1, 0, 2)).reshape(rows, -1)

    def join_even(self, array):
        return jnp.transpose(array, (1, 0, 2)).reshape(array.shape[1], -1).astype(F32)

    def value_sum(self, array):
        step = 1
        while step < self.vs:
            pairs = [(i, i ^ step) for i in range(self.ranks)]
            array = array + lax.ppermute(array, "seq", pairs)
            step *= 2
        return array


def after(value, *earlier):
    return lax.optimization_barrier((value,) + earlier)[0]


def ring_order(count):
    return [0, 1, 3, 2] if count == 4 else list(range(count))


def ring_pairs(count):
    order = ring_order(count)
    right = [(order[i], order[(i + 1) % count]) for i in range(count)]
    return right, [(there, here) for here, there in right]


def ring_place():
    me = lax.axis_index("dp")
    return me ^ (me >> 1)


def swap_blocks(array):
    size = array.shape[1] // 4
    return jnp.concatenate(
        [array[:, : 2 * size], array[:, 3 * size :], array[:, 2 * size : 3 * size]], axis=1
    )


def to_ring(array):
    if lax.axis_size("dp") != 4:
        return array
    width = array.shape[1]
    turned = swap_blocks(array)
    twice = jnp.concatenate([turned, turned], axis=1)
    return lax.dynamic_slice_in_dim(twice, ring_place() * (width // 4), width, 1)


def from_ring(array):
    if lax.axis_size("dp") != 4:
        return array
    width = array.shape[1]
    twice = jnp.concatenate([array, array], axis=1)
    at = (4 - ring_place()) * (width // 4)
    return swap_blocks(lax.dynamic_slice_in_dim(twice, at, width, 1))


def gather_start(own):
    if lax.axis_size("dp") != 4:
        return ()
    right, left = ring_pairs(4)
    return lax.ppermute(own, "dp", right), lax.ppermute(own, "dp", left)


def gather_end(own, near):
    if lax.axis_size("dp") != 4:
        return lax.all_gather(own, "dp", axis=0, tiled=True)
    right, left = ring_pairs(4)
    half = own.shape[0] // 2
    from_left, from_right = near
    far_a = lax.ppermute(from_left[:half], "dp", right)
    far_b = lax.ppermute(from_right[half:], "dp", left)
    return jnp.concatenate([own, from_right, far_a, far_b, from_left])


class RingGrad:
    def __init__(self, left, right, kernel=True):
        self.ring = lax.axis_size("dp") == 4
        self.left, self.right, self.kernel = left, right, kernel
        rows = self.rows = left.shape[1] // lax.axis_size("dp")
        half = self.half = rows // 2
        self.sent, self.far, self.sums, self.near = (), (), (), ()
        if self.ring:
            to_right, to_left = ring_pairs(4)
            self.sent = self.products((2 * rows, half, ()), (2 * rows + half, half, ()))
            self.far = (
                lax.ppermute(self.sent[0], "dp", to_right),
                lax.ppermute(self.sent[1], "dp", to_left),
            )

    def products(self, *spans):
        if self.kernel:
            return tuple(grad_rows(self.left, self.right, spans))
        out = []
        for at, size, arrived in spans:
            total = tn(self.left[:, at : at + size], self.right)
            for array, row in arrived:
                rest = size - row - array.shape[0]
                total = total + jnp.pad(array.astype(F32), ((row, rest), (0, 0)))
            out.append(total.astype(BF))
        return tuple(out)

    def second(self, *earlier):
        if self.ring:
            to_right, to_left = ring_pairs(4)
            far_a, far_b = lax.optimization_barrier(self.far + earlier)[:2]
            rows, half = self.rows, self.half
            self.sums = self.products(
                (rows, rows, ((far_a, 0),)), (3 * rows, rows, ((far_b, half),))
            )
            self.near = (
                lax.ppermute(self.sums[0], "dp", to_right),
                lax.ppermute(self.sums[1], "dp", to_left),
            )

    def total(self, *earlier):
        if not self.ring:
            whole = tn(self.left, self.right).astype(BF)
            return lax.psum_scatter(whole, "dp", scatter_dimension=0, tiled=True)
        held = lax.optimization_barrier(self.near + earlier)
        return self.products((0, self.rows, ((held[0], 0), (held[1], 0))))[0]


class RingPair:
    def __init__(self, *pairs):
        self.ring = lax.axis_size("dp") == 4
        self.pairs = pairs
        rows = self.rows = pairs[0][0].shape[1] // lax.axis_size("dp")
        self.half = rows // 2
        self.sent, self.near, self.sums, self.late = (), (), (), ()
        if self.ring:
            to_right, to_left = ring_pairs(4)
            self.sent = self.blocks((4, 5, 3, 6))
            self.near = (
                lax.ppermute(self.sent[0], "dp", to_right),
                lax.ppermute(self.sent[1], "dp", to_left),
                lax.ppermute(self.sent[2], "dp", to_right),
                lax.ppermute(self.sent[3], "dp", to_left),
            )

    def blocks(self, which, *extra):
        return tuple(grad_blocks(self.half, which, self.pairs, *extra))

    def second(self, *earlier):
        if self.ring:
            to_right, to_left = ring_pairs(4)
            held = lax.optimization_barrier(self.near + earlier)
            far, self.near = held[:2], held[:4]
            self.sums = self.blocks((2, 7), far)
            self.late = (
                lax.ppermute(self.sums[0], "dp", to_right),
                lax.ppermute(self.sums[1], "dp", to_left),
            )

    def total(self, *earlier):
        if not self.ring:
            whole = jnp.concatenate([tn(a, b).astype(BF) for a, b in self.pairs], axis=1)
            return lax.psum_scatter(whole, "dp", scatter_dimension=0, tiled=True)
        held = lax.optimization_barrier(self.near[2:] + self.late + earlier)
        right_b, left_a, right_a, left_b = held[:4]
        return jnp.concatenate(self.blocks((0, 1), (right_a, right_b), (left_a, left_b)))


def rank_major(packed):
    return jnp.transpose(packed, (1, 0, 2)).reshape(-1, packed.shape[2])


def exchange(packed):
    return lax.all_to_all(packed, "seq", 0, 0, tiled=True)


def to_rows(mine, ranks):
    turned = lax.all_to_all(mine, "seq", 0, 0, tiled=True)
    return turned.reshape(ranks, -1, mine.shape[1])


def sum_dp(values):
    count = lax.axis_size("dp")
    if count & (count - 1):
        return lax.psum(values, "dp")
    step = 1
    while step < count:
        values = values + lax.ppermute(values, "dp", [(i, i ^ step) for i in range(count)])
        step *= 2
    return values


def gather_small(values):
    ranks = lax.axis_size("seq")
    if ranks & (ranks - 1):
        return lax.all_gather(values, "seq", axis=0, tiled=True)
    rank = lax.axis_index("seq")
    step = 1
    while step < ranks:
        other = lax.ppermute(values, "seq", [(i, i ^ step) for i in range(ranks)])
        upper = (rank & step) != 0
        values = jnp.concatenate(
            [jnp.where(upper, other, values), jnp.where(upper, values, other)]
        )
        step *= 2
    return values


class Pair:
    def __init__(self, value):
        self.value = value
        self.high = value.astype(BF)
        self.low = (value - self.high.astype(F32)).astype(BF)


def pair(value):
    return value if isinstance(value, Pair) else Pair(value)


NN = ((1,), (0,))
NT = ((1,), (1,))
TN = ((0,), (0,))


def dot(left, right, dims):
    a, b = pair(left), pair(right)
    return dot_f32(a.high, b.high, dims) + (
        dot_f32(a.high, b.low, dims) + dot_f32(a.low, b.high, dims)
    )


def stack(top, bottom):
    return jnp.concatenate([top, bottom], axis=0)


def grids(n):
    t = lax.broadcasted_iota(jnp.int32, (n, n), 0)
    s = lax.broadcasted_iota(jnp.int32, (n, n), 1)
    return t, s


def inverses(stricts, t, s):
    n = t.shape[0]
    eye = jnp.where(t == s, 1.0, 0.0).astype(F32)
    same = (t // 8) == (s // 8)
    small = [Pair(jnp.where(same, a, 0.0)) for a in stricts]
    square = [Pair(dot(a, a, NN)) for a in small]
    fourth = [dot(a, a, NN) for a in square]
    first = [eye - a.value for a in small]
    inv = [f + dot(f, a, NN) for f, a in zip(first, square)]
    inv = [f + dot(f, a, NN) for f, a in zip(inv, fourth)]
    size = 8
    while size < n:
        take = ((t // (2 * size)) == (s // (2 * size))) & ((t // size) != (s // size))
        held = [Pair(f) for f in inv]
        part = [dot(f, jnp.where(take, a, 0.0), NN) for f, a in zip(held, stricts)]
        inv = [f.value - dot(p, f, NN) for f, p in zip(held, part)]
        size *= 2
    return inv


def decays(cols, hp, t, s):
    n = t.shape[0]
    tri = jnp.where(t >= s, 1.0, 0.0).astype(F32)
    run = dot(tri, cols, NN)
    turned = jnp.transpose(run)
    offs = cols[:, 2 * hp : 2 * hp + 1]
    row = t[:, :1].astype(F32)
    gap = (t - s).astype(F32)
    same = (gap >= 0.0) & (offs >= gap)
    keep = offs[n - 1 : n, :] >= (n - 1.0) - row
    out = []
    for h in range(hp):
        g = run[:, h : h + 1]
        g_row = turned[h : h + 1, :]
        pairwise = jnp.where(same, jnp.exp(jnp.where(same, g - g_row, 0.0)), 0.0)
        start = jnp.where(offs > row, jnp.exp(g), 0.0)
        end = jnp.where(keep, jnp.exp(jnp.where(keep, g[n - 1 : n, :] - g, 0.0)), 0.0)
        out.append((pairwise, start, end, start[n - 1 : n, :], cols[:, hp + h : hp + h + 1]))
    return out


def lanes_of(hp, dk, dv):
    q = [slice(h * dk, (h + 1) * dk) for h in range(hp)]
    k = [slice((hp + h) * dk, (hp + h + 1) * dk) for h in range(hp)]
    v = [slice(2 * hp * dk + h * dv, 2 * hp * dk + (h + 1) * dv) for h in range(hp)]
    return q, k, v


def chunk_rows(c):
    return pl.ds(pl.multiple_of(c * CHUNK, CHUNK), CHUNK)


def chunk_cols(hp, rows, small_ref, rider_ref, const_ref):
    lane = lax.broadcasted_iota(jnp.int32, (CHUNK, LANES), 1)
    x = small_ref[rows, :]
    y = x + const_ref[1:2, :]
    logs = const_ref[0:1, :] * (jnp.maximum(y, 0.0) + jnp.log1p(jnp.exp(-jnp.abs(y))))
    beta = jax.nn.sigmoid(x)
    offs = rider_ref[rows, 0:1]
    cols = jnp.where(lane < hp, logs, jnp.where(lane < 2 * hp, beta, 0.0))
    return jnp.where(lane == 2 * hp, offs, cols), offs


def conved_lanes(c, lanes, offs, pre_ref, taps_ref):
    rows = chunk_rows(c)
    above = pl.ds(pl.multiple_of(jnp.maximum(c * CHUNK - 16, 0), 16), 16)
    block = pre_ref[rows, lanes].astype(F32)
    ext = stack(pre_ref[above, lanes].astype(F32), block)
    total = taps_ref[0:1, lanes] * block
    for by in range(1, KERNEL):
        moved = pltpu.roll(ext, by, 0)[16:]
        total = total + taps_ref[by : by + 1, lanes] * jnp.where(offs >= by, moved, 0.0)
    return total


def unit_scale(u):
    return lax.rsqrt(jnp.sum(u * u, axis=1, keepdims=True) + 1e-06)


def fill_front(hp, dk, dv, c, pre_ref, small_ref, rider_ref, taps_ref, const_ref, qkv_ref, cols_ref, conv_ref):
    rows = chunk_rows(c)
    cols, offs = chunk_cols(hp, rows, small_ref, rider_ref, const_ref)
    cols_ref[rows, :] = cols
    for kind, slices in enumerate(lanes_of(hp, dk, dv)):
        for lanes in slices:
            conved = conved_lanes(c, lanes, offs, pre_ref, taps_ref)
            if conv_ref is not None:
                conv_ref[rows, lanes] = conved
            u = conved * jax.nn.sigmoid(conved)
            if kind == 0:
                u = u * (unit_scale(u) * dk ** (-0.5))
            elif kind == 1:
                u = u * unit_scale(u)
            qkv_ref[rows, lanes] = u


def fwd_kernel(
    hp, dk, dv, pre_ref, small_ref, rider_ref, taps_ref, const_ref,
    mixed_ref, state_ref, upd_ref, inv_ref, seen_ref,
    qkv_ref, cols_ref, p_ref, cur_ref,
):
    n = CHUNK
    chunks = pre_ref.shape[0] // n
    group = 2 if chunks % 2 == 0 else 1
    t, s = grids(n)
    q_at, k_at, v_at = lanes_of(hp, dk, dv)

    def prepare(step, carry):
        jobs = []
        for j in range(group):
            c = step * group + j
            fill_front(
                hp, dk, dv, c, pre_ref, small_ref, rider_ref, taps_ref, const_ref, qkv_ref, cols_ref, None
            )
            rows = chunk_rows(c)
            for h, d in enumerate(decays(cols_ref[rows, :], hp, t, s)):
                jobs.append((c, rows, h) + d)
        keys = [qkv_ref[r, k_at[h]] for _, r, h, *_ in jobs]
        both = [dot(stack(k, qkv_ref[job[1], q_at[job[2]]]), k, NT) for k, job in zip(keys, jobs)]
        strict = [jnp.where(t > s, job[3] * b[:n], 0.0) * job[7] for job, b in zip(jobs, both)]
        inv = [Pair(i) for i in inverses(strict, t, s)]
        for job, b, i, k in zip(jobs, both, inv, keys):
            c, r, h, pairwise, start, end, last, beta = job
            p_ref[c * hp + h] = pairwise * b[n:]
            inv_ref[c * hp + h] = i.value
            upd_ref[r, h * dv : (h + 1) * dv] = dot(i, beta * qkv_ref[r, v_at[h]], NN)
            seen_ref[r, h * dk : (h + 1) * dk] = dot(i, (beta * start) * k, NN)
        return carry

    lax.fori_loop(0, chunks // group, prepare, 0)
    cur_ref[...] = jnp.zeros_like(cur_ref)

    def advance(c, carry):
        rows = chunk_rows(c)
        for h, (pairwise, start, end, last, beta) in enumerate(decays(cols_ref[rows, :], hp, t, s)):
            vv = slice(h * dv, (h + 1) * dv)
            state = cur_ref[h]
            state_ref[c * hp + h] = state
            seen = seen_ref[rows, h * dk : (h + 1) * dk]
            both = dot(stack(seen, qkv_ref[rows, q_at[h]] * start), state, NN)
            update = Pair(upd_ref[rows, vv] - both[:n])
            upd_ref[rows, vv] = update.value
            mixed_ref[rows, vv] = both[n:] + dot(p_ref[c * hp + h], update, NN)
            cur_ref[h] = last * state + dot(qkv_ref[rows, k_at[h]] * end, update, TN)
        return carry

    lax.fori_loop(0, chunks, advance, 0)


def bwd_kernel(
    hp, dk, dv, pre_ref, small_ref, rider_ref, taps_ref, const_ref,
    state_ref, upd_ref, inv_ref, seen_ref, dm_ref, gain_ref,
    dpre_ref, dtaps_ref,
    qkv_ref, cols_ref, conv_ref, dcon_ref, dcols_ref, du_ref, ds_ref, cur_ref,
):
    n = CHUNK
    total = pre_ref.shape[0]
    chunks = total // n
    t, s = grids(n)
    q_at, k_at, v_at = lanes_of(hp, dk, dv)
    wide = 2 * hp * dk + hp * dv
    cur_ref[...] = jnp.zeros_like(cur_ref)
    dtaps_ref[...] = jnp.zeros_like(dtaps_ref)
    dtaps_ref[6:7, : gain_ref.shape[1]] = gain_ref[0:1, :]
    dcon_ref[total:, :] = jnp.zeros((dcon_ref.shape[0] - total, wide), F32)
    cols_ref[total:, :] = jnp.zeros((cols_ref.shape[0] - total, LANES), F32)

    def retreat(step, carry):
        c = chunks - 1 - step
        rows = chunk_rows(c)
        fill_front(
            hp, dk, dv, c, pre_ref, small_ref, rider_ref, taps_ref, const_ref, qkv_ref, cols_ref, conv_ref
        )
        for h, (pairwise, start, end, last, beta) in enumerate(decays(cols_ref[rows, :], hp, t, s)):
            vv = slice(h * dv, (h + 1) * dv)
            d_state = cur_ref[h]
            ds_ref[c * hp + h] = d_state
            dm = Pair(dm_ref[rows, vv])
            q, k = qkv_ref[rows, q_at[h]], qkv_ref[rows, k_at[h]]
            p = pairwise * dot(q, k, NT)
            du = dot(p, dm, TN) + dot(k * end, d_state, NN)
            du_ref[rows, vv] = du
            seen = seen_ref[rows, h * dk : (h + 1) * dk]
            cur_ref[h] = last * d_state + dot(q * start, dm, TN) - dot(seen, du, TN)
        return carry

    lax.fori_loop(0, chunks, retreat, 0)
    lane = lax.broadcasted_iota(jnp.int32, (n, LANES), 1)

    def through_silu(rows, lanes, dy, unit):
        conved = conv_ref[rows, lanes]
        sig = jax.nn.sigmoid(conved)
        if unit:
            u = conved * sig
            scale = unit_scale(u)
            dy = scale * dy - (scale * scale * scale) * u * jnp.sum(u * dy, axis=1, keepdims=True)
        dcon_ref[rows, lanes] = dy * (sig * (1.0 + conved * (1.0 - sig)))

    def finish(c, carry):
        rows = chunk_rows(c)
        d_cols = jnp.zeros((n, LANES), F32)
        for h, (pairwise, start, end, last, beta) in enumerate(decays(cols_ref[rows, :], hp, t, s)):
            vv = slice(h * dv, (h + 1) * dv)
            q, k, v = qkv_ref[rows, q_at[h]], qkv_ref[rows, k_at[h]], qkv_ref[rows, v_at[h]]
            dm = dm_ref[rows, vv]
            q_p, k_p, u_p = Pair(q), Pair(k), Pair(upd_ref[rows, vv])
            state = Pair(state_ref[c * hp + h])
            d_state = Pair(ds_ref[c * hp + h])
            w = dot(inv_ref[c * hp + h], du_ref[rows, vv], TN)
            scores = dot(stack(w, dm), u_p, NT)
            d_a = jnp.where(t > s, -scores[:n], 0.0)
            d_p = scores[n:]
            keys = dot(stack(k, q), k_p, NT)
            met = dot(stack(k, q), state, NN)
            r, qs = met[:n], met[n:]
            back = dot(stack(start * dm, -(beta * start) * w), state, NT)
            x = dot(u_p, d_state, NT)
            d_qk = pairwise * d_p
            d_kk = beta * (pairwise * d_a)
            d_query = back[:n] + dot(d_qk, k_p, NN)
            d_key = (
                back[n:]
                + dot(d_qk, q_p, TN)
                + dot(d_kk + jnp.transpose(d_kk), k_p, NN)
                + end * x
            )
            through_silu(rows, q_at[h], d_query * dk ** (-0.5), True)
            through_silu(rows, k_at[h], d_key, True)
            through_silu(rows, v_at[h], beta * w, False)
            inner = pairwise * d_a * keys[:n]
            d_beta = jnp.sum(w * (v - start * r), axis=1, keepdims=True) + jnp.sum(
                inner, axis=1, keepdims=True
            )
            d_start = jnp.sum(dm * qs, axis=1, keepdims=True) - beta * jnp.sum(
                w * r, axis=1, keepdims=True
            )
            e = pairwise * d_p * keys[n:] + beta * inner
            d_end = end * jnp.sum(k * x, axis=1, keepdims=True)
            d_g = (
                jnp.sum(e, axis=1, keepdims=True)
                - jnp.sum(jnp.transpose(e), axis=1, keepdims=True)
                + d_start * start
                - d_end
            )
            held = jnp.sum(
                jnp.sum(state.value * d_state.value, axis=1, keepdims=True), axis=0, keepdims=True
            )
            tail = jnp.sum(d_end, axis=0, keepdims=True) + last * held
            d_g = d_g + jnp.where(t[:, :1] == n - 1, tail, 0.0)
            d_cols = jnp.where(lane == h, d_g, d_cols)
            d_cols = jnp.where(lane == hp + h, d_beta, d_cols)
        tri = jnp.where(t >= s, 1.0, 0.0).astype(F32)
        dcols_ref[rows, :] = jnp.where(lane < hp, dot(tri, d_cols, TN), d_cols)
        return carry

    lax.fori_loop(0, chunks, finish, 0)

    def spread(c, carry):
        rows = chunk_rows(c)
        below = pl.ds(pl.multiple_of((c + 1) * n, n), 8)
        cols = cols_ref[rows, :]
        offs = cols[:, 2 * hp : 2 * hp + 1]
        offs_below = cols_ref[below, 2 * hp : 2 * hp + 1]
        for slices in (q_at, k_at, v_at):
            for lanes in slices:
                pre = pre_ref[rows, lanes].astype(F32)
                d_con = dcon_ref[rows, lanes]
                d_below = dcon_ref[below, lanes]
                out = taps_ref[0:1, lanes] * d_con
                dtaps_ref[0:1, lanes] += jnp.sum(pre * d_con, axis=0, keepdims=True)
                for by in range(1, KERNEL):
                    ext = stack(
                        jnp.where(offs >= by, d_con, 0.0), jnp.where(offs_below >= by, d_below, 0.0)
                    )
                    moved = pltpu.roll(ext, n + 8 - by, 0)[:n]
                    out = out + taps_ref[by : by + 1, lanes] * moved
                    dtaps_ref[by : by + 1, lanes] += jnp.sum(pre * moved, axis=0, keepdims=True)
                dpre_ref[rows, lanes] = out.astype(BF)
        d_cols = dcols_ref[rows, :]
        slope = const_ref[0:1, :] * jax.nn.sigmoid(small_ref[rows, :] + const_ref[1:2, :])
        d_small = jnp.where(lane < hp, d_cols * slope, d_cols * cols * (1.0 - cols))
        d_small = jnp.where(lane < 2 * hp, d_small, 0.0)
        dpre_ref[rows, wide:] = d_small.astype(BF)
        dtaps_ref[4:5, :LANES] += jnp.sum(d_small, axis=0, keepdims=True)
        dtaps_ref[5:6, :LANES] += jnp.sum(d_cols * cols, axis=0, keepdims=True)
        return carry

    lax.fori_loop(0, chunks, spread, 0)


def gate_kernel(hp, dv, mixed_ref, gate_ref, gain_ref, out_ref):
    for h in range(hp):
        at = slice(h * dv, (h + 1) * dv)
        mixed = mixed_ref[:, at]
        scale = lax.rsqrt(jnp.mean(mixed * mixed, axis=1, keepdims=True) + 1e-05)
        gate = gate_ref[:, at]
        out_ref[:, at] = (mixed * scale * gain_ref[0:1, :] * (gate * jax.nn.sigmoid(gate))).astype(BF)


def gate_back_kernel(hp, dv, d_ref, mixed_ref, gate_ref, gain_ref, dm_ref, dgate_ref, dgain_ref):
    @pl.when(pl.program_id(0) == 0)
    def _():
        dgain_ref[...] = jnp.zeros_like(dgain_ref)

    gain = gain_ref[0:1, :]
    for h in range(hp):
        at = slice(h * dv, (h + 1) * dv)
        mixed = mixed_ref[:, at]
        scale = lax.rsqrt(jnp.mean(mixed * mixed, axis=1, keepdims=True) + 1e-05)
        m = mixed * scale
        gate = gate_ref[:, at]
        sig = jax.nn.sigmoid(gate)
        through = d_ref[:, at] * (gate * sig)
        dgain_ref[0:1, :] += jnp.sum(through * m, axis=0, keepdims=True)
        em = through * gain
        dm_ref[:, at] = scale * (em - m * jnp.mean(em * m, axis=1, keepdims=True))
        slope = sig * (1.0 + gate * (1.0 - sig))
        dgate_ref[:, at] = (d_ref[:, at] * m * gain * slope).astype(BF)


def pack_kernel(ranks, *refs):
    *ins, out_ref = refs
    rows = ins[0].shape[0]
    parts = [ref[...].astype(F32) for ref in ins]
    for r in range(ranks):
        pieces = [p[:, r * (p.shape[1] // ranks) : (r + 1) * (p.shape[1] // ranks)] for p in parts]
        out_ref[r * rows : (r + 1) * rows, :] = jnp.concatenate(pieces, axis=1).astype(BF)


def mix_pack_kernel(ranks, hp, vs, q_ref, k_ref, v_ref, decay_ref, beta_ref, gain_ref, out_ref):
    rows = q_ref.shape[0]
    groups = ranks // vs
    k_wide, v_wide = q_ref.shape[1] // groups, v_ref.shape[1] // ranks
    lane = lax.broadcasted_iota(jnp.int32, (rows, LANES), 1)
    decay, beta = decay_ref[...].astype(F32), beta_ref[...].astype(F32)
    gain = gain_ref[...].astype(F32)
    for r in range(ranks):
        at, g = slice(r * rows, (r + 1) * rows), r // vs
        out_ref[at, :k_wide] = q_ref[:, g * k_wide : (g + 1) * k_wide]
        out_ref[at, k_wide : 2 * k_wide] = k_ref[:, g * k_wide : (g + 1) * k_wide]
        out_ref[at, 2 * k_wide : 2 * k_wide + v_wide] = v_ref[:, r * v_wide : (r + 1) * v_wide]
        small = jnp.zeros((rows, LANES), F32)
        for j in range(hp):
            small = jnp.where(lane == j, decay[:, g * hp + j : g * hp + j + 1], small)
            small = jnp.where(lane == hp + j, beta[:, g * hp + j : g * hp + j + 1], small)
        small = jnp.where(lane == 2 * hp, gain[:, 0:1], small)
        small = jnp.where(lane == 2 * hp + 1, gain[:, 1:2], small)
        out_ref[at, 2 * k_wide + v_wide :] = small.astype(BF)


def unpack_kernel(ranks, in_ref, *outs):
    rows = outs[0].shape[0]
    for i, out_ref in enumerate(outs):
        size = out_ref.shape[1] // ranks
        pieces = [
            in_ref[r * rows : (r + 1) * rows, :].astype(F32)[:, i * size : (i + 1) * size]
            for r in range(ranks)
        ]
        out_ref[...] = jnp.concatenate(pieces, axis=1)


def grad_kernel(spans, left_ref, right_ref, *refs):
    adds, outs = refs[: -len(spans)], refs[-len(spans) :]
    taken = 0
    for (at, size, places), out_ref in zip(spans, outs):
        for row in range(0, size, 256):
            high = min(256, size - row)
            piece = dot_f32(left_ref[:, at + row : at + row + high], right_ref[...], TN)
            for k, (first, rows) in enumerate(places):
                if first <= row < first + rows:
                    piece = piece + adds[taken + k][row - first : row - first + high, :].astype(F32)
            out_ref[row : row + high, :] = piece.astype(BF)
        taken += len(places)


def block_kernel(half, blocks, pairs, extra, *refs):
    lefts, rights = refs[:pairs], refs[pairs : 2 * pairs]
    adds, outs = refs[2 * pairs : -len(blocks)], refs[-len(blocks) :]
    for i, block in enumerate(blocks):
        lane = 0
        for left_ref, right_ref in zip(lefts, rights):
            wide = right_ref.shape[1]
            at = slice(lane, lane + wide)
            piece = dot_f32(left_ref[:, block * half : (block + 1) * half], right_ref[...], TN)
            for k in range(extra):
                piece = piece + adds[k * len(blocks) + i][:, at].astype(F32)
            outs[i][:, at] = piece.astype(BF)
            lane += wide


VMEM_LIMIT = 60 * 2**20


def shape_of(*dims, dtype=F32):
    return jax.ShapeDtypeStruct(dims, dtype)


def grad_rows(left, right, spans):
    wide = right.shape[1]
    rows = sum(size for _, size, _ in spans)
    fixed = tuple(
        (at, size, tuple((row, x.shape[0]) for x, row in arrived)) for at, size, arrived in spans
    )
    return pl.pallas_call(
        functools.partial(grad_kernel, fixed),
        out_shape=tuple(shape_of(size, wide, dtype=BF) for _, size, _ in spans),
        compiler_params=pltpu.CompilerParams(vmem_limit_bytes=VMEM_LIMIT),
        cost_estimate=pl.CostEstimate(
            flops=2 * rows * wide * left.shape[0],
            transcendentals=0,
            bytes_accessed=2 * (left.size + right.size + rows * wide),
        ),
        name="grad_rows",
    )(left, right, *(x for _, _, arrived in spans for x, _ in arrived))


def grad_blocks(half, blocks, pairs, *extra):
    wide = sum(b.shape[1] for _, b in pairs)
    arrays = [a for a, _ in pairs] + [b for _, b in pairs] + [x for xs in extra for x in xs]
    return pl.pallas_call(
        functools.partial(block_kernel, half, blocks, len(pairs), len(extra)),
        out_shape=(shape_of(half, wide, dtype=BF),) * len(blocks),
        compiler_params=pltpu.CompilerParams(vmem_limit_bytes=VMEM_LIMIT),
        cost_estimate=pl.CostEstimate(
            flops=half * len(blocks) * wide * pairs[0][0].shape[0] // 8,
            transcendentals=0,
            bytes_accessed=half * len(blocks) * wide,
        ),
        name="grad_blocks",
    )(*arrays)


def back_kernel(pairs, *refs):
    total = dot_f32(refs[0][...], refs[pairs][...], NT)
    for i in range(1, pairs):
        total = total + dot_f32(refs[i][...], refs[pairs + i][...], NT)
    refs[-1][...] = total.astype(BF)


def column_block(at):
    return lambda i: (0, at)


def back_product(*terms):
    total, wide = terms[0][0].shape[0], terms[0][1].shape[0]
    rows = 256
    return pl.pallas_call(
        functools.partial(back_kernel, len(terms)),
        grid=(total // rows,),
        in_specs=[pl.BlockSpec((rows, a.shape[1]), lambda i: (i, 0)) for a, _, _ in terms]
        + [pl.BlockSpec((wide, a.shape[1]), column_block(at)) for a, _, at in terms],
        out_specs=pl.BlockSpec((rows, wide), lambda i: (i, 0)),
        out_shape=shape_of(total, wide, dtype=BF),
        compiler_params=pltpu.CompilerParams(vmem_limit_bytes=VMEM_LIMIT),
        cost_estimate=pl.CostEstimate(
            flops=total * wide * 256, transcendentals=0, bytes_accessed=total * wide
        ),
        name="back_product",
    )(*(a for a, _, _ in terms), *(b for _, b, _ in terms))


def pack_even(ranks, *arrays):
    rows = arrays[0].shape[0]
    wide = sum(a.shape[1] for a in arrays) // ranks
    return pl.pallas_call(
        functools.partial(pack_kernel, ranks),
        out_shape=shape_of(ranks * rows, wide, dtype=BF),
        compiler_params=pltpu.CompilerParams(vmem_limit_bytes=VMEM_LIMIT),
        name="pack_even",
    )(*arrays)


def pack_mix(ranks, hp, vs, w_query, w_key, w_value, *smalls):
    rows = w_query.shape[0]
    wide = 2 * w_query.shape[1] * vs // ranks + w_value.shape[1] // ranks + LANES
    return pl.pallas_call(
        functools.partial(mix_pack_kernel, ranks, hp, vs),
        out_shape=shape_of(ranks * rows, wide, dtype=BF),
        compiler_params=pltpu.CompilerParams(vmem_limit_bytes=VMEM_LIMIT),
        name="pack_mix",
    )(w_query, w_key, w_value, *smalls)


def unpack_even(ranks, packed, count):
    rows = packed.shape[0] // ranks
    size = packed.shape[1] // count
    return pl.pallas_call(
        functools.partial(unpack_kernel, ranks),
        out_shape=(shape_of(rows, ranks * size),) * count,
        compiler_params=pltpu.CompilerParams(vmem_limit_bytes=VMEM_LIMIT),
        name="unpack_even",
    )(packed)


def delta_forward(pre, small, rider, taps, const, hp, dk, dv):
    total, wide = pre.shape
    jobs = total // CHUNK * hp
    return pl.pallas_call(
        functools.partial(fwd_kernel, hp, dk, dv),
        out_shape=(
            shape_of(total, hp * dv),
            shape_of(jobs, dk, dv),
            shape_of(total, hp * dv),
            shape_of(jobs, CHUNK, CHUNK),
            shape_of(total, hp * dk),
        ),
        scratch_shapes=[
            pltpu.VMEM((total, wide), F32),
            pltpu.VMEM((total, LANES), F32),
            pltpu.VMEM((jobs, CHUNK, CHUNK), F32),
            pltpu.VMEM((hp, dk, dv), F32),
        ],
        compiler_params=pltpu.CompilerParams(vmem_limit_bytes=VMEM_LIMIT),
        cost_estimate=pl.CostEstimate(
            flops=total * hp * 21_000_000,
            transcendentals=total * hp * CHUNK,
            bytes_accessed=total * wide * 16,
        ),
        name="delta_forward",
    )(pre, small, rider, taps, const)


def delta_backward(pre, small, rider, taps, const, saved, d_mixed, gain, hp, dk, dv):
    total, wide = pre.shape
    jobs = total // CHUNK * hp
    return pl.pallas_call(
        functools.partial(bwd_kernel, hp, dk, dv),
        out_shape=(
            shape_of(total, wide + LANES, dtype=BF),
            shape_of(8, wide),
        ),
        scratch_shapes=[
            pltpu.VMEM((total, wide), F32),
            pltpu.VMEM((total + 8, LANES), F32),
            pltpu.VMEM((total, wide), F32),
            pltpu.VMEM((total + 8, wide), F32),
            pltpu.VMEM((total, LANES), F32),
            pltpu.VMEM((total, hp * dv), F32),
            pltpu.VMEM((jobs, dk, dv), F32),
            pltpu.VMEM((hp, dk, dv), F32),
        ],
        compiler_params=pltpu.CompilerParams(vmem_limit_bytes=VMEM_LIMIT),
        cost_estimate=pl.CostEstimate(
            flops=total * hp * 5_000_000,
            transcendentals=total * hp * CHUNK,
            bytes_accessed=total * wide * 20,
        ),
        name="delta_backward",
    )(pre, small, rider, taps, const, *saved, d_mixed, gain)


GATE_ROWS = 256


def gate_forward(mixed, gate, gain, hp, dv):
    total, wide = mixed.shape
    rows = min(GATE_ROWS, total)
    block = pl.BlockSpec((rows, wide), lambda i: (i, 0))
    return pl.pallas_call(
        functools.partial(gate_kernel, hp, dv),
        grid=(total // rows,),
        in_specs=[block, block, pl.BlockSpec((1, dv), lambda i: (0, 0))],
        out_specs=block,
        out_shape=shape_of(total, wide, dtype=BF),
        name="gate_forward",
    )(mixed, gate, gain)


def gate_backward(d_gated, mixed, gate, gain, hp, dv):
    total, wide = mixed.shape
    rows = min(GATE_ROWS, total)
    block = pl.BlockSpec((rows, wide), lambda i: (i, 0))
    return pl.pallas_call(
        functools.partial(gate_back_kernel, hp, dv),
        grid=(total // rows,),
        in_specs=[block, block, block, pl.BlockSpec((1, dv), lambda i: (0, 0))],
        out_specs=(block, block, pl.BlockSpec((8, dv), lambda i: (0, 0))),
        out_shape=(
            shape_of(total, wide),
            shape_of(total, wide, dtype=BF),
            shape_of(8, dv),
        ),
        name="gate_backward",
    )(d_gated, mixed, gate, gain)


def local(
    tokens,
    attn_gain,
    w_query,
    w_key,
    w_value,
    w_decay,
    w_beta,
    w_gate,
    w_out,
    conv_query,
    conv_key,
    conv_value,
    decay_log,
    decay_bias,
    out_gain,
    mlp_gain,
    w_hidden,
    w_up,
    w_down,
    offsets,
    cotangent,
):
    ranks = lax.axis_size("seq")
    rank = lax.axis_index("seq")
    heads = decay_log.shape[0]
    width = tokens.shape[-1]
    tok = tokens.shape[1]
    length = tok * ranks
    plan = Plan(ranks, heads, w_query.shape[1] // heads, out_gain.shape[0], w_hidden.shape[1])
    hp, vs, dk, dv, ff = plan.hp, plan.vs, plan.key_dim, plan.dv, plan.ff
    rows = w_query.shape[0]

    own_tokens = to_ring(tokens[0])
    own_cot = to_ring(cotangent[0])
    gains = jnp.stack([attn_gain, mlp_gain], axis=1)
    mix_pack = pack_mix(ranks, hp, vs, w_query, w_key, w_value, w_decay, w_beta, gains)
    side_pack = rank_major(
        jnp.concatenate([plan.split_even(w_gate), plan.split_even(w_out)], axis=2)
    )
    mlp_pack = pack_even(ranks, w_hidden, w_up, w_down)
    mix_own = exchange(mix_pack)
    row_offsets = gather_small(offsets.astype(F32))
    held = lax.optimization_barrier(
        (own_tokens, side_pack, mlp_pack, mix_own, row_offsets)
    )
    gathered = lax.all_gather(held[0], "seq", axis=0, tiled=True)
    side_own = exchange(held[1])
    mix_own, row_offsets = held[3], held[4]
    w_mix = gather_end(mix_own, gather_start(mix_own))
    mlp_own_cols = exchange(after(held[2], side_own, gathered))
    side_own = after(side_own, w_mix)
    side_near = gather_start(side_own)

    at_k = hp * dk
    at_v = 2 * hp * dk
    at_s = at_v + hp * dv
    attn_gain_full = w_mix[:, at_s + 2 * hp].astype(F32)
    mlp_gain_full = w_mix[:, at_s + 2 * hp + 1].astype(F32)

    tokens_all = gathered.astype(F32)
    normed_all = tokens_all * rms_scale(tokens_all)
    attn = (normed_all * attn_gain_full).astype(BF)
    pre = nn(attn, w_mix[:, :at_s]).astype(BF)
    pre_small = nn(attn, w_mix[:, at_s:])
    cot_all = lax.all_gather(after(own_cot, pre), "seq", axis=0, tiled=True)
    group = rank // vs
    taps_query = lax.dynamic_slice_in_dim(conv_query, group * hp * dk, hp * dk, 1)
    taps_key = lax.dynamic_slice_in_dim(conv_key, group * hp * dk, hp * dk, 1)
    taps_value = lax.dynamic_slice_in_dim(conv_value, rank * hp * dv, hp * dv, 1)
    own_log = lax.dynamic_slice_in_dim(decay_log, group * hp, hp, 0)
    own_bias = lax.dynamic_slice_in_dim(decay_bias, group * hp, hp, 0)
    own_gain = lax.dynamic_slice_in_dim(out_gain, (rank % vs) * dv, dv, 0)

    taps = jnp.concatenate([taps_query, taps_key, taps_value], axis=1)
    const = jnp.pad(jnp.stack([-jnp.exp(own_log), own_bias]), ((0, 0), (0, LANES - hp)))
    pre, pre_small = lax.optimization_barrier((pre, pre_small, side_own))[:2]
    rider_all = jnp.pad(row_offsets.reshape(length, 1), ((0, 0), (0, LANES - 1)))
    mixed, *saved = delta_forward(pre, pre_small, rider_all, taps, const, hp, dk, dv)
    mixed, *side_near = lax.optimization_barrier((mixed,) + tuple(side_near))
    w_side = gather_end(side_own, side_near)
    gate_cols = w_side[:, : hp * dv]
    out_cols = w_side[:, hp * dv :]
    mlp_near = gather_start(after(mlp_own_cols, w_side))
    pre_gate = nn(attn, gate_cols)

    def by_head(array):
        return array.reshape(length, hp, -1)

    def gate_apply(mixed_in, gate_in, gain_in):
        m = by_head(mixed_in)
        square = plan.value_sum(jnp.sum(m * m, axis=-1, keepdims=True))
        scale = lax.rsqrt(square / plan.value_dim + 1e-05)
        return (m * scale * gain_in * silu(by_head(gate_in))).reshape(length, -1)

    def gate_apply_back(d_out, mixed_in, gate_in, gain_in):
        d, mixed_in, gate_in = by_head(d_out), by_head(mixed_in), by_head(gate_in)
        square = plan.value_sum(jnp.sum(mixed_in * mixed_in, axis=-1, keepdims=True))
        scale = lax.rsqrt(square / plan.value_dim + 1e-05)
        m = mixed_in * scale
        through = d * silu(gate_in)
        em = through * gain_in
        mean = plan.value_sum(jnp.sum(em * m, axis=-1, keepdims=True)) / plan.value_dim
        d_mix = scale * (em - m * mean)
        d_gt = d * m * gain_in * silu_slope(gate_in)
        return (
            d_mix.reshape(length, -1),
            d_gt.reshape(length, -1).astype(BF),
            jnp.sum(through * m, axis=(0, 1)),
        )

    if vs == 1:
        gated = gate_forward(mixed, pre_gate, own_gain[None], hp, dv)
    else:
        gated = gate_apply(mixed, pre_gate, own_gain).astype(BF)
    branch = lax.psum_scatter(
        after(nt(gated, out_cols).astype(BF), mlp_own_cols, cot_all), "seq", scatter_dimension=0, tiled=True
    )
    inputs = own_tokens.astype(F32)
    middle = inputs + branch.astype(F32)
    r2 = rms_scale(middle)
    n2 = middle * r2
    near_and_cot = lax.optimization_barrier(
        ((n2 * mlp_gain_full).astype(BF), cot_all) + tuple(mlp_near)
    )
    mlp_own, cot_all, mlp_near = near_and_cot[0], near_and_cot[1], near_and_cot[2:]
    mlp_cols = gather_end(mlp_own_cols, mlp_near)
    mlp_all = lax.all_gather(mlp_own, "seq", axis=0, tiled=True)
    both_w = mlp_cols[:, : 2 * ff]
    down_w = mlp_cols[:, 2 * ff :]
    d_product = nn(cot_all, down_w)
    mlp_all, d_product = lax.optimization_barrier((mlp_all, d_product))
    both_pre = nn(mlp_all, both_w)
    hidden_pre = both_pre[:, :ff]
    up_pre = both_pre[:, ff:]
    sh = silu(hidden_pre)
    product = (sh * up_pre).astype(BF)
    d_both = jnp.concatenate(
        [
            (d_product * up_pre * silu_slope(hidden_pre)).astype(BF),
            (d_product * sh).astype(BF),
        ],
        axis=1,
    )
    d_mlp = lax.psum_scatter(
        nt(d_both, both_w).astype(BF), "seq", scatter_dimension=0, tiled=True
    ).astype(F32)
    d_output = own_cot.astype(F32)
    e2 = d_mlp * mlp_gain_full
    d_middle = d_output + r2 * (e2 - n2 * jnp.mean(e2 * n2, axis=-1, keepdims=True))
    down_sum = RingGrad(cot_all, product, kernel=False)
    both_sum = RingGrad(mlp_all, d_both, kernel=False)
    mlp_part = nt(product, down_w).astype(BF)
    down_sum.second(mlp_part)
    both_sum.second(mlp_part)
    d_branch_own = after(d_middle.astype(BF), *both_sum.sums, *down_sum.sums)
    d_branch_all = lax.all_gather(d_branch_own, "seq", axis=0, tiled=True)
    mlp_mine = jnp.concatenate([both_sum.total(d_branch_own), down_sum.total(d_branch_own)], axis=1)
    mlp_rows = exchange(mlp_mine)
    d_branch_all = after(d_branch_all, mlp_mine)
    mlp_out = lax.psum_scatter(
        after(mlp_part, d_branch_all), "seq", scatter_dimension=0, tiled=True
    )

    d_gated = nn(d_branch_all, out_cols)
    if vs == 1:
        d_mixed, d_gate, gain_part = gate_backward(
            d_gated, mixed, pre_gate, own_gain[None], hp, dv
        )
    else:
        d_mixed, d_gate, gain_part = gate_apply_back(d_gated, mixed, pre_gate, own_gain)
        gain_part = jnp.pad(gain_part[None], ((0, 7), (0, 0)))
    side_sum = RingPair((attn, d_gate), (d_branch_all, gated))
    d_mixed = after(d_mixed, *side_sum.sent)
    d_pre, d_sums = delta_backward(
        pre, pre_small, rider_all, taps, const, saved, d_mixed, gain_part, hp, dk, dv
    )
    held = lax.optimization_barrier((d_pre, d_sums) + side_sum.near)
    d_pre, d_sums = held[:2]
    side_sum.near = held[2:]
    side_sum.second()
    d_sums = sum_dp(d_sums)
    held = lax.optimization_barrier((d_pre, d_sums, mlp_rows) + side_sum.sums)
    d_pre, d_sums, mlp_rows = held[:3]
    d_attn_part = back_product((d_pre, w_mix, 0), (d_gate, w_side, 0))
    d_attn = lax.psum_scatter(d_attn_part, "seq", scatter_dimension=0, tiled=True).astype(F32)
    mix_sum = RingGrad(attn, after(d_pre, d_attn_part))
    every = gather_small(after(d_sums, d_attn_part))
    mlp_out, every, *held = lax.optimization_barrier(
        (mlp_out, every) + side_sum.late + mix_sum.far
    )
    count = len(side_sum.late)
    side_sum.late, mix_sum.far = tuple(held[:count]), tuple(held[count:])
    mix_sum.second()
    side_mine = side_sum.total(*mix_sum.sums)
    side_rows = to_rows(side_mine, ranks)
    every = every.reshape(ranks, 8, -1)
    held = lax.optimization_barrier((mlp_rows, mlp_out, side_rows) + mix_sum.near)
    mlp_rows, mlp_out, side_rows = held[:3]
    mix_sum.near = held[3:]
    mix_rows = to_rows(mix_sum.total(), ranks)
    grad_hidden, grad_up, grad_down = unpack_even(ranks, mlp_rows, 3)

    output = from_ring((middle + mlp_out.astype(F32)).astype(BF))
    n = inputs * rms_scale(inputs)
    e = d_attn * attn_gain_full
    grad_tokens = from_ring(
        (d_middle + rms_scale(inputs) * (e - n * jnp.mean(e * n, axis=-1, keepdims=True))).astype(BF)
    )

    def per_head(part, lead):
        part = part.reshape(ranks // vs, vs, lead, -1).sum(axis=1)
        return jnp.transpose(part, (1, 0, 2)).reshape(lead, -1)

    every_taps = every[:, :KERNEL]
    grad_conv_value = jnp.transpose(every_taps[:, :, at_v:], (1, 0, 2)).reshape(KERNEL, -1)
    gain_sum = every[:, 6, :dv].reshape(ranks // vs, vs, dv).sum(axis=0).reshape(-1)
    grad_query = plan.join_keys(mix_rows[:, :, :at_k])
    grad_key = plan.join_keys(mix_rows[:, :, at_k:at_v])
    grad_value = plan.join_even(mix_rows[:, :, at_v:at_s])
    grad_decay = plan.join_keys(mix_rows[:, :, at_s : at_s + hp])
    grad_beta = plan.join_keys(mix_rows[:, :, at_s + hp : at_s + 2 * hp])
    grad_gate = plan.join_even(side_rows[:, :, : hp * dv])

    def gain_grad(gain, pairs):
        total = sum(jnp.sum(w.astype(F32) * g, axis=1) for w, g in pairs)
        return total / gain.astype(F32)

    return (
        output[None],
        grad_tokens[None],
        gain_grad(
            attn_gain,
            (
                (w_query, grad_query),
                (w_key, grad_key),
                (w_value, grad_value),
                (w_decay, grad_decay),
                (w_beta, grad_beta),
                (w_gate, grad_gate),
            ),
        ),
        grad_query,
        grad_key,
        grad_value,
        grad_decay,
        grad_beta,
        grad_gate,
        plan.join_even(side_rows[:, :, hp * dv :]),
        per_head(every_taps[:, :, :at_k], KERNEL),
        per_head(every_taps[:, :, at_k:at_v], KERNEL),
        grad_conv_value,
        per_head(every[:, 5, :hp], 1)[0],
        per_head(every[:, 4, :hp], 1)[0],
        gain_sum,
        gain_grad(mlp_gain, ((w_hidden, grad_hidden), (w_up, grad_up))),
        grad_hidden,
        grad_up,
        grad_down,
    )


def solution(mesh):
    flat = ("dp", "seq")
    tok_spec = P("dp", "seq", None)
    row_spec = P(flat, None)
    gain_spec = P(flat)
    in_specs = (
        (tok_spec, gain_spec)
        + (row_spec,) * 7
        + (P(),) * 6
        + (gain_spec,)
        + (row_spec,) * 3
        + (P("dp", "seq"), tok_spec)
    )
    out_specs = (
        (tok_spec, tok_spec, gain_spec)
        + (row_spec,) * 7
        + (P(),) * 6
        + (gain_spec,)
        + (row_spec,) * 3
    )
    return jax.shard_map(local, mesh=mesh, in_specs=in_specs, out_specs=out_specs, check_vma=False)
```
